128 devices in a mesh: sec: 8 (over z, core), blk: 16 (over y, x).
Axes of the slice: x: 4, y: 4, z: 4, core: 2. Of those that a mesh axis runs over, the one named last changes fastest.
Arguments:
- wavefunction: bfloat16 [8, 192, 128, 128], P('sec', 'blk')
- left_env: bfloat16 [8, 20, 192, 128, 128], P('sec', None, 'blk')
- right_env: bfloat16 [8, 20, 192, 128, 128], P('sec', None, 'blk')
- row_offset: int32 [8, 12], P('sec'), may hold values from 0 to 15, as said below
- sector_dims: int32 [8, 192, 2], P('sec', 'blk'), may hold values from 64 to 128
- trunc_ranks: int32 [8, 192], P('sec', 'blk'), may hold values from 32 to 128
Outputs:
- state_new: bfloat16 [8, 192, 128, 128], P('sec', 'blk')
- hstate_new: bfloat16 [8, 192, 128, 128], P('sec', 'blk')
- energy: float32 [8], P('sec')
- next_left: bfloat16 [8, 20, 192, 128, 128], P('sec', None, 'blk')
The draws below stay inside these ranges and needn't reach their ends.
Inputs may be any that keep to these rules, and one draw needn't show every extreme that they name: The sector with up-charge u and down-charge e is stored in slot u of device (e + row_offset[u]) mod 16; in every section the offsets of some two adjacent up-charges differ by 16 / 2 modulo 16.
All inputs are finite; a program needn't handle non-finite values.
Results may differ from the reference program's by a relative error of at most 0.0067.
Values may be sent and summed in bfloat16 or wider, within the bound.
A program may use at most 128 MiB of HBM per device.

```python
import math
import jax
import jax.numpy as jnp

SB = 128
NW = 20
Q_DEV = 12
NSEC = 8
NQ = 192
N_BLK = 16


def draw_wavefunction(key, part):
    key_block, key_row, key_col, key_base = jax.random.split(key, 4)
    slots = jnp.arange(NQ, dtype=jnp.int32)
    device = (slots // Q_DEV).astype(jnp.float32)
    rising = 1.0 + 2.0 * device / float(max(N_BLK - 1, 1))
    block_scale = jnp.exp(jax.random.uniform(key_block, (NSEC, NQ, 1, 1), jnp.float32) * math.log(10.0))
    block_scale = block_scale * rising[None, :, None, None]
    row_scale = jnp.exp(jax.random.uniform(key_row, (NSEC, NQ, SB, 1), jnp.float32) * math.log(3.0))
    col_scale = jnp.exp(jax.random.uniform(key_col, (NSEC, NQ, 1, SB), jnp.float32) * math.log(3.0))
    base = jax.random.normal(key_base, (NSEC, NQ, SB, SB), jnp.float32)
    return (base * block_scale * row_scale * col_scale).astype(jnp.bfloat16)


def environment_draw(key):
    key_noise, key_diag = jax.random.split(key, 2)
    slots = jnp.arange(NQ, dtype=jnp.int32)
    device = (slots // Q_DEV).astype(jnp.float32) / float(max(N_BLK - 1, 1))
    noise = jax.random.normal(key_noise, (NSEC, NW, NQ, SB, SB), jnp.float32)
    rising = 0.5 + device
    noise = noise / math.sqrt(float(SB))
    jitter = jax.random.uniform(key_diag, (NSEC, NW, NQ, 1, 1), jnp.float32, 0.8, 1.25)
    channel_on = (jnp.arange(NW, dtype=jnp.int32) % 5 == 0).astype(jnp.float32)
    lines = jnp.arange(SB, dtype=jnp.int32)
    identity = (lines[:, None] == lines[None, :]).astype(jnp.float32)
    diag = channel_on[None, :, None, None, None] * rising[None, None, :, None, None] * jitter * identity[None, None, None, :, :]
    return (noise + diag).astype(jnp.bfloat16)


def draw_left_env(key, part):
    return environment_draw(jax.random.fold_in(key, 31))


def draw_right_env(key, part):
    return environment_draw(jax.random.fold_in(key, 37))


def draw_row_offset(key, part):
    key_first, key_step, key_place = jax.random.split(jax.random.fold_in(key, 17), 3)
    first = jax.random.randint(key_first, (NSEC, 1), 0, N_BLK, dtype=jnp.int32)
    steps = jax.random.randint(key_step, (NSEC, Q_DEV - 1), 0, N_BLK, dtype=jnp.int32)
    place = jax.random.randint(key_place, (NSEC, 1), 0, Q_DEV - 1, dtype=jnp.int32)
    columns = jnp.arange(Q_DEV - 1, dtype=jnp.int32)[None, :]
    steps = jnp.where(columns == place, jnp.int32(N_BLK // 2), steps)
    offsets = jnp.concatenate([first, first + jnp.cumsum(steps, axis=1, dtype=jnp.int32)], axis=1)
    return (offsets % N_BLK).astype(jnp.int32)


def touch_ends(entries, own_key, least, largest):
    index_at = [jax.random.randint(jax.random.fold_in(own_key, axis), (), 0, length) for axis, length in enumerate(entries.shape)]
    longest = entries.shape.index(max(entries.shape))
    beside = index_at[:longest] + [(index_at[longest] + 1) % entries.shape[longest]] + index_at[longest + 1:]
    return entries.at[tuple(index_at)].set(least).at[tuple(beside)].set(largest)


def setup_inputs(seed: int = 0) -> dict:
    key_list = jax.random.split(jax.random.key(seed), 7)
    return {
        "wavefunction": draw_wavefunction(jax.random.fold_in(key_list[6], 71), 0),
        "left_env": draw_left_env(jax.random.fold_in(key_list[6], 71), 0),
        "right_env": draw_right_env(jax.random.fold_in(key_list[6], 71), 0),
        "row_offset": draw_row_offset(jax.random.fold_in(key_list[6], 71), 0),
        "sector_dims": touch_ends(jax.random.randint(key_list[4], (NSEC, NQ, 2), SB // 2, SB + 1), jax.random.fold_in(key_list[4], 1), SB // 2, SB).astype(jnp.int32),
        "trunc_ranks": touch_ends(jax.random.randint(key_list[5], (NSEC, NQ), SB // 4, SB + 1), jax.random.fold_in(key_list[5], 1), SB // 4, SB).astype(jnp.int32),
    }


def source_slots(offsets):
    slots = jnp.arange(NQ, dtype=jnp.int32)
    device = slots // Q_DEV
    up_val = slots % Q_DEV
    own_off = jnp.take(offsets, up_val)
    prev_off = jnp.take(offsets, (up_val - 1) % Q_DEV)
    next_off = jnp.take(offsets, (up_val + 1) % Q_DEV)
    down_val = (device - own_off) % N_BLK
    row_lo = jnp.clip(up_val - 1, 0, Q_DEV - 1)
    row_hi = jnp.clip(up_val + 1, 0, Q_DEV - 1)
    sources = [slots, (down_val + prev_off) % N_BLK * Q_DEV + row_lo, (down_val + next_off) % N_BLK * Q_DEV + row_hi, (device - 1) % N_BLK * Q_DEV + up_val, (device + 1) % N_BLK * Q_DEV + up_val]
    exists = [slots >= 0, up_val >= 1, up_val <= Q_DEV - 2, down_val >= 1, down_val <= N_BLK - 2]
    return ([s.astype(jnp.int32) for s in sources], exists)

def picked_blocks(state, sources, exists):
    result = []
    for ctype in range(5):
        taken = jnp.take(state, sources[ctype], axis=0)
        result.append(jnp.where(exists[ctype][:, None, None], taken, jnp.zeros_like(taken)))
    return result

def apply_ham(state, lenv, renv, sources, exists, mask):
    blocks = picked_blocks(state, sources, exists)
    total = jnp.zeros(state.shape, jnp.float32)
    for ctype in range(5):
        inner = jnp.einsum('wtab,tbc->wtac', lenv[ctype::5].astype(jnp.float32), blocks[ctype].astype(jnp.float32)).astype(jnp.bfloat16)
        total = total + jnp.einsum('wtac,wtdc->tad', inner.astype(jnp.float32), renv[ctype::5].astype(jnp.float32))
    return total * mask

def env_update(kept, lenv, sources, exists):
    blocks = picked_blocks(kept, sources, exists)
    parts = []
    for ctype in range(5):
        inner = jnp.einsum('wtab,tbc->wtac', lenv[ctype::5].astype(jnp.float32), blocks[ctype].astype(jnp.float32)).astype(jnp.bfloat16)
        parts.append(jnp.einsum('tba,wtbc->wtac', kept.astype(jnp.float32), inner.astype(jnp.float32)).astype(jnp.bfloat16))
    stacked = jnp.stack(parts, axis=1)
    return stacked.reshape((NW, NQ, SB, SB))

def reference(wavefunction, left_env, right_env, row_offset, sector_dims, trunc_ranks):
    cells = float(NQ * SB * SB)
    lines = jnp.arange(SB, dtype=jnp.int32)
    states, hstates, energies, updates = ([], [], [], [])
    for section in range(NSEC):
        sources, exists = source_slots(row_offset[section])
        dims = sector_dims[section]
        mask_on = (lines[None, :, None] < dims[:, 0][:, None, None]) & (lines[None, None, :] < dims[:, 1][:, None, None])
        mask = mask_on.astype(jnp.float32)
        lenv = left_env[section]
        renv = right_env[section]
        start = wavefunction[section]
        vzero = jnp.where(mask_on, start, jnp.zeros_like(start))
        hzero = apply_ham(vzero, lenv, renv, sources, exists, mask)
        vzero_f = vzero.astype(jnp.float32)
        nzero = jnp.sum(vzero_f * vzero_f)
        pzero = jnp.sum(vzero_f * hzero)
        scale = jnp.sqrt(cells / nzero)
        uzero = vzero_f * scale
        huzero = hzero * scale
        a_zero = pzero / nzero
        resid = huzero - a_zero * uzero
        beta = jnp.sqrt(jnp.sum(resid * resid) / cells + 1e-06)
        vone = (resid / beta).astype(jnp.bfloat16)
        hone = apply_ham(vone, lenv, renv, sources, exists, mask)
        a_one = jnp.sum(vone.astype(jnp.float32) * hone) / cells
        half_gap = (a_zero - a_one) / 2.0
        ritz = (a_zero + a_one) / 2.0 - jnp.sqrt(half_gap * half_gap + beta * beta)
        gap_val = ritz - a_zero
        length = jnp.sqrt(beta * beta + gap_val * gap_val)
        xcoef = beta / length
        ycoef = gap_val / length
        state_new = (xcoef * uzero + ycoef * vone.astype(jnp.float32)).astype(jnp.bfloat16)
        hstate_new = (xcoef * huzero + ycoef * hone).astype(jnp.bfloat16)
        kept_on = lines[None, None, :] < trunc_ranks[section][:, None, None]
        kept = jnp.where(kept_on, state_new, jnp.zeros_like(state_new))
        updates.append(env_update(kept, lenv, sources, exists))
        states.append(state_new)
        hstates.append(hstate_new)
        energies.append(ritz)
    next_left = jnp.stack([left_env[0]] + updates[:-1], axis=0)
    return (jnp.stack(states, 0), jnp.stack(hstates, 0), jnp.stack(energies, 0).astype(jnp.float32), next_left)
```

```python
import functools

import jax
import jax.numpy as jnp
from jax import lax
from jax.experimental import pallas as pl
from jax.experimental.pallas import tpu as pltpu
from jax.sharding import PartitionSpec as P

MESH = pl.DeviceIdType.MESH
VMEM_SPEC = pl.BlockSpec(memory_space=pltpu.VMEM)
SMEM_SPEC = pl.BlockSpec(memory_space=pltpu.SMEM)
ANY_SPEC = pl.BlockSpec(memory_space=pl.ANY)
F32 = jnp.float32
BF16 = jnp.bfloat16
NB = 16
NU = 12
NC = 20
SB = 128
HALF = NU // 2
ROWS = 16
NCH = SB // ROWS


def lane_tile(values):
    row = lax.broadcasted_iota(jnp.int32, (8, SB), 0)
    lane = lax.broadcasted_iota(jnp.int32, (8, SB), 1)
    tile = jnp.zeros((8, SB), F32)
    for i, entries in enumerate(values):
        for u, entry in enumerate(entries):
            tile = jnp.where((row == i) & (lane == u), entry, tile)
    return tile


def slot_mask(dim_a, dim_b):
    line_a = lax.broadcasted_iota(jnp.int32, (SB, SB), 0)
    line_b = lax.broadcasted_iota(jnp.int32, (SB, SB), 1)
    return (line_a < dim_a) & (line_b < dim_b)


def exchange_kernel(first, off_ref, *refs):
    if first:
        dims_ref, trunc_ref, x_ref, v0_ref, o12_ref, o3_ref, o4_ref, os_ref, xs, small = refs[:10]
        rest = refs[10:]
    else:
        xs, small, o12_ref, o3_ref, o4_ref, os_ref = refs[:6]
        rest = refs[6:]
    recv1, sendb, side_s, side_r, s1s, s1r, s2s, s2r, sms, smr, loc = rest
    me = lax.axis_index("blk")
    par = me // NCH
    lo = pl.multiple_of((me % NCH) * ROWS, ROWS)

    barrier = pltpu.get_barrier_semaphore()
    for k in range(1, NB):
        pl.semaphore_signal(barrier, inc=1, device_id={"blk": (me + k) % NB}, device_id_type=MESH)

    if first:
        for u in range(NU):
            on = slot_mask(dims_ref[0, u, 0], dims_ref[0, u, 1])
            xs[u // 2, u % 2] = jnp.where(on, x_ref[u // 2, u % 2], jnp.zeros((SB, SB), BF16))
        small[...] = lane_tile([[trunc_ref[0, u].astype(F32) for u in range(NU)]])
    pl.semaphore_wait(barrier, NB - 1)

    def phase1(k):
        to = (me + k) % NB
        at = pl.multiple_of((to % NCH) * ROWS, ROWS)
        return pltpu.make_async_remote_copy(
            src_ref=xs.at[:, to // NCH, pl.ds(at, ROWS), :],
            dst_ref=recv1.at[me],
            send_sem=s1s.at[k],
            recv_sem=s1r.at[k],
            device_id={"blk": to},
            device_id_type=MESH,
        )

    def tiny(k):
        to = (me + k) % NB
        return pltpu.make_async_remote_copy(
            src_ref=small,
            dst_ref=os_ref.at[me],
            send_sem=sms.at[k],
            recv_sem=smr.at[k],
            device_id={"blk": to},
            device_id_type=MESH,
        )

    def side(i):
        return pltpu.make_async_remote_copy(
            src_ref=xs,
            dst_ref=(o3_ref, o4_ref)[i],
            send_sem=side_s.at[i],
            recv_sem=side_r.at[i],
            device_id={"blk": (me + (1, NB - 1)[i]) % NB},
            device_id_type=MESH,
        )

    def phase2(k):
        to = (me + k) % NB
        return pltpu.make_async_remote_copy(
            src_ref=sendb.at[to],
            dst_ref=o12_ref.at[:, pl.ds(par, HALF), 1 - par, pl.ds(lo, ROWS), :],
            send_sem=s2s.at[k],
            recv_sem=s2r.at[k],
            device_id={"blk": to},
            device_id_type=MESH,
        )

    @pl.loop(1, NB)
    def _(k):
        phase1(k).start()

    own1 = pltpu.make_async_copy(xs.at[:, par, pl.ds(lo, ROWS), :], recv1.at[me], loc.at[0])
    own1.start()
    own_small = pltpu.make_async_copy(small, os_ref.at[me], loc.at[1])
    own_small.start()
    copies = []
    if first:
        copies.append(pltpu.make_async_copy(xs, v0_ref, loc.at[3]))
        copies[0].start()
    side(0).start()
    side(1).start()

    @pl.loop(1, NB)
    def _(k):
        tiny(k).start()

    own1.wait()

    @pl.loop(1, NB)
    def _(k):
        phase1(k).wait_recv()

    @pl.loop(0, NB)
    def _(t):
        for r in range(HALF):
            up = 2 * r + par
            own = off_ref[0, up] + t + NB
            above = (own - off_ref[0, jnp.minimum(up + 1, NU - 1)]) & (NB - 1)
            below = (own - off_ref[0, jnp.maximum(up - 1, 0)]) & (NB - 1)
            sendb[t, 0, r] = recv1[above, r]
            sendb[t, 1, r] = recv1[below, r]

    @pl.loop(1, NB)
    def _(k):
        phase2(k).start()

    own2 = pltpu.make_async_copy(
        sendb.at[me], o12_ref.at[:, pl.ds(par, HALF), 1 - par, pl.ds(lo, ROWS), :], loc.at[2]
    )
    own2.start()
    for i in range(2):
        side(i).wait()

    @pl.loop(1, NB)
    def _(k):
        phase1(k).wait_send()
        tiny(k).wait()

    own2.wait()
    own_small.wait()
    for copy in copies:
        copy.wait()

    @pl.loop(1, NB)
    def _(k):
        phase2(k).wait()


def exchange(first, offsets, *args):
    pair = jax.ShapeDtypeStruct((HALF, 2, SB, SB), BF16)
    outs = [
        jax.ShapeDtypeStruct((2, HALF + 1, 2, SB, SB), BF16),
        pair,
        pair,
        jax.ShapeDtypeStruct((NB, 8, SB), F32),
    ]
    scratch = [
        pltpu.VMEM((NB, HALF, ROWS, SB), BF16),
        pltpu.VMEM((NB, 2, HALF, ROWS, SB), BF16),
        pltpu.SemaphoreType.DMA((2,)),
        pltpu.SemaphoreType.DMA((2,)),
    ] + [pltpu.SemaphoreType.DMA((NB,)) for _ in range(6)] + [pltpu.SemaphoreType.DMA((4,))]
    in_specs = [SMEM_SPEC, VMEM_SPEC, VMEM_SPEC]
    if first:
        in_specs = [SMEM_SPEC, SMEM_SPEC, SMEM_SPEC, VMEM_SPEC]
        outs = [pair] + outs
        scratch = [pltpu.VMEM((HALF, 2, SB, SB), BF16), pltpu.VMEM((8, SB), F32)] + scratch
    return pl.pallas_call(
        functools.partial(exchange_kernel, first),
        out_shape=outs,
        in_specs=in_specs,
        out_specs=[ANY_SPEC] * len(outs),
        scratch_shapes=scratch,
        compiler_params=pltpu.CompilerParams(collective_id=0 if first else 1, has_side_effects=True),
        name="exchange_v0" if first else "exchange_g",
    )(offsets, *args)


def hpsi(l_ref, r_ref, xs):
    inner = [None] * NC
    per = NC // 5
    for c in range(5):
        stack = jnp.concatenate([l_ref[c + 5 * k, 0] for k in range(per)], axis=0)
        product = jnp.dot(stack, xs[c], preferred_element_type=F32).astype(BF16)
        for k in range(per):
            inner[c + 5 * k] = product[k * SB : (k + 1) * SB]
    left = jnp.concatenate(inner, axis=1)
    right = jnp.concatenate([r_ref[w, 0] for w in range(NC)], axis=1)
    return lax.dot_general(left, right, (((1,), (1,)), ((), ())), preferred_element_type=F32)


def exists(off_ref, t, c):
    if c == 1:
        return t >= 1
    if c == 2:
        return t <= NU - 2
    down = (lax.axis_index("blk") + NB - off_ref[0, t]) & (NB - 1)
    return down >= 1 if c == 3 else down <= NB - 2


def source_device(off_ref, t, c):
    me = lax.axis_index("blk")
    if c == 1:
        return (me + NB - off_ref[0, t] + off_ref[0, jnp.maximum(t - 1, 0)]) & (NB - 1)
    if c == 2:
        return (me + NB - off_ref[0, t] + off_ref[0, jnp.minimum(t + 1, NU - 1)]) & (NB - 1)
    return (me + (NB - 1 if c == 3 else 1)) & (NB - 1)


def source_slot(t, c):
    if c == 1:
        return jnp.maximum(t - 1, 0)
    if c == 2:
        return jnp.minimum(t + 1, NU - 1)
    return t


def total(x):
    return jnp.sum(jnp.sum(x, axis=0, keepdims=True), axis=1, keepdims=True)


def put(tile_ref, row, t, value):
    rows = lax.broadcasted_iota(jnp.int32, (8, SB), 0)
    lanes = lax.broadcasted_iota(jnp.int32, (8, SB), 1)
    tile_ref[...] = jnp.where((rows == row) & (lanes == t), value, tile_ref[...])


def first_kernel(off_ref, dims_ref, l_ref, r_ref, v_ref, up_ref, dn_ref, e3_ref, e4_ref, h_ref, g_ref, s_ref):
    t = pl.program_id(0)
    zero = jnp.zeros((SB, SB), BF16)
    v = v_ref[0]
    xs = [v]
    for c, ref in ((1, up_ref), (2, dn_ref)):
        xs.append(jnp.where(exists(off_ref, t, c), ref[0, 0], zero))
    for c, ref in ((3, e3_ref), (4, e4_ref)):
        xs.append(jnp.where(exists(off_ref, t, c), ref[0], zero))
    h = jnp.where(slot_mask(dims_ref[0, t, 0], dims_ref[0, t, 1]), hpsi(l_ref, r_ref, xs), 0.0)
    vf = v.astype(F32)
    n = total(vf * vf)
    p = total(vf * h)
    alpha = jnp.where(n > 0.0, p / jnp.where(n > 0.0, n, 1.0), 0.0)
    g = h - alpha * vf
    h_ref[0] = h
    g_ref[0] = g.astype(BF16)

    @pl.when(t == 0)
    def _():
        s_ref[...] = jnp.zeros((8, SB), F32)

    put(s_ref, 0, t, n)
    put(s_ref, 1, t, p)
    put(s_ref, 2, t, total(g * g))
    put(s_ref, 3, t, alpha)


def slot_specs():
    env = pl.BlockSpec((NC, 1, SB, SB), lambda t, *_: (0, t, 0, 0))
    one = pl.BlockSpec((1, SB, SB), lambda t, *_: (t, 0, 0))
    up = pl.BlockSpec((1, 1, SB, SB), lambda t, *_: (0, jnp.maximum(t, 1), 0, 0))
    dn = pl.BlockSpec((1, 1, SB, SB), lambda t, *_: (1, jnp.minimum(t + 2, NU), 0, 0))
    tile = pl.BlockSpec((8, SB), lambda t, *_: (0, 0))
    tiles = pl.BlockSpec((NB, 8, SB), lambda t, *_: (0, 0, 0))
    return env, one, up, dn, tile, tiles


COST = pl.CostEstimate(flops=2 * 2 * NC * NU * SB**3, bytes_accessed=2 * 2 * NC * NU * SB**2, transcendentals=0)


def first_product(offsets, dims, lenv, renv, v, s12, s3, s4):
    env, one, up, dn, tile, _ = slot_specs()
    state = jax.ShapeDtypeStruct((NU, SB, SB), F32)
    return pl.pallas_call(
        first_kernel,
        grid_spec=pltpu.PrefetchScalarGridSpec(
            num_scalar_prefetch=2,
            grid=(NU,),
            in_specs=[env, env, one, up, dn, one, one],
            out_specs=[one, one, tile],
        ),
        out_shape=[state, jax.ShapeDtypeStruct((NU, SB, SB), BF16), jax.ShapeDtypeStruct((8, SB), F32)],
        cost_estimate=COST,
        name="first_product",
    )(offsets, dims, lenv, renv, v, s12, s12, s3, s4)


def second_kernel(
    off_ref, dims_ref, l_ref, r_ref, v_ref, up_ref, dn_ref, e3_ref, e4_ref, gup_ref, gdn_ref, g3_ref, g4_ref, h0_ref,
    sm_ref, sv_ref, v1_ref, src_ref, h_ref, q_ref, k_ref, acc
):
    t = pl.program_id(0)
    sums = sv_ref[...]
    nt, pt, rt, at = sums[:, 0, :], sums[:, 1, :], sums[:, 2, :], sums[:, 3, :]
    n = total(nt)
    a = total(pt) / n
    gap = at - a
    beta = jnp.sqrt(total(rt + gap * gap * nt) / n + 1e-6)
    scale = jnp.sqrt(float(NB * NU * SB * SB) / n)
    kappa = scale / beta
    v = v_ref[0].astype(F32)
    own = (kappa * (h0_ref[0] - a * v)).astype(BF16)
    xs = [own]
    sources = ((1, up_ref, gup_ref), (2, dn_ref, gdn_ref), (3, e3_ref, g3_ref), (4, e4_ref, g4_ref))
    for c, ref, gref in sources:
        lead = (0, 0) if c < 3 else (0,)
        alpha = sm_ref[source_device(off_ref, t, c), 3, source_slot(t, c)]
        x = kappa * (gref[lead].astype(F32) + (alpha - a) * ref[lead].astype(F32))
        x = jnp.where(exists(off_ref, t, c), x, 0.0).astype(BF16)
        src_ref[c - 1, 0] = x
        xs.append(x)
    h = jnp.where(slot_mask(dims_ref[0, t, 0], dims_ref[0, t, 1]), hpsi(l_ref, r_ref, xs), 0.0)
    v1_ref[0] = own
    h_ref[0] = h

    @pl.when(t == 0)
    def _():
        acc[...] = jnp.zeros((1, SB), F32)
        row = lax.broadcasted_iota(jnp.int32, (8, SB), 0)
        k_ref[...] = jnp.where(row == 0, a, jnp.where(row == 1, beta, scale))

    acc[...] += jnp.sum(own.astype(F32) * h, axis=0, keepdims=True)
    q_ref[...] = jnp.broadcast_to(acc[...], (8, SB))


def second_product(offsets, dims, lenv, renv, v, s12, s3, s4, g12, g3, g4, h0, sums):
    env, one, up, dn, tile, tiles = slot_specs()
    state = jax.ShapeDtypeStruct((NU, SB, SB), F32)
    return pl.pallas_call(
        second_kernel,
        grid_spec=pltpu.PrefetchScalarGridSpec(
            num_scalar_prefetch=2,
            grid=(NU,),
            in_specs=[env, env, one, up, dn, one, one, up, dn, one, one, one, SMEM_SPEC, tiles],
            out_specs=[one, pl.BlockSpec((4, 1, SB, SB), lambda t, *_: (0, t, 0, 0)), one, tile, tile],
            scratch_shapes=[pltpu.VMEM((1, SB), F32)],
        ),
        out_shape=[
            jax.ShapeDtypeStruct((NU, SB, SB), BF16),
            jax.ShapeDtypeStruct((4, NU, SB, SB), BF16),
            state,
            jax.ShapeDtypeStruct((8, SB), F32),
            jax.ShapeDtypeStruct((8, SB), F32),
        ],
        cost_estimate=COST,
        name="second_product",
    )(offsets, dims, lenv, renv, v, s12, s12, s3, s4, g12, g12, g3, g4, h0, sums, sums)


def kept_kernel(
    nsec, off_ref, tr_ref, q_ref, k_ref, v_ref, s12_ref, s3_ref, s4_ref, v1_ref, src_ref, kept_ref, coef_ref,
    kept, qs, q_send, q_recv, z_send, z_recv
):
    me = lax.axis_index("blk")
    sec = lax.axis_index("sec")
    after = {"sec": (sec + 1) % nsec}
    barrier = pltpu.get_barrier_semaphore()
    for k in range(1, NB):
        pl.semaphore_signal(barrier, inc=1, device_id={"blk": (me + k) % NB}, device_id_type=MESH)
    pl.semaphore_signal(barrier, inc=1, device_id=after, device_id_type=MESH)
    pl.semaphore_signal(barrier, inc=1, device_id={"sec": (sec + nsec - 1) % nsec}, device_id_type=MESH)
    pl.semaphore_wait(barrier, NB + 1)

    def tiny(k):
        return pltpu.make_async_remote_copy(
            src_ref=q_ref,
            dst_ref=qs.at[me],
            send_sem=q_send.at[k],
            recv_sem=q_recv.at[k],
            device_id={"blk": (me + k) % NB},
            device_id_type=MESH,
        )

    @pl.loop(1, NB)
    def _(k):
        tiny(k).start()

    qs[me] = q_ref[...]

    @pl.loop(1, NB)
    def _(k):
        tiny(k).wait()

    a0, beta, scale = k_ref[0:1, 0:1], k_ref[1:2, 0:1], k_ref[2:3, 0:1]
    a1 = total(jnp.sum(qs[...], axis=0)[0:1]) / float(NB * NU * SB * SB)
    half = (a0 - a1) / 2.0
    ritz = (a0 + a1) / 2.0 - jnp.sqrt(half * half + beta * beta)
    gap = ritz - a0
    length = jnp.sqrt(beta * beta + gap * gap)
    xcoef, ycoef = beta / length, gap / length
    row = lax.broadcasted_iota(jnp.int32, (8, SB), 0)
    coef_ref[...] = jnp.where(row == 0, ritz, jnp.where(row == 1, xcoef, jnp.where(row == 2, ycoef, scale)))
    lane = lax.broadcasted_iota(jnp.int32, (SB, SB), 1).astype(F32)

    def send(c):
        return pltpu.make_async_remote_copy(
            src_ref=kept.at[c],
            dst_ref=kept_ref.at[c],
            send_sem=z_send.at[c],
            recv_sem=z_recv.at[c],
            device_id=after,
            device_id_type=MESH,
        )

    for c in range(5):

        @pl.loop(0, NU)
        def _(t):
            if c == 0:
                v, v1 = v_ref[t], v1_ref[t]
                rank = tr_ref[me, 0, t]
            else:
                v1 = src_ref[c - 1, t]
                rank = tr_ref[source_device(off_ref, t, c), 0, source_slot(t, c)]
                if c == 1:
                    v = s12_ref[0, jnp.maximum(t, 1)]
                elif c == 2:
                    v = s12_ref[1, jnp.minimum(t + 2, NU)]
                else:
                    v = (s3_ref, s4_ref)[c - 3][t]
            x = xcoef * (v.astype(F32) * scale) + ycoef * v1.astype(F32)
            on = lane < rank
            if c:
                on = on & exists(off_ref, t, c)
            kept[c, t] = jnp.where(on, x, 0.0).astype(BF16)

    for c in range(5):
        send(c).start()
    for c in range(5):
        send(c).wait()


def kept_blocks(nsec, offsets, ranks, q, k, v, s12, s3, s4, v1, src):
    blocks = (5, NU, SB, SB)
    return pl.pallas_call(
        functools.partial(kept_kernel, nsec),
        out_shape=[jax.ShapeDtypeStruct(blocks, BF16), jax.ShapeDtypeStruct((8, SB), F32)],
        in_specs=[SMEM_SPEC, SMEM_SPEC] + [VMEM_SPEC] * 8,
        out_specs=[ANY_SPEC, VMEM_SPEC],
        scratch_shapes=[
            pltpu.VMEM(blocks, BF16),
            pltpu.VMEM((NB, 8, SB), F32),
            pltpu.SemaphoreType.DMA((NB,)),
            pltpu.SemaphoreType.DMA((NB,)),
            pltpu.SemaphoreType.DMA((5,)),
            pltpu.SemaphoreType.DMA((5,)),
        ],
        compiler_params=pltpu.CompilerParams(collective_id=2, has_side_effects=True),
        name="kept_blocks",
    )(offsets, ranks, q, k, v, s12, s3, s4, v1, src)


def update_kernel(head_ref, coef_ref, own_ref, l_ref, k_ref, v_ref, v1_ref, h0_ref, h1_ref, next_ref, s_ref, hs_ref):
    first_section = head_ref[0] == 1
    xcoef, ycoef, scale = coef_ref[1:2, 0:1], coef_ref[2:3, 0:1], coef_ref[3:4, 0:1]
    s_ref[0] = (xcoef * (v_ref[0].astype(F32) * scale) + ycoef * v1_ref[0].astype(F32)).astype(BF16)
    hs_ref[0] = (xcoef * (h0_ref[0] * scale) + ycoef * h1_ref[0]).astype(BF16)

    @pl.when(first_section)
    def _():
        next_ref[...] = own_ref[...]

    @pl.when(jnp.logical_not(first_section))
    def _():
        per = NC // 5
        kept = k_ref[0, 0]
        for c in range(5):
            stack = jnp.concatenate([l_ref[c + 5 * k, 0] for k in range(per)], axis=0)
            inner = jnp.dot(stack, k_ref[c, 0], preferred_element_type=F32).astype(BF16)
            wide = jnp.concatenate([inner[k * SB : (k + 1) * SB] for k in range(per)], axis=1)
            out = lax.dot_general(kept, wide, (((0,), (0,)), ((), ())), preferred_element_type=F32).astype(BF16)
            for k in range(per):
                next_ref[c + 5 * k, 0] = out[:, k * SB : (k + 1) * SB]


def update(head, coef, lenv, prev, kept, v, v1, h0, h1):
    _, one, _, _, tile, _ = slot_specs()
    own = pl.BlockSpec((NC, 1, SB, SB), lambda t, head: (0, t * head[0], 0, 0))
    far = pl.BlockSpec((NC, 1, SB, SB), lambda t, head: (0, t * (1 - head[0]), 0, 0))
    state = jax.ShapeDtypeStruct((NU, SB, SB), BF16)
    return pl.pallas_call(
        update_kernel,
        grid_spec=pltpu.PrefetchScalarGridSpec(
            num_scalar_prefetch=1,
            grid=(NU,),
            in_specs=[
                tile, own, far, pl.BlockSpec((5, 1, SB, SB), lambda t, *_: (0, t, 0, 0)), one, one, one, one,
            ],
            out_specs=[pl.BlockSpec((NC, 1, SB, SB), lambda t, *_: (0, t, 0, 0)), one, one],
        ),
        out_shape=[jax.ShapeDtypeStruct((NC, NU, SB, SB), BF16), state, state],
        cost_estimate=COST,
        name="update",
    )(head, coef, lenv, prev, kept, v, v1, h0, h1)


def shards(wavefunction, left_env, right_env, offsets, dims, ranks):
    nsec = lax.axis_size("sec")
    lenv, renv = left_env[0], right_env[0]
    pairs = (HALF, 2, SB, SB)
    flat = (NU, SB, SB)
    prev = lax.ppermute(lenv, "sec", [(i, i + 1) for i in range(nsec - 1)])
    v, s12, s3, s4, rank_all = exchange(True, offsets, dims, ranks, wavefunction[0].reshape(pairs))
    v, s3, s4 = v.reshape(flat), s3.reshape(flat), s4.reshape(flat)
    s12 = s12.reshape((2, NU + 2, SB, SB))
    h0, g, sums = first_product(offsets, dims, lenv, renv, v, s12, s3, s4)
    g12, g3, g4, sums_all = exchange(False, offsets, g.reshape(pairs), sums)
    g3, g4 = g3.reshape(flat), g4.reshape(flat)
    g12 = g12.reshape((2, NU + 2, SB, SB))
    v1, src, h1, q, k = second_product(offsets, dims, lenv, renv, v, s12, s3, s4, g12, g3, g4, h0, sums_all)
    kept, coef = kept_blocks(nsec, offsets, rank_all, q, k, v, s12, s3, s4, v1, src)
    head = jnp.where(lax.axis_index("sec") == 0, 1, 0).astype(jnp.int32).reshape((1,))
    next_left, state, hstate = update(head, coef, lenv, prev, kept, v, v1, h0, h1)
    return state[None], hstate[None], coef[0, 0:1], next_left[None]


def solution(mesh):
    placed = (
        P("sec", "blk", None, None),
        P("sec", None, "blk", None, None),
        P("sec", None, "blk", None, None),
        P("sec", None),
        P("sec", "blk", None),
        P("sec", "blk"),
    )
    return jax.shard_map(
        shards,
        mesh=mesh,
        in_specs=placed,
        out_specs=(
            P("sec", "blk", None, None),
            P("sec", "blk", None, None),
            P("sec"),
            P("sec", None, "blk", None, None),
        ),
        check_vma=False,
    )
```

```python
import functools

import jax
import jax.numpy as jnp
from jax import lax
from jax.experimental import pallas as pl
from jax.experimental.pallas import tpu as pltpu
from jax.sharding import PartitionSpec as P

MESH = pl.DeviceIdType.MESH
VMEM_SPEC = pl.BlockSpec(memory_space=pltpu.VMEM)
SMEM_SPEC = pl.BlockSpec(memory_space=pltpu.SMEM)
ANY_SPEC = pl.BlockSpec(memory_space=pl.ANY)
F32 = jnp.float32
BF16 = jnp.bfloat16
NB = 16
NU = 12
NC = 20
SB = 128
HALF = NU // 2
ROWS = 16
NCH = SB // ROWS
PER = NC // 5
FAR = 6
CELLS = float(NB * NU * SB * SB)


def lane_tile(values):
    row = lax.broadcasted_iota(jnp.int32, (8, SB), 0)
    lane = lax.broadcasted_iota(jnp.int32, (8, SB), 1)
    tile = jnp.zeros((8, SB), F32)
    for i, entries in enumerate(values):
        for u, entry in enumerate(entries):
            tile = jnp.where((row == i) & (lane == u), entry, tile)
    return tile


def slot_mask(dim_a, dim_b):
    line_a = lax.broadcasted_iota(jnp.int32, (SB, SB), 0)
    line_b = lax.broadcasted_iota(jnp.int32, (SB, SB), 1)
    return (line_a < dim_a) & (line_b < dim_b)


def exists(off_ref, t, c):
    if c == 1:
        return t >= 1
    if c == 2:
        return t <= NU - 2
    down = (lax.axis_index("blk") + NB - off_ref[0, t]) & (NB - 1)
    return down >= 1 if c == 3 else down <= NB - 2


def source_device(off_ref, t, c):
    me = lax.axis_index("blk")
    if c == 1:
        return (me + NB - off_ref[0, t] + off_ref[0, jnp.maximum(t - 1, 0)]) & (NB - 1)
    if c == 2:
        return (me + NB - off_ref[0, t] + off_ref[0, jnp.minimum(t + 1, NU - 1)]) & (NB - 1)
    return (me + (NB - 1 if c == 3 else 1)) & (NB - 1)


def source_slot(t, c):
    if c == 1:
        return jnp.maximum(t - 1, 0)
    if c == 2:
        return jnp.minimum(t + 1, NU - 1)
    return t


def total(x):
    return jnp.sum(jnp.sum(x, axis=0, keepdims=True), axis=1, keepdims=True)


def far_entry(tiles_ref, device, row, slot):
    lane = lax.broadcasted_iota(jnp.int32, (8, SB), 1)
    rows = lax.broadcasted_iota(jnp.int32, (8, SB), 0)
    return total(jnp.where((lane == slot) & (rows == row), tiles_ref[device], 0.0))


def products(l_ref, r_ref, acc_ref, work, fresh):
    inner = []
    for c, t, x in work:
        stack = jnp.concatenate([l_ref[c + 5 * k, t] for k in range(PER)], axis=0)
        product = jnp.dot(stack, x, preferred_element_type=F32).astype(BF16)
        inner.append(jnp.concatenate([product[k * SB : (k + 1) * SB] for k in range(PER)], axis=1))
    sums = {}
    slots = {}
    for left, (c, t, _) in zip(inner, work):
        right = jnp.concatenate([r_ref[c + 5 * k, t] for k in range(PER)], axis=1)
        term = lax.dot_general(left, right, (((1,), (1,)), ((), ())), preferred_element_type=F32)
        key = id(t)
        sums[key] = sums[key] + term if key in sums else term
        slots[key] = t
    for key, t in slots.items():
        acc_ref[t] = sums[key] if fresh else acc_ref[t] + sums[key]


def main_kernel(
    nsec, off_ref, dims_ref, rank_ref, x_ref, l_hbm, r_hbm,
    prev_ref, rel1, rel2, kept_ref, state_ref, hstate_ref, coef_ref,
    lv, rv, xs, va, v3, v4, gs, ga, g3, g4, recv_v, recv_g, send_v, send_g, h0, h1, v1, vs, kept, st, hst,
    ranks, ranks_all, sums, sums_all, qt, qt_all,
    l_sem, r_sem, side_s, side_r, p1s, p1r, p2s, p2r, ts, tr, loc, zs, zr, ks, kr, fin
):
    me = lax.axis_index("blk")
    sec = lax.axis_index("sec")
    odd = sec % 2 == 1
    par = me // NCH
    lo = pl.multiple_of((me % NCH) * ROWS, ROWS)

    def section(by):
        return {"sec": (sec + by + nsec) % nsec}

    def peer(k):
        return {"blk": (me + k) % NB}

    def remote(src, dst, send, recv, where):
        return pltpu.make_async_remote_copy(
            src_ref=src, dst_ref=dst, send_sem=send, recv_sem=recv, device_id=where, device_id_type=MESH
        )

    barrier = pltpu.get_barrier_semaphore()
    for k in range(1, NB):
        pl.semaphore_signal(barrier, inc=1, device_id=peer(k), device_id_type=MESH)
    for by in (1, -1, 2, -2, 3, -3):
        pl.semaphore_signal(barrier, inc=1, device_id=section(by), device_id_type=MESH)

    def load(w, i):
        src, dst, sem = ((l_hbm, lv, l_sem), (r_hbm, rv, r_sem))[i]
        return pltpu.make_async_copy(src.at[w], dst.at[w], sem.at[w])

    for c in (0, 3, 4, 1, 2):
        for k in range(PER):
            load(c + 5 * k, 0).start()
            load(c + 5 * k, 1).start()

    def loaded(c):
        for k in range(PER):
            load(c + 5 * k, 0).wait()
            load(c + 5 * k, 1).wait()

    for u in range(NU):
        on = slot_mask(dims_ref[0, 0, u], dims_ref[0, 1, u])
        xs[u // 2, u % 2] = jnp.where(on, x_ref[u // 2, u % 2], jnp.zeros((SB, SB), BF16))
    ranks[...] = lane_tile([[rank_ref[0, u].astype(F32) for u in range(NU)]])
    sums[...] = jnp.zeros((8, SB), F32)
    pl.semaphore_wait(barrier, NB + 5)

    state_of = (xs, gs)
    recv_of = (recv_v, recv_g)
    send_of = (send_v, send_g)
    wide_of = (va, ga)
    side_of = ((v3, v4), (g3, g4))
    tile_of = (ranks, sums, qt)
    tiles_of = (ranks_all, sums_all, qt_all)

    def phase1(i, k):
        to = (me + k) % NB
        at = pl.multiple_of((to % NCH) * ROWS, ROWS)
        return remote(
            state_of[i].at[:, to // NCH, pl.ds(at, ROWS), :], recv_of[i].at[me], p1s.at[i, k], p1r.at[i, k], peer(k)
        )

    def mine(ref):
        return ref.at[:, pl.ds(par, HALF), 1 - par, pl.ds(lo, ROWS), :]

    def phase2(i, k):
        return remote(send_of[i].at[(me + k) % NB], mine(wide_of[i]), p2s.at[i, k], p2r.at[i, k], peer(k))

    def side(i, j):
        return remote(state_of[i], side_of[i][j], side_s.at[i, j], side_r.at[i, j], peer((1, NB - 1)[j]))

    def tiny(i, k):
        return remote(tile_of[i], tiles_of[i].at[me], ts.at[i, k], tr.at[i, k], peer(k))

    def own1(i):
        return pltpu.make_async_copy(state_of[i].at[:, par, pl.ds(lo, ROWS), :], recv_of[i].at[me], loc.at[i, 0])

    def own2(i):
        return pltpu.make_async_copy(send_of[i].at[me], mine(wide_of[i]), loc.at[i, 1])

    def direct(channels):
        part = pl.ds(0, channels)
        return remote(l_hbm.at[part], prev_ref.at[part], zs.at[0], zr.at[0], section(1))

    far = pl.ds(NC - FAR, FAR)

    def hop(i):
        if i == 0:
            return remote(l_hbm.at[far], rel1, zs.at[1], zr.at[1], section(-2))
        if i == 1:
            return remote(rel1, rel2, zs.at[2], zr.at[2], section(-2))
        return remote(rel2, prev_ref.at[far], zs.at[3], zr.at[3], section(-3))

    def begin(i):
        @pl.loop(1, NB)
        def _(k):
            phase1(i, k).start()

        own1(i).start()

    def middle(i):
        own1(i).wait()

        @pl.loop(1, NB)
        def _(k):
            phase1(i, k).wait_recv()

        @pl.loop(0, NB)
        def _(t):
            for r in range(HALF):
                up = 2 * r + par
                own = off_ref[0, up] + t + NB
                above = (own - off_ref[0, jnp.minimum(up + 1, NU - 1)]) & (NB - 1)
                below = (own - off_ref[0, jnp.maximum(up - 1, 0)]) & (NB - 1)
                send_of[i][t, 0, r] = recv_of[i][above, r]
                send_of[i][t, 1, r] = recv_of[i][below, r]

        @pl.loop(1, NB)
        def _(k):
            phase2(i, k).start()

        own2(i).start()

    def end(i):
        own2(i).wait()

        @pl.loop(1, NB)
        def _(k):
            phase2(i, k).wait_recv()

    begin(0)

    @pl.when(odd)
    def _():
        direct(NC - FAR).start()
        hop(0).start()

    @pl.when(jnp.logical_not(odd))
    def _():
        direct(NC).start()

    for j in range(2):
        side(0, j).start()

    @pl.loop(1, NB)
    def _(k):
        tiny(0, k).start()

    ranks_all[me] = ranks[...]
    middle(0)

    def own_v(t):
        return xs[t // 2, t % 2]

    def source(i, c, t):
        if c == 1:
            at = jnp.maximum(t, 1)
            return wide_of[i][0, at // 2, at % 2]
        if c == 2:
            at = jnp.minimum(t + 2, NU)
            return wide_of[i][1, at // 2, at % 2]
        return side_of[i][c - 3][t // 2, t % 2]

    def first_source(c, t):
        return jnp.where(exists(off_ref, t, c), source(0, c, t), jnp.zeros((SB, SB), BF16))

    loaded(0)

    @pl.loop(0, NU, step=2)
    def _(t0):
        ts_ = [t0, t0 + 1]
        products(lv, rv, h0, [(0, t, own_v(t)) for t in ts_], True)

    for j in range(2):
        side(0, j).wait_recv()
    loaded(3)
    loaded(4)

    @pl.loop(0, NU)
    def _(t):
        products(lv, rv, h0, [(c, t, first_source(c, t)) for c in (3, 4)], False)

    end(0)
    loaded(1)
    loaded(2)

    @pl.loop(0, NU)
    def _(t):
        products(lv, rv, h0, [(c, t, first_source(c, t)) for c in (1, 2)], False)
        h = jnp.where(slot_mask(dims_ref[0, 0, t], dims_ref[0, 1, t]), h0[t], 0.0)
        v = own_v(t).astype(F32)
        n = total(v * v)
        p = total(v * h)
        alpha = jnp.where(n > 0.0, p / jnp.where(n > 0.0, n, 1.0), 0.0)
        g = h - alpha * v
        h0[t] = h
        gs[t // 2, t % 2] = g.astype(BF16)
        rest = total(g * g)
        rows = lax.broadcasted_iota(jnp.int32, (8, SB), 0)
        lanes = lax.broadcasted_iota(jnp.int32, (8, SB), 1)
        entry = jnp.where(rows == 0, n, jnp.where(rows == 1, p, jnp.where(rows == 2, rest, alpha)))
        sums[...] = jnp.where((lanes == t) & (rows < 4), entry, sums[...])

    @pl.loop(1, NB)
    def _(k):
        tiny(1, k).start()

    begin(1)
    for j in range(2):
        side(1, j).start()
    sums_all[me] = sums[...]

    @pl.when(odd)
    def _():
        hop(0).wait_recv()
        hop(1).start()

    @pl.loop(1, NB)
    def _(k):
        tiny(1, k).wait_recv()

    every = sums_all[...]
    nt, pt, rt, at = every[:, 0, :], every[:, 1, :], every[:, 2, :], every[:, 3, :]
    norm = total(nt)
    a0 = total(pt) / norm
    gap = at - a0
    beta = jnp.sqrt(total(rt + gap * gap * nt) / norm + 1e-6)
    scale = jnp.sqrt(CELLS / norm)
    kappa = scale / beta

    def second_source(c, t):
        alpha = far_entry(sums_all, source_device(off_ref, t, c), 3, source_slot(t, c))
        x = kappa * (source(1, c, t).astype(F32) + (alpha - a0) * source(0, c, t).astype(F32))
        x = jnp.where(exists(off_ref, t, c), x, 0.0).astype(BF16)
        vs[c - 1, t] = x
        return x

    middle(1)

    @pl.loop(0, NU, step=2)
    def _(t0):
        work = []
        for t in (t0, t0 + 1):
            x = (kappa * (h0[t] - a0 * own_v(t).astype(F32))).astype(BF16)
            v1[t] = x
            work.append((0, t, x))
        products(lv, rv, h1, work, True)

    for j in range(2):
        side(1, j).wait_recv()

    @pl.loop(0, NU)
    def _(t):
        products(lv, rv, h1, [(c, t, second_source(c, t)) for c in (3, 4)], False)

    end(1)
    qt[...] = jnp.zeros((8, SB), F32)

    @pl.loop(0, NU)
    def _(t):
        products(lv, rv, h1, [(c, t, second_source(c, t)) for c in (1, 2)], False)
        h = jnp.where(slot_mask(dims_ref[0, 0, t], dims_ref[0, 1, t]), h1[t], 0.0)
        h1[t] = h
        qt[0:1, :] += jnp.sum(v1[t].astype(F32) * h, axis=0, keepdims=True)

    @pl.loop(1, NB)
    def _(k):
        tiny(2, k).start()

    qt_all[me] = qt[...]

    @pl.when(odd)
    def _():
        hop(1).wait_recv()
        hop(2).start()

    @pl.loop(1, NB)
    def _(k):
        tiny(0, k).wait_recv()
        tiny(2, k).wait_recv()

    a1 = total(jnp.sum(qt_all[...], axis=0)) / CELLS
    half = (a0 - a1) / 2.0
    ritz = (a0 + a1) / 2.0 - jnp.sqrt(half * half + beta * beta)
    slip = ritz - a0
    length = jnp.sqrt(beta * beta + slip * slip)
    xcoef, ycoef = beta / length, slip / length
    coef_ref[...] = jnp.broadcast_to(ritz, (8, SB))
    lane = lax.broadcasted_iota(jnp.int32, (SB, SB), 1).astype(F32)

    def onward(c):
        return remote(kept.at[c], kept_ref.at[c], ks.at[c], kr.at[c], section(1))

    for c in range(5):

        @pl.loop(0, NU)
        def _(t):
            if c == 0:
                x = (xcoef * (own_v(t).astype(F32) * scale) + ycoef * v1[t].astype(F32)).astype(BF16)
                st[t] = x
                on = lane < far_entry(ranks_all, me, 0, t)
            else:
                x = xcoef * (source(0, c, t).astype(F32) * scale) + ycoef * vs[c - 1, t].astype(F32)
                rank = far_entry(ranks_all, source_device(off_ref, t, c), 0, source_slot(t, c))
                on = (lane < rank) & exists(off_ref, t, c)
            kept[c, t] = jnp.where(on, x.astype(F32), 0.0).astype(BF16)

        if c:
            onward(c - 1).start()

    @pl.loop(0, NU)
    def _(t):
        hst[t] = (xcoef * (h0[t] * scale) + ycoef * h1[t]).astype(BF16)

    onward(4).start()
    outs = [
        pltpu.make_async_copy(st, state_ref, fin.at[0]),
        pltpu.make_async_copy(hst, hstate_ref, fin.at[1]),
    ]
    for copy in outs:
        copy.start()

    for i in range(2):
        for j in range(2):
            side(i, j).wait_send()

    @pl.loop(1, NB)
    def _(k):
        for i in range(2):
            phase1(i, k).wait_send()
            phase2(i, k).wait_send()
        for i in range(3):
            tiny(i, k).wait_send()

    for copy in outs:
        copy.wait()

    @pl.when(odd)
    def _():
        direct(NC - FAR).wait_send()
        for i in range(3):
            hop(i).wait_send()
        direct(NC).wait_recv()

    @pl.when(jnp.logical_not(odd))
    def _():
        direct(NC).wait_send()
        direct(NC - FAR).wait_recv()
        hop(2).wait_recv()

    for c in range(5):
        onward(c).wait()


def main_call(nsec, offsets, dims, ranks, x, lenv, renv):
    pair = (HALF, 2, SB, SB)
    flat = (NU, SB, SB)
    tile, tiles = (8, SB), (NB, 8, SB)
    far = jax.ShapeDtypeStruct((FAR, NU, SB, SB), BF16)
    wide = pltpu.VMEM((2, HALF + 1, 2, SB, SB), BF16)
    bf = lambda *shape: pltpu.VMEM(shape, BF16)
    f32 = lambda *shape: pltpu.VMEM(shape, F32)
    dma = lambda *shape: pltpu.SemaphoreType.DMA(shape)
    return pl.pallas_call(
        functools.partial(main_kernel, nsec),
        out_shape=[
            jax.ShapeDtypeStruct((NC,) + flat, BF16),
            far,
            far,
            jax.ShapeDtypeStruct((5,) + flat, BF16),
            jax.ShapeDtypeStruct(flat, BF16),
            jax.ShapeDtypeStruct(flat, BF16),
            jax.ShapeDtypeStruct(tile, F32),
        ],
        in_specs=[SMEM_SPEC, SMEM_SPEC, SMEM_SPEC, VMEM_SPEC, ANY_SPEC, ANY_SPEC],
        out_specs=[ANY_SPEC] * 6 + [VMEM_SPEC],
        scratch_shapes=[
            bf(NC, *flat), bf(NC, *flat), bf(*pair), wide, bf(*pair), bf(*pair), bf(*pair), wide, bf(*pair), bf(*pair),
            bf(NB, HALF, ROWS, SB), bf(NB, HALF, ROWS, SB),
            bf(NB, 2, HALF, ROWS, SB), bf(NB, 2, HALF, ROWS, SB),
            f32(*flat), f32(*flat), bf(*flat), bf(4, *flat), bf(5, *flat), bf(*flat), bf(*flat),
            f32(*tile), f32(*tiles), f32(*tile), f32(*tiles), f32(*tile), f32(*tiles),
            dma(NC), dma(NC), dma(2, 2), dma(2, 2), dma(2, NB), dma(2, NB), dma(2, NB), dma(2, NB),
            dma(3, NB), dma(3, NB), dma(2, 2), dma(4), dma(4), dma(5), dma(5), dma(2),
        ],
        compiler_params=pltpu.CompilerParams(collective_id=0, has_side_effects=True),
        name="davidson",
    )(offsets, dims, ranks, x, lenv, renv)


def update_kernel(slots, head_ref, coef_ref, own_ref, l_ref, k_ref, si_ref, hi_ref, next_ref, s_ref, hs_ref, e_ref):
    first_section = head_ref[0] == 1
    s_ref[...] = si_ref[...]
    hs_ref[...] = hi_ref[...]
    e_ref[0] = coef_ref[0, 0]

    @pl.when(first_section)
    def _():
        next_ref[...] = own_ref[...]

    @pl.when(jnp.logical_not(first_section))
    def _():
        for i in range(slots):
            kept = k_ref[0, i]
            for c in range(5):
                stack = jnp.concatenate([l_ref[c + 5 * k, i] for k in range(PER)], axis=0)
                inner = jnp.dot(stack, k_ref[c, i], preferred_element_type=F32).astype(BF16)
                wide = jnp.concatenate([inner[k * SB : (k + 1) * SB] for k in range(PER)], axis=1)
                out = lax.dot_general(kept, wide, (((0,), (0,)), ((), ())), preferred_element_type=F32).astype(BF16)
                for k in range(PER):
                    next_ref[c + 5 * k, i] = out[:, k * SB : (k + 1) * SB]


SLOTS = 2


def update(head, coef, lenv, prev, kept, state, hstate):
    tile = pl.BlockSpec((8, SB), lambda t, *_: (0, 0))
    one = pl.BlockSpec((SLOTS, SB, SB), lambda t, *_: (t, 0, 0))
    env = (NC, SLOTS, SB, SB)
    own = pl.BlockSpec(env, lambda t, head: (0, t * head[0], 0, 0))
    far = pl.BlockSpec(env, lambda t, head: (0, t * (1 - head[0]), 0, 0))
    flat = jax.ShapeDtypeStruct((NU, SB, SB), BF16)
    return pl.pallas_call(
        functools.partial(update_kernel, SLOTS),
        grid_spec=pltpu.PrefetchScalarGridSpec(
            num_scalar_prefetch=1,
            grid=(NU // SLOTS,),
            in_specs=[tile, own, far, pl.BlockSpec((5, SLOTS, SB, SB), lambda t, *_: (0, t, 0, 0)), one, one],
            out_specs=[pl.BlockSpec(env, lambda t, *_: (0, t, 0, 0)), one, one, SMEM_SPEC],
        ),
        out_shape=[
            jax.ShapeDtypeStruct((NC, NU, SB, SB), BF16),
            flat,
            flat,
            jax.ShapeDtypeStruct((1,), F32),
        ],
        name="update",
    )(head, coef, lenv, prev, kept, state, hstate)


def shards(wavefunction, left_env, right_env, offsets, dims, ranks):
    nsec = lax.axis_size("sec")
    lenv, renv = left_env[0], right_env[0]
    prev, _, _, kept, state, hstate, coef = main_call(
        nsec, offsets, dims.transpose(0, 2, 1), ranks, wavefunction[0].reshape((HALF, 2, SB, SB)), lenv, renv
    )
    head = jnp.where(lax.axis_index("sec") == 0, 1, 0).astype(jnp.int32).reshape((1,))
    next_left, state, hstate, energy = update(head, coef, lenv, prev, kept, state, hstate)
    return state[None], hstate[None], energy, next_left[None]


def solution(mesh):
    placed = (
        P("sec", "blk", None, None),
        P("sec", None, "blk", None, None),
        P("sec", None, "blk", None, None),
        P("sec", None),
        P("sec", "blk", None),
        P("sec", "blk"),
    )
    return jax.shard_map(
        shards,
        mesh=mesh,
        in_specs=placed,
        out_specs=(
            P("sec", "blk", None, None),
            P("sec", "blk", None, None),
            P("sec"),
            P("sec", None, "blk", None, None),
        ),
        check_vma=False,
    )
```

```python
import functools

import jax
import jax.numpy as jnp
from jax import lax
from jax.experimental import pallas as pl
from jax.experimental.pallas import tpu as pltpu
from jax.sharding import PartitionSpec as P

MESH = pl.DeviceIdType.MESH
VMEM_SPEC = pl.BlockSpec(memory_space=pltpu.VMEM)
SMEM_SPEC = pl.BlockSpec(memory_space=pltpu.SMEM)
ANY_SPEC = pl.BlockSpec(memory_space=pl.ANY)
F32 = jnp.float32
BF16 = jnp.bfloat16
NB = 16
NU = 12
NC = 20
SB = 128
HALF = NU // 2
ROWS = 16
NCH = SB // ROWS
PER = NC // 5
FAR = 5
CELLS = float(NB * NU * SB * SB)


def slot_tile(entries):
    row = lax.broadcasted_iota(jnp.int32, (16, SB), 0)
    tile = jnp.zeros((16, SB), F32)
    for u, entry in enumerate(entries):
        tile = jnp.where(row == u, entry, tile)
    return tile


def slot_mask(dim_a, dim_b):
    line_a = lax.broadcasted_iota(jnp.int32, (SB, SB), 0)
    line_b = lax.broadcasted_iota(jnp.int32, (SB, SB), 1)
    return (line_a < dim_a) & (line_b < dim_b)


def exists(off_ref, t, c):
    if c == 1:
        return t >= 1
    if c == 2:
        return t <= NU - 2
    down = (lax.axis_index("blk") + NB - off_ref[0, t]) & (NB - 1)
    return down >= 1 if c == 3 else down <= NB - 2


def source_device(off_ref, t, c):
    me = lax.axis_index("blk")
    if c == 1:
        return (me + NB - off_ref[0, t] + off_ref[0, jnp.maximum(t - 1, 0)]) & (NB - 1)
    if c == 2:
        return (me + NB - off_ref[0, t] + off_ref[0, jnp.minimum(t + 1, NU - 1)]) & (NB - 1)
    return (me + (NB - 1 if c == 3 else 1)) & (NB - 1)


def source_slot(t, c):
    if c == 1:
        return jnp.maximum(t - 1, 0)
    if c == 2:
        return jnp.minimum(t + 1, NU - 1)
    return t


def total(x):
    return jnp.sum(jnp.sum(x, axis=0, keepdims=True), axis=1, keepdims=True)


def products(l_ref, r_ref, acc_ref, work, fresh):
    inner = []
    for c, t, x in work:
        stack = jnp.concatenate([l_ref[c + 5 * k, t] for k in range(PER)], axis=0)
        product = jnp.dot(stack, x, preferred_element_type=F32).astype(BF16)
        inner.append(jnp.concatenate([product[k * SB : (k + 1) * SB] for k in range(PER)], axis=1))
    sums = {}
    slots = {}
    for left, (c, t, _) in zip(inner, work):
        right = jnp.concatenate([r_ref[c + 5 * k, t] for k in range(PER)], axis=1)
        term = lax.dot_general(left, right, (((1,), (1,)), ((), ())), preferred_element_type=F32)
        key = id(t)
        sums[key] = sums[key] + term if key in sums else term
        slots[key] = t
    for key, t in slots.items():
        acc_ref[t] = sums[key] if fresh else acc_ref[t] + sums[key]


def main_kernel(
    nsec, off_ref, dims_ref, rank_ref, x_ref, l_hbm, r_hbm,
    prev_ref, rel1, rel2, kept_ref, state_ref, hstate_ref, coef_ref,
    lv, rv, xs, va, v3, v4, gs, ga, g3, g4, recv_v, recv_g, send_v, send_g, h0, h1, v1, vs, kept, st, hst,
    ranks, ranks_all, sums, sums_all, qt, qt_all, part_n, part_p, part_r, alphas, alpha_all,
    l_sem, r_sem, side_s, side_r, p1s, p1r, p2s, p2r, ts, tr, loc, zs, zr, ks, kr, fin
):
    me = lax.axis_index("blk")
    sec = lax.axis_index("sec")
    odd = sec % 2 == 1
    par = me // NCH
    lo = pl.multiple_of((me % NCH) * ROWS, ROWS)

    def section(by):
        return {"sec": (sec + by + nsec) % nsec}

    def peer(k):
        return {"blk": (me + k) % NB}

    def remote(src, dst, send, recv, where):
        return pltpu.make_async_remote_copy(
            src_ref=src, dst_ref=dst, send_sem=send, recv_sem=recv, device_id=where, device_id_type=MESH
        )

    barrier = pltpu.get_barrier_semaphore()
    for k in range(1, NB):
        pl.semaphore_signal(barrier, inc=1, device_id=peer(k), device_id_type=MESH)
    for by in (1, -1, 2, -2, 3, -3):
        pl.semaphore_signal(barrier, inc=1, device_id=section(by), device_id_type=MESH)

    def load(w, i):
        src, dst, sem = ((l_hbm, lv, l_sem), (r_hbm, rv, r_sem))[i]
        return pltpu.make_async_copy(src.at[w], dst.at[w], sem.at[w])

    for c in (0, 3, 4, 1, 2):
        for k in range(PER):
            load(c + 5 * k, 0).start()
            load(c + 5 * k, 1).start()

    def loaded(c):
        for k in range(PER):
            load(c + 5 * k, 0).wait()
            load(c + 5 * k, 1).wait()

    for u in range(NU):
        on = slot_mask(dims_ref[0, 0, u], dims_ref[0, 1, u])
        xs[u // 2, u % 2] = jnp.where(on, x_ref[u // 2, u % 2], jnp.zeros((SB, SB), BF16))
    ranks[...] = slot_tile([rank_ref[0, u].astype(F32) for u in range(NU)])
    for ref in (part_n, part_p, part_r):
        ref[...] = jnp.zeros((16, SB), F32)
    pl.semaphore_wait(barrier, NB + 5)

    state_of = (xs, gs)
    recv_of = (recv_v, recv_g)
    send_of = (send_v, send_g)
    wide_of = (va, ga)
    side_of = ((v3, v4), (g3, g4))
    tile_of = (ranks, sums, qt)
    tiles_of = (ranks_all, sums_all, qt_all)

    def phase1(i, k):
        to = (me + k) % NB
        at = pl.multiple_of((to % NCH) * ROWS, ROWS)
        return remote(
            state_of[i].at[:, to // NCH, pl.ds(at, ROWS), :], recv_of[i].at[me], p1s.at[i, k], p1r.at[i, k], peer(k)
        )

    def mine(ref):
        return ref.at[:, pl.ds(par, HALF), 1 - par, pl.ds(lo, ROWS), :]

    def phase2(i, k):
        return remote(send_of[i].at[(me + k) % NB], mine(wide_of[i]), p2s.at[i, k], p2r.at[i, k], peer(k))

    def side(i, j):
        return remote(state_of[i], side_of[i][j], side_s.at[i, j], side_r.at[i, j], peer((1, NB - 1)[j]))

    def tiny(i, k):
        return remote(tile_of[i], tiles_of[i].at[me], ts.at[i, k], tr.at[i, k], peer(k))

    def own1(i):
        return pltpu.make_async_copy(state_of[i].at[:, par, pl.ds(lo, ROWS), :], recv_of[i].at[me], loc.at[i, 0])

    def own2(i):
        return pltpu.make_async_copy(send_of[i].at[me], mine(wide_of[i]), loc.at[i, 1])

    def direct(channels):
        part = pl.ds(0, channels)
        return remote(l_hbm.at[part], prev_ref.at[part], zs.at[0], zr.at[0], section(1))

    far = pl.ds(NC - FAR, FAR)

    def hop(i):
        if i == 0:
            return remote(l_hbm.at[far], rel1, zs.at[1], zr.at[1], section(-2))
        if i == 1:
            return remote(rel1, rel2, zs.at[2], zr.at[2], section(-2))
        return remote(rel2, prev_ref.at[far], zs.at[3], zr.at[3], section(-3))

    def begin(i):
        @pl.loop(1, NB)
        def _(k):
            phase1(i, k).start()

        own1(i).start()

    def middle(i):
        own1(i).wait()

        @pl.loop(1, NB)
        def _(k):
            phase1(i, k).wait_recv()

        @pl.loop(0, NB)
        def _(t):
            for r in range(HALF):
                up = 2 * r + par
                own = off_ref[0, up] + t + NB
                above = (own - off_ref[0, jnp.minimum(up + 1, NU - 1)]) & (NB - 1)
                below = (own - off_ref[0, jnp.maximum(up - 1, 0)]) & (NB - 1)
                send_of[i][t, 0, r] = recv_of[i][above, r]
                send_of[i][t, 1, r] = recv_of[i][below, r]

        @pl.loop(1, NB)
        def _(k):
            phase2(i, k).start()

        own2(i).start()

    def end(i):
        own2(i).wait()

        @pl.loop(1, NB)
        def _(k):
            phase2(i, k).wait_recv()

    begin(0)

    @pl.when(odd)
    def _():
        direct(NC - FAR).start()
        hop(0).start()

    @pl.when(jnp.logical_not(odd))
    def _():
        direct(NC).start()

    for j in range(2):
        side(0, j).start()

    @pl.loop(1, NB)
    def _(k):
        tiny(0, k).start()

    ranks_all[me] = ranks[...]
    middle(0)

    def own_v(t):
        return xs[t // 2, t % 2]

    def source(i, c, t):
        if c == 1:
            at = jnp.maximum(t, 1)
            return wide_of[i][0, at // 2, at % 2]
        if c == 2:
            at = jnp.minimum(t + 2, NU)
            return wide_of[i][1, at // 2, at % 2]
        return side_of[i][c - 3][t // 2, t % 2]

    def first_source(c, t):
        return jnp.where(exists(off_ref, t, c), source(0, c, t), jnp.zeros((SB, SB), BF16))

    loaded(0)

    @pl.loop(0, NU, step=2)
    def _(t0):
        pair = [t0, t0 + 1]
        products(lv, rv, h0, [(0, t, own_v(t)) for t in pair], True)
        for t in pair:
            v = own_v(t).astype(F32)
            part_n[pl.ds(t, 1), :] = jnp.sum(v * v, axis=0, keepdims=True)

    for j in range(2):
        side(0, j).wait_recv()
    loaded(3)
    loaded(4)

    @pl.loop(0, NU)
    def _(t):
        products(lv, rv, h0, [(c, t, first_source(c, t)) for c in (3, 4)], False)

    end(0)
    loaded(1)
    loaded(2)

    @pl.loop(0, NU, step=2)
    def _(t0):
        pair = [t0, t0 + 1]
        products(lv, rv, h0, [(c, t, first_source(c, t)) for t in pair for c in (1, 2)], False)
        for t in pair:
            h = jnp.where(slot_mask(dims_ref[0, 0, t], dims_ref[0, 1, t]), h0[t], 0.0)
            h0[t] = h
            part_p[pl.ds(t, 1), :] = jnp.sum(own_v(t).astype(F32) * h, axis=0, keepdims=True)

    n_own = jnp.sum(part_n[...], axis=1, keepdims=True)
    p_own = jnp.sum(part_p[...], axis=1, keepdims=True)
    alpha_own = jnp.where(n_own > 0.0, p_own / jnp.where(n_own > 0.0, n_own, 1.0), 0.0)
    alphas[...] = jnp.broadcast_to(alpha_own, (16, SB))

    @pl.loop(0, NU, step=2)
    def _(t0):
        for t in (t0, t0 + 1):
            g = h0[t] - alphas[pl.ds(t, 1), :] * own_v(t).astype(F32)
            gs[t // 2, t % 2] = g.astype(BF16)
            part_r[pl.ds(t, 1), :] = jnp.sum(g * g, axis=0, keepdims=True)

    r_own = jnp.sum(part_r[...], axis=1, keepdims=True)
    lanes = lax.broadcasted_iota(jnp.int32, (16, SB), 1)
    sums[...] = jnp.where(lanes == 0, n_own, jnp.where(lanes == 1, p_own, jnp.where(lanes == 2, r_own, alpha_own)))
    begin(1)

    @pl.loop(1, NB)
    def _(k):
        tiny(1, k).start()

    for j in range(2):
        side(1, j).start()
    sums_all[me] = sums[...]

    @pl.when(odd)
    def _():
        hop(0).wait_recv()
        hop(1).start()

    @pl.loop(1, NB)
    def _(k):
        tiny(1, k).wait_recv()

    every = sums_all[...]
    place = lax.broadcasted_iota(jnp.int32, (NB, 16, SB), 2)
    nt, pt, rt, at = [jnp.sum(jnp.where(place == i, every, 0.0), axis=2, keepdims=True) for i in range(4)]
    alpha_all[...] = jnp.broadcast_to(at, (NB, 16, SB))
    norm = total(jnp.sum(nt, axis=0))
    a0 = total(jnp.sum(pt, axis=0)) / norm
    gap = at - a0
    beta = jnp.sqrt(total(jnp.sum(rt + gap * gap * nt, axis=0)) / norm + 1e-6)
    scale = jnp.sqrt(CELLS / norm)
    kappa = scale / beta

    def second_source(c, t):
        alpha = alpha_all[source_device(off_ref, t, c), pl.ds(source_slot(t, c), 1), :]
        x = kappa * (source(1, c, t).astype(F32) + (alpha - a0) * source(0, c, t).astype(F32))
        x = jnp.where(exists(off_ref, t, c), x, 0.0).astype(BF16)
        vs[c - 1, t] = x
        return x

    middle(1)

    @pl.loop(0, NU, step=2)
    def _(t0):
        work = []
        for t in (t0, t0 + 1):
            x = (kappa * (h0[t] - a0 * own_v(t).astype(F32))).astype(BF16)
            v1[t] = x
            work.append((0, t, x))
        products(lv, rv, h1, work, True)

    for j in range(2):
        side(1, j).wait_recv()

    @pl.loop(0, NU)
    def _(t):
        products(lv, rv, h1, [(c, t, second_source(c, t)) for c in (3, 4)], False)

    end(1)
    qt[...] = jnp.zeros((8, SB), F32)

    @pl.loop(0, NU, step=2)
    def _(t0):
        pair = [t0, t0 + 1]
        products(lv, rv, h1, [(c, t, second_source(c, t)) for t in pair for c in (1, 2)], False)
        for t in pair:
            h = jnp.where(slot_mask(dims_ref[0, 0, t], dims_ref[0, 1, t]), h1[t], 0.0)
            h1[t] = h
            qt[0:1, :] += jnp.sum(v1[t].astype(F32) * h, axis=0, keepdims=True)

    @pl.loop(1, NB)
    def _(k):
        tiny(2, k).start()

    qt_all[me] = qt[...]

    @pl.when(odd)
    def _():
        hop(1).wait_recv()
        hop(2).start()

    @pl.loop(1, NB)
    def _(k):
        tiny(0, k).wait_recv()
        tiny(2, k).wait_recv()

    a1 = total(jnp.sum(qt_all[...], axis=0)) / CELLS
    half = (a0 - a1) / 2.0
    ritz = (a0 + a1) / 2.0 - jnp.sqrt(half * half + beta * beta)
    slip = ritz - a0
    length = jnp.sqrt(beta * beta + slip * slip)
    xcoef, ycoef = beta / length, slip / length
    coef_ref[...] = jnp.broadcast_to(ritz, (8, SB))
    lane = lax.broadcasted_iota(jnp.int32, (1, SB), 1).astype(F32)
    v_coef = xcoef * scale

    def onward(c):
        return remote(kept.at[c], kept_ref.at[c], ks.at[c], kr.at[c], section(1))

    for c in range(5):

        @pl.loop(0, NU, step=2)
        def _(t0):
            for t in (t0, t0 + 1):
                if c == 0:
                    x = (v_coef * own_v(t).astype(F32) + ycoef * v1[t].astype(F32)).astype(BF16)
                    st[t] = x
                    on = lane < ranks[pl.ds(t, 1), :]
                else:
                    x = v_coef * source(0, c, t).astype(F32) + ycoef * vs[c - 1, t].astype(F32)
                    rank = ranks_all[source_device(off_ref, t, c), pl.ds(source_slot(t, c), 1), :]
                    on = (lane < rank) & exists(off_ref, t, c)
                kept[c, t] = jnp.where(on, x.astype(F32), 0.0).astype(BF16)

        if c:
            onward(c - 1).start()

    onward(4).start()

    @pl.loop(0, NU)
    def _(t):
        hst[t] = (v_coef * h0[t] + ycoef * h1[t]).astype(BF16)

    outs = [
        pltpu.make_async_copy(st, state_ref, fin.at[0]),
        pltpu.make_async_copy(hst, hstate_ref, fin.at[1]),
    ]
    for copy in outs:
        copy.start()

    for i in range(2):
        for j in range(2):
            side(i, j).wait_send()

    @pl.loop(1, NB)
    def _(k):
        for i in range(2):
            phase1(i, k).wait_send()
            phase2(i, k).wait_send()
        for i in range(3):
            tiny(i, k).wait_send()

    for copy in outs:
        copy.wait()

    @pl.when(odd)
    def _():
        direct(NC - FAR).wait_send()
        for i in range(3):
            hop(i).wait_send()
        direct(NC).wait_recv()

    @pl.when(jnp.logical_not(odd))
    def _():
        direct(NC).wait_send()
        direct(NC - FAR).wait_recv()
        hop(2).wait_recv()

    for c in range(5):
        onward(c).wait()


def main_call(nsec, offsets, dims, ranks, x, lenv, renv):
    pair = (HALF, 2, SB, SB)
    flat = (NU, SB, SB)
    tile, slots = (8, SB), (16, SB)
    far = jax.ShapeDtypeStruct((FAR, NU, SB, SB), BF16)
    wide = pltpu.VMEM((2, HALF + 1, 2, SB, SB), BF16)
    bf = lambda *shape: pltpu.VMEM(shape, BF16)
    f32 = lambda *shape: pltpu.VMEM(shape, F32)
    dma = lambda *shape: pltpu.SemaphoreType.DMA(shape)
    return pl.pallas_call(
        functools.partial(main_kernel, nsec),
        out_shape=[
            jax.ShapeDtypeStruct((NC,) + flat, BF16),
            far,
            far,
            jax.ShapeDtypeStruct((5,) + flat, BF16),
            jax.ShapeDtypeStruct(flat, BF16),
            jax.ShapeDtypeStruct(flat, BF16),
            jax.ShapeDtypeStruct(tile, F32),
        ],
        in_specs=[SMEM_SPEC, SMEM_SPEC, SMEM_SPEC, VMEM_SPEC, ANY_SPEC, ANY_SPEC],
        out_specs=[ANY_SPEC] * 6 + [VMEM_SPEC],
        scratch_shapes=[
            bf(NC, *flat), bf(NC, *flat), bf(*pair), wide, bf(*pair), bf(*pair), bf(*pair), wide, bf(*pair), bf(*pair),
            bf(NB, HALF, ROWS, SB), bf(NB, HALF, ROWS, SB),
            bf(NB, 2, HALF, ROWS, SB), bf(NB, 2, HALF, ROWS, SB),
            f32(*flat), f32(*flat), bf(*flat), bf(4, *flat), bf(5, *flat), bf(*flat), bf(*flat),
            f32(*slots), f32(NB, *slots), f32(*slots), f32(NB, *slots), f32(*tile), f32(NB, *tile),
            f32(*slots), f32(*slots), f32(*slots), f32(*slots), f32(NB, *slots),
            dma(NC), dma(NC), dma(2, 2), dma(2, 2), dma(2, NB), dma(2, NB), dma(2, NB), dma(2, NB),
            dma(3, NB), dma(3, NB), dma(2, 2), dma(4), dma(4), dma(5), dma(5), dma(2),
        ],
        compiler_params=pltpu.CompilerParams(collective_id=0, has_side_effects=True),
        name="davidson",
    )(offsets, dims, ranks, x, lenv, renv)


def update_kernel(slots, head_ref, coef_ref, own_ref, l_ref, k_ref, si_ref, hi_ref, next_ref, s_ref, hs_ref, e_ref):
    first_section = head_ref[0] == 1
    s_ref[...] = si_ref[...]
    hs_ref[...] = hi_ref[...]
    e_ref[0] = coef_ref[0, 0]

    @pl.when(first_section)
    def _():
        next_ref[...] = own_ref[...]

    @pl.when(jnp.logical_not(first_section))
    def _():
        for i in range(slots):
            kept = k_ref[0, i]
            for c in range(5):
                stack = jnp.concatenate([l_ref[c + 5 * k, i] for k in range(PER)], axis=0)
                inner = jnp.dot(stack, k_ref[c, i], preferred_element_type=F32).astype(BF16)
                wide = jnp.concatenate([inner[k * SB : (k + 1) * SB] for k in range(PER)], axis=1)
                out = lax.dot_general(kept, wide, (((0,), (0,)), ((), ())), preferred_element_type=F32).astype(BF16)
                for k in range(PER):
                    next_ref[c + 5 * k, i] = out[:, k * SB : (k + 1) * SB]


SLOTS = 2


def update(head, coef, lenv, prev, kept, state, hstate):
    tile = pl.BlockSpec((8, SB), lambda t, *_: (0, 0))
    one = pl.BlockSpec((SLOTS, SB, SB), lambda t, *_: (t, 0, 0))
    env = (NC, SLOTS, SB, SB)
    own = pl.BlockSpec(env, lambda t, head: (0, t * head[0], 0, 0))
    far = pl.BlockSpec(env, lambda t, head: (0, t * (1 - head[0]), 0, 0))
    flat = jax.ShapeDtypeStruct((NU, SB, SB), BF16)
    return pl.pallas_call(
        functools.partial(update_kernel, SLOTS),
        grid_spec=pltpu.PrefetchScalarGridSpec(
            num_scalar_prefetch=1,
            grid=(NU // SLOTS,),
            in_specs=[tile, own, far, pl.BlockSpec((5, SLOTS, SB, SB), lambda t, *_: (0, t, 0, 0)), one, one],
            out_specs=[pl.BlockSpec(env, lambda t, *_: (0, t, 0, 0)), one, one, SMEM_SPEC],
        ),
        out_shape=[
            jax.ShapeDtypeStruct((NC, NU, SB, SB), BF16),
            flat,
            flat,
            jax.ShapeDtypeStruct((1,), F32),
        ],
        name="update",
    )(head, coef, lenv, prev, kept, state, hstate)


def shards(wavefunction, left_env, right_env, offsets, dims, ranks):
    nsec = lax.axis_size("sec")
    lenv, renv = left_env[0], right_env[0]
    prev, _, _, kept, state, hstate, coef = main_call(
        nsec, offsets, dims.transpose(0, 2, 1), ranks, wavefunction[0].reshape((HALF, 2, SB, SB)), lenv, renv
    )
    head = jnp.where(lax.axis_index("sec") == 0, 1, 0).astype(jnp.int32).reshape((1,))
    next_left, state, hstate, energy = update(head, coef, lenv, prev, kept, state, hstate)
    return state[None], hstate[None], energy, next_left[None]


def solution(mesh):
    placed = (
        P("sec", "blk", None, None),
        P("sec", None, "blk", None, None),
        P("sec", None, "blk", None, None),
        P("sec", None),
        P("sec", "blk", None),
        P("sec", "blk"),
    )
    return jax.shard_map(
        shards,
        mesh=mesh,
        in_specs=placed,
        out_specs=(
            P("sec", "blk", None, None),
            P("sec", "blk", None, None),
            P("sec"),
            P("sec", None, "blk", None, None),
        ),
        check_vma=False,
    )
```

```python
import functools

import jax
import jax.numpy as jnp
from jax import lax
from jax.experimental import pallas as pl
from jax.experimental.pallas import tpu as pltpu
from jax.sharding import PartitionSpec as P

MESH = pl.DeviceIdType.MESH
VMEM_SPEC = pl.BlockSpec(memory_space=pltpu.VMEM)
SMEM_SPEC = pl.BlockSpec(memory_space=pltpu.SMEM)
ANY_SPEC = pl.BlockSpec(memory_space=pl.ANY)
F32 = jnp.float32
BF16 = jnp.bfloat16
NB = 16
NU = 12
NC = 20
SB = 128
HALF = NU // 2
ROWS = 16
NCH = SB // ROWS
PER = NC // 5
FAR = 5
CELLS = float(NB * NU * SB * SB)


def slot_tile(entries):
    row = lax.broadcasted_iota(jnp.int32, (16, SB), 0)
    tile = jnp.zeros((16, SB), F32)
    for u, entry in enumerate(entries):
        tile = jnp.where(row == u, entry, tile)
    return tile


def slot_mask(dim_a, dim_b):
    line_a = lax.broadcasted_iota(jnp.int32, (SB, SB), 0)
    line_b = lax.broadcasted_iota(jnp.int32, (SB, SB), 1)
    return (line_a < dim_a) & (line_b < dim_b)


def exists(off_ref, t, c):
    if c == 1:
        return t >= 1
    if c == 2:
        return t <= NU - 2
    down = (lax.axis_index("blk") + NB - off_ref[0, t]) & (NB - 1)
    return down >= 1 if c == 3 else down <= NB - 2


def source_device(off_ref, t, c):
    me = lax.axis_index("blk")
    if c == 1:
        return (me + NB - off_ref[0, t] + off_ref[0, jnp.maximum(t - 1, 0)]) & (NB - 1)
    if c == 2:
        return (me + NB - off_ref[0, t] + off_ref[0, jnp.minimum(t + 1, NU - 1)]) & (NB - 1)
    return (me + (NB - 1 if c == 3 else 1)) & (NB - 1)


def source_slot(t, c):
    if c == 1:
        return jnp.maximum(t - 1, 0)
    if c == 2:
        return jnp.minimum(t + 1, NU - 1)
    return t


def total(x):
    return jnp.sum(jnp.sum(x, axis=0, keepdims=True), axis=1, keepdims=True)


def products(l_ref, r_ref, acc_ref, work, fresh):
    inner = []
    for c, t, x in work:
        stack = jnp.concatenate([l_ref[c + 5 * k, t] for k in range(PER)], axis=0)
        product = jnp.dot(stack, x, preferred_element_type=F32).astype(BF16)
        inner.append(jnp.concatenate([product[k * SB : (k + 1) * SB] for k in range(PER)], axis=1))
    sums = {}
    slots = {}
    for left, (c, t, _) in zip(inner, work):
        right = jnp.concatenate([r_ref[c + 5 * k, t] for k in range(PER)], axis=1)
        term = lax.dot_general(left, right, (((1,), (1,)), ((), ())), preferred_element_type=F32)
        key = id(t)
        sums[key] = sums[key] + term if key in sums else term
        slots[key] = t
    for key, t in slots.items():
        acc_ref[t] = sums[key] if fresh else acc_ref[t] + sums[key]


def main_kernel(
    nsec, off_ref, dims_ref, rank_ref, x_ref, l_hbm, r_hbm,
    prev_ref, rel1, rel2, kept_ref, flag_ref, state_ref, hstate_ref, coef_ref,
    lv, rv, xs, va, v3, v4, gs, ga, g3, g4, recv_v, recv_g, send_v, send_g, h0, h1, v1, vs, kept, st, hst,
    ranks, ranks_all, sums, sums_all, qt, qt_all, part_n, part_p, part_r, alphas, alpha_all, flags,
    l_sem, r_sem, side_s, side_r, p1s, p1r, p2s, p2r, ts, tr, loc, zs, zr, ks, kr, fs, fr, fin
):
    me = lax.axis_index("blk")
    sec = lax.axis_index("sec")
    odd = sec % 2 == 1
    par = me // NCH
    lo = pl.multiple_of((me % NCH) * ROWS, ROWS)

    def section(by):
        return {"sec": (sec + by + nsec) % nsec}

    def peer(k):
        return {"blk": (me + k) % NB}

    def remote(src, dst, send, recv, where):
        return pltpu.make_async_remote_copy(
            src_ref=src, dst_ref=dst, send_sem=send, recv_sem=recv, device_id=where, device_id_type=MESH
        )

    barrier = pltpu.get_barrier_semaphore()
    for k in range(1, NB):
        pl.semaphore_signal(barrier, inc=1, device_id=peer(k), device_id_type=MESH)
    for by in (1, -1, 2, -2, 3, -3):
        pl.semaphore_signal(barrier, inc=1, device_id=section(by), device_id_type=MESH)

    def load(w, i):
        src, dst, sem = ((l_hbm, lv, l_sem), (r_hbm, rv, r_sem))[i]
        return pltpu.make_async_copy(src.at[w], dst.at[w], sem.at[w])

    for c in (0, 3, 4, 1, 2):
        for k in range(PER):
            load(c + 5 * k, 0).start()
            load(c + 5 * k, 1).start()

    def loaded(c):
        for k in range(PER):
            load(c + 5 * k, 0).wait()
            load(c + 5 * k, 1).wait()

    for u in range(NU):
        on = slot_mask(dims_ref[0, 0, u], dims_ref[0, 1, u])
        xs[u // 2, u % 2] = jnp.where(on, x_ref[u // 2, u % 2], jnp.zeros((SB, SB), BF16))
    ranks[...] = slot_tile([rank_ref[0, u].astype(F32) for u in range(NU)])
    down = [jnp.where(exists(off_ref, u, 3), 1.0, 0.0) for u in range(NU)]
    above_it = [jnp.where(exists(off_ref, u, 4), 1.0, 0.0) for u in range(NU)]
    line = lax.broadcasted_iota(jnp.int32, (16, SB), 1)
    flags[...] = jnp.where(line == 0, slot_tile(down), slot_tile(above_it))
    for ref in (part_n, part_p, part_r):
        ref[...] = jnp.zeros((16, SB), F32)
    pl.semaphore_wait(barrier, NB + 5)

    state_of = (xs, gs)
    recv_of = (recv_v, recv_g)
    send_of = (send_v, send_g)
    wide_of = (va, ga)
    side_of = ((v3, v4), (g3, g4))
    tile_of = (ranks, sums, qt)
    tiles_of = (ranks_all, sums_all, qt_all)

    def phase1(i, k):
        to = (me + k) % NB
        at = pl.multiple_of((to % NCH) * ROWS, ROWS)
        return remote(
            state_of[i].at[:, to // NCH, pl.ds(at, ROWS), :], recv_of[i].at[me], p1s.at[i, k], p1r.at[i, k], peer(k)
        )

    def mine(ref):
        return ref.at[:, pl.ds(par, HALF), 1 - par, pl.ds(lo, ROWS), :]

    def phase2(i, k):
        return remote(send_of[i].at[(me + k) % NB], mine(wide_of[i]), p2s.at[i, k], p2r.at[i, k], peer(k))

    def side(i, j):
        return remote(state_of[i], side_of[i][j], side_s.at[i, j], side_r.at[i, j], peer((1, NB - 1)[j]))

    def tiny(i, k):
        return remote(tile_of[i], tiles_of[i].at[me], ts.at[i, k], tr.at[i, k], peer(k))

    def own1(i):
        return pltpu.make_async_copy(state_of[i].at[:, par, pl.ds(lo, ROWS), :], recv_of[i].at[me], loc.at[i, 0])

    def own2(i):
        return pltpu.make_async_copy(send_of[i].at[me], mine(wide_of[i]), loc.at[i, 1])

    def direct(channels):
        part = pl.ds(0, channels)
        return remote(l_hbm.at[part], prev_ref.at[part], zs.at[0], zr.at[0], section(1))

    far = pl.ds(NC - FAR, FAR)
    flag_copy = remote(flags, flag_ref, ks.at[3], kr.at[3], section(1))

    def hop(i):
        if i == 0:
            return remote(l_hbm.at[far], rel1, zs.at[1], zr.at[1], section(-2))
        if i == 1:
            return remote(rel1, rel2, zs.at[2], zr.at[2], section(-2))
        return remote(rel2, prev_ref.at[far], zs.at[3], zr.at[3], section(-3))

    def begin(i):
        @pl.loop(1, NB)
        def _(k):
            phase1(i, k).start()

        own1(i).start()

    def middle(i):
        own1(i).wait()

        @pl.loop(1, NB)
        def _(k):
            phase1(i, k).wait_recv()

        @pl.loop(0, NB)
        def _(t):
            for r in range(HALF):
                up = 2 * r + par
                own = off_ref[0, up] + t + NB
                above = (own - off_ref[0, jnp.minimum(up + 1, NU - 1)]) & (NB - 1)
                below = (own - off_ref[0, jnp.maximum(up - 1, 0)]) & (NB - 1)
                send_of[i][t, 0, r] = recv_of[i][above, r]
                send_of[i][t, 1, r] = recv_of[i][below, r]

        @pl.loop(1, NB)
        def _(k):
            phase2(i, k).start()

        own2(i).start()

    def end(i):
        own2(i).wait()

        @pl.loop(1, NB)
        def _(k):
            phase2(i, k).wait_recv()

    begin(0)

    @pl.when(odd)
    def _():
        direct(NC - FAR).start()
        hop(0).start()

    @pl.when(jnp.logical_not(odd))
    def _():
        direct(NC).start()

    for j in range(2):
        side(0, j).start()

    @pl.loop(1, NB)
    def _(k):
        tiny(0, k).start()

    flag_copy.start()
    ranks_all[me] = ranks[...]
    middle(0)

    def own_v(t):
        return xs[t // 2, t % 2]

    def source(i, c, t):
        if c == 1:
            at = jnp.maximum(t, 1)
            return wide_of[i][0, at // 2, at % 2]
        if c == 2:
            at = jnp.minimum(t + 2, NU)
            return wide_of[i][1, at // 2, at % 2]
        return side_of[i][c - 3][t // 2, t % 2]

    def first_source(c, t):
        return jnp.where(exists(off_ref, t, c), source(0, c, t), jnp.zeros((SB, SB), BF16))

    loaded(0)

    @pl.loop(0, NU, step=2)
    def _(t0):
        pair = [t0, t0 + 1]
        products(lv, rv, h0, [(0, t, own_v(t)) for t in pair], True)
        for t in pair:
            v = own_v(t).astype(F32)
            part_n[pl.ds(t, 1), :] = jnp.sum(v * v, axis=0, keepdims=True)

    for j in range(2):
        side(0, j).wait_recv()
    loaded(3)
    loaded(4)

    @pl.loop(0, NU)
    def _(t):
        products(lv, rv, h0, [(c, t, first_source(c, t)) for c in (3, 4)], False)

    end(0)
    loaded(1)
    loaded(2)

    @pl.loop(0, NU, step=2)
    def _(t0):
        pair = [t0, t0 + 1]
        products(lv, rv, h0, [(c, t, first_source(c, t)) for t in pair for c in (1, 2)], False)
        for t in pair:
            h = jnp.where(slot_mask(dims_ref[0, 0, t], dims_ref[0, 1, t]), h0[t], 0.0)
            h0[t] = h
            part_p[pl.ds(t, 1), :] = jnp.sum(own_v(t).astype(F32) * h, axis=0, keepdims=True)

    @pl.when(odd)
    def _():
        hop(0).wait_recv()
        hop(1).start()

    n_own = jnp.sum(part_n[...], axis=1, keepdims=True)
    p_own = jnp.sum(part_p[...], axis=1, keepdims=True)
    alpha_own = jnp.where(n_own > 0.0, p_own / jnp.where(n_own > 0.0, n_own, 1.0), 0.0)
    alphas[...] = jnp.broadcast_to(alpha_own, (16, SB))

    @pl.loop(0, NU, step=2)
    def _(t0):
        for t in (t0, t0 + 1):
            g = h0[t] - alphas[pl.ds(t, 1), :] * own_v(t).astype(F32)
            gs[t // 2, t % 2] = g.astype(BF16)
            part_r[pl.ds(t, 1), :] = jnp.sum(g * g, axis=0, keepdims=True)

    r_own = jnp.sum(part_r[...], axis=1, keepdims=True)
    lanes = lax.broadcasted_iota(jnp.int32, (16, SB), 1)
    sums[...] = jnp.where(lanes == 0, n_own, jnp.where(lanes == 1, p_own, jnp.where(lanes == 2, r_own, alpha_own)))
    begin(1)

    @pl.loop(1, NB)
    def _(k):
        tiny(1, k).start()

    for j in range(2):
        side(1, j).start()
    sums_all[me] = sums[...]

    @pl.loop(1, NB)
    def _(k):
        tiny(1, k).wait_recv()

    every = sums_all[...]
    place = lax.broadcasted_iota(jnp.int32, (NB, 16, SB), 2)
    nt, pt, rt, at = [jnp.sum(jnp.where(place == i, every, 0.0), axis=2, keepdims=True) for i in range(4)]
    alpha_all[...] = jnp.broadcast_to(at, (NB, 16, SB))
    norm = total(jnp.sum(nt, axis=0))
    a0 = total(jnp.sum(pt, axis=0)) / norm
    gap = at - a0
    beta = jnp.sqrt(total(jnp.sum(rt + gap * gap * nt, axis=0)) / norm + 1e-6)
    scale = jnp.sqrt(CELLS / norm)
    kappa = scale / beta

    def second_source(c, t):
        alpha = alpha_all[source_device(off_ref, t, c), pl.ds(source_slot(t, c), 1), :]
        x = kappa * (source(1, c, t).astype(F32) + (alpha - a0) * source(0, c, t).astype(F32))
        x = jnp.where(exists(off_ref, t, c), x, 0.0).astype(BF16)
        if c < 3:
            vs[c - 1, t] = x
        return x

    middle(1)

    @pl.loop(0, NU, step=2)
    def _(t0):
        work = []
        for t in (t0, t0 + 1):
            x = (kappa * (h0[t] - a0 * own_v(t).astype(F32))).astype(BF16)
            v1[t] = x
            work.append((0, t, x))
        products(lv, rv, h1, work, True)

    for j in range(2):
        side(1, j).wait_recv()

    @pl.loop(0, NU)
    def _(t):
        products(lv, rv, h1, [(c, t, second_source(c, t)) for c in (3, 4)], False)

    end(1)

    @pl.when(odd)
    def _():
        hop(1).wait_recv()
        hop(2).start()

    qt[...] = jnp.zeros((8, SB), F32)

    @pl.loop(0, NU, step=2)
    def _(t0):
        pair = [t0, t0 + 1]
        products(lv, rv, h1, [(c, t, second_source(c, t)) for t in pair for c in (1, 2)], False)
        for t in pair:
            h = jnp.where(slot_mask(dims_ref[0, 0, t], dims_ref[0, 1, t]), h1[t], 0.0)
            h1[t] = h
            qt[0:1, :] += jnp.sum(v1[t].astype(F32) * h, axis=0, keepdims=True)

    @pl.loop(1, NB)
    def _(k):
        tiny(2, k).start()

    qt_all[me] = qt[...]

    @pl.loop(1, NB)
    def _(k):
        tiny(0, k).wait_recv()
        tiny(2, k).wait_recv()

    a1 = total(jnp.sum(qt_all[...], axis=0)) / CELLS
    half = (a0 - a1) / 2.0
    ritz = (a0 + a1) / 2.0 - jnp.sqrt(half * half + beta * beta)
    slip = ritz - a0
    length = jnp.sqrt(beta * beta + slip * slip)
    xcoef, ycoef = beta / length, slip / length
    coef_ref[...] = jnp.broadcast_to(ritz, (8, SB))
    lane = lax.broadcasted_iota(jnp.int32, (1, SB), 1).astype(F32)
    v_coef = xcoef * scale

    def onward(c):
        return remote(kept.at[c], kept_ref.at[c], ks.at[c], kr.at[c], section(1))

    def forward(j):
        return remote(kept_ref.at[0], kept_ref.at[3 + j], fs.at[j], fr.at[j], peer((1, NB - 1)[j]))

    for c in range(3):

        @pl.loop(0, NU, step=2)
        def _(t0):
            for t in (t0, t0 + 1):
                if c == 0:
                    x = (v_coef * own_v(t).astype(F32) + ycoef * v1[t].astype(F32)).astype(BF16)
                    st[t] = x
                    on = lane < ranks[pl.ds(t, 1), :]
                else:
                    x = v_coef * source(0, c, t).astype(F32) + ycoef * vs[c - 1, t].astype(F32)
                    rank = ranks_all[source_device(off_ref, t, c), pl.ds(source_slot(t, c), 1), :]
                    on = (lane < rank) & exists(off_ref, t, c)
                kept[c, t] = jnp.where(on, x.astype(F32), 0.0).astype(BF16)

        if c:
            onward(c - 1).start()

    onward(2).start()

    @pl.loop(0, NU)
    def _(t):
        hst[t] = (v_coef * h0[t] + ycoef * h1[t]).astype(BF16)

    outs = [
        pltpu.make_async_copy(st, state_ref, fin.at[0]),
        pltpu.make_async_copy(hst, hstate_ref, fin.at[1]),
    ]
    for copy in outs:
        copy.start()
    onward(0).wait_recv()
    for j in range(2):
        forward(j).start()

    for i in range(2):
        for j in range(2):
            side(i, j).wait_send()

    @pl.loop(1, NB)
    def _(k):
        for i in range(2):
            phase1(i, k).wait_send()
            phase2(i, k).wait_send()
        for i in range(3):
            tiny(i, k).wait_send()

    for copy in outs:
        copy.wait()

    @pl.when(odd)
    def _():
        direct(NC - FAR).wait_send()
        for i in range(3):
            hop(i).wait_send()
        direct(NC).wait_recv()

    @pl.when(jnp.logical_not(odd))
    def _():
        direct(NC).wait_send()
        direct(NC - FAR).wait_recv()
        hop(2).wait_recv()

    onward(0).wait_send()
    for c in (1, 2):
        onward(c).wait()
    flag_copy.wait()
    for j in range(2):
        forward(j).wait()


def main_call(nsec, offsets, dims, ranks, x, lenv, renv):
    pair = (HALF, 2, SB, SB)
    flat = (NU, SB, SB)
    tile, slots = (8, SB), (16, SB)
    far = jax.ShapeDtypeStruct((FAR, NU, SB, SB), BF16)
    wide = pltpu.VMEM((2, HALF + 1, 2, SB, SB), BF16)
    bf = lambda *shape: pltpu.VMEM(shape, BF16)
    f32 = lambda *shape: pltpu.VMEM(shape, F32)
    dma = lambda *shape: pltpu.SemaphoreType.DMA(shape)
    return pl.pallas_call(
        functools.partial(main_kernel, nsec),
        out_shape=[
            jax.ShapeDtypeStruct((NC,) + flat, BF16),
            far,
            far,
            jax.ShapeDtypeStruct((5,) + flat, BF16),
            jax.ShapeDtypeStruct(slots, F32),
            jax.ShapeDtypeStruct(flat, BF16),
            jax.ShapeDtypeStruct(flat, BF16),
            jax.ShapeDtypeStruct(tile, F32),
        ],
        in_specs=[SMEM_SPEC, SMEM_SPEC, SMEM_SPEC, VMEM_SPEC, ANY_SPEC, ANY_SPEC],
        out_specs=[ANY_SPEC] * 7 + [VMEM_SPEC],
        scratch_shapes=[
            bf(NC, *flat), bf(NC, *flat), bf(*pair), wide, bf(*pair), bf(*pair), bf(*pair), wide, bf(*pair), bf(*pair),
            bf(NB, HALF, ROWS, SB), bf(NB, HALF, ROWS, SB),
            bf(NB, 2, HALF, ROWS, SB), bf(NB, 2, HALF, ROWS, SB),
            f32(*flat), f32(*flat), bf(*flat), bf(2, *flat), bf(3, *flat), bf(*flat), bf(*flat),
            f32(*slots), f32(NB, *slots), f32(*slots), f32(NB, *slots), f32(*tile), f32(NB, *tile),
            f32(*slots), f32(*slots), f32(*slots), f32(*slots), f32(NB, *slots), f32(*slots),
            dma(NC), dma(NC), dma(2, 2), dma(2, 2), dma(2, NB), dma(2, NB), dma(2, NB), dma(2, NB),
            dma(3, NB), dma(3, NB), dma(2, 2), dma(4), dma(4), dma(4), dma(4), dma(2), dma(2), dma(2),
        ],
        compiler_params=pltpu.CompilerParams(collective_id=0, has_side_effects=True),
        name="davidson",
    )(offsets, dims, ranks, x, lenv, renv)


def update_kernel(slots, head_ref, flag_ref, coef_ref, own_ref, l_ref, k_ref, si_ref, hi_ref, next_ref, s_ref, hs_ref, e_ref):
    first_section = head_ref[0] == 1
    s_ref[...] = si_ref[...]
    hs_ref[...] = hi_ref[...]
    e_ref[0] = coef_ref[0, 0]

    @pl.when(first_section)
    def _():
        next_ref[...] = own_ref[...]

    @pl.when(jnp.logical_not(first_section))
    def _():
        for i in range(slots):
            kept = k_ref[0, i]
            for c in range(5):
                stack = jnp.concatenate([l_ref[c + 5 * k, i] for k in range(PER)], axis=0)
                x = k_ref[c, i]
                if c > 2:
                    x = jnp.where(flag_ref[pl.program_id(0) * slots + i, c - 3] > 0.5, x, jnp.zeros_like(x))
                inner = jnp.dot(stack, x, preferred_element_type=F32).astype(BF16)
                wide = jnp.concatenate([inner[k * SB : (k + 1) * SB] for k in range(PER)], axis=1)
                out = lax.dot_general(kept, wide, (((0,), (0,)), ((), ())), preferred_element_type=F32).astype(BF16)
                for k in range(PER):
                    next_ref[c + 5 * k, i] = out[:, k * SB : (k + 1) * SB]


SLOTS = 2


def update(head, flags, coef, lenv, prev, kept, state, hstate):
    tile = pl.BlockSpec((8, SB), lambda t, *_: (0, 0))
    one = pl.BlockSpec((SLOTS, SB, SB), lambda t, *_: (t, 0, 0))
    env = (NC, SLOTS, SB, SB)
    own = pl.BlockSpec(env, lambda t, head: (0, t * head[0], 0, 0))
    far = pl.BlockSpec(env, lambda t, head: (0, t * (1 - head[0]), 0, 0))
    flat = jax.ShapeDtypeStruct((NU, SB, SB), BF16)
    return pl.pallas_call(
        functools.partial(update_kernel, SLOTS),
        grid_spec=pltpu.PrefetchScalarGridSpec(
            num_scalar_prefetch=1,
            grid=(NU // SLOTS,),
            in_specs=[SMEM_SPEC, tile, own, far, pl.BlockSpec((5, SLOTS, SB, SB), lambda t, *_: (0, t, 0, 0)), one, one],
            out_specs=[pl.BlockSpec(env, lambda t, *_: (0, t, 0, 0)), one, one, SMEM_SPEC],
        ),
        out_shape=[
            jax.ShapeDtypeStruct((NC, NU, SB, SB), BF16),
            flat,
            flat,
            jax.ShapeDtypeStruct((1,), F32),
        ],
        name="update",
    )(head, flags, coef, lenv, prev, kept, state, hstate)


def shards(wavefunction, left_env, right_env, offsets, dims, ranks):
    nsec = lax.axis_size("sec")
    lenv, renv = left_env[0], right_env[0]
    prev, _, _, kept, flags, state, hstate, coef = main_call(
        nsec, offsets, dims.transpose(0, 2, 1), ranks, wavefunction[0].reshape((HALF, 2, SB, SB)), lenv, renv
    )
    head = jnp.where(lax.axis_index("sec") == 0, 1, 0).astype(jnp.int32).reshape((1,))
    next_left, state, hstate, energy = update(head, flags, coef, lenv, prev, kept, state, hstate)
    return state[None], hstate[None], energy, next_left[None]


def solution(mesh):
    placed = (
        P("sec", "blk", None, None),
        P("sec", None, "blk", None, None),
        P("sec", None, "blk", None, None),
        P("sec", None),
        P("sec", "blk", None),
        P("sec", "blk"),
    )
    return jax.shard_map(
        shards,
        mesh=mesh,
        in_specs=placed,
        out_specs=(
            P("sec", "blk", None, None),
            P("sec", "blk", None, None),
            P("sec"),
            P("sec", None, "blk", None, None),
        ),
        check_vma=False,
    )
```

```python
import functools

import jax
import jax.numpy as jnp
from jax import lax
from jax.experimental import pallas as pl
from jax.experimental.pallas import tpu as pltpu
from jax.sharding import PartitionSpec as P

MESH = pl.DeviceIdType.MESH
VMEM_SPEC = pl.BlockSpec(memory_space=pltpu.VMEM)
SMEM_SPEC = pl.BlockSpec(memory_space=pltpu.SMEM)
ANY_SPEC = pl.BlockSpec(memory_space=pl.ANY)
F32 = jnp.float32
BF16 = jnp.bfloat16
NB = 16
NU = 12
NC = 20
SB = 128
HALF = NU // 2
ROWS = 16
NCH = SB // ROWS
PER = NC // 5
FAR = 6
CELLS = float(NB * NU * SB * SB)


def slot_tile(entries):
    row = lax.broadcasted_iota(jnp.int32, (16, SB), 0)
    tile = jnp.zeros((16, SB), F32)
    for u, entry in enumerate(entries):
        tile = jnp.where(row == u, entry, tile)
    return tile


def slot_mask(dim_a, dim_b):
    line_a = lax.broadcasted_iota(jnp.int32, (SB, SB), 0)
    line_b = lax.broadcasted_iota(jnp.int32, (SB, SB), 1)
    return (line_a < dim_a) & (line_b < dim_b)


def exists(off_ref, t, c):
    if c == 1:
        return t >= 1
    if c == 2:
        return t <= NU - 2
    down = (lax.axis_index("blk") + NB - off_ref[0, t]) & (NB - 1)
    return down >= 1 if c == 3 else down <= NB - 2


def source_device(off_ref, t, c):
    me = lax.axis_index("blk")
    if c == 1:
        return (me + NB - off_ref[0, t] + off_ref[0, jnp.maximum(t - 1, 0)]) & (NB - 1)
    if c == 2:
        return (me + NB - off_ref[0, t] + off_ref[0, jnp.minimum(t + 1, NU - 1)]) & (NB - 1)
    return (me + (NB - 1 if c == 3 else 1)) & (NB - 1)


def source_slot(t, c):
    if c == 1:
        return jnp.maximum(t - 1, 0)
    if c == 2:
        return jnp.minimum(t + 1, NU - 1)
    return t


def total(x):
    return jnp.sum(jnp.sum(x, axis=0, keepdims=True), axis=1, keepdims=True)


def products(l_ref, r_ref, acc_ref, work, fresh):
    inner = []
    for c, t, x in work:
        stack = jnp.concatenate([l_ref[c + 5 * k, t] for k in range(PER)], axis=0)
        product = jnp.dot(stack, x, preferred_element_type=F32).astype(BF16)
        inner.append(jnp.concatenate([product[k * SB : (k + 1) * SB] for k in range(PER)], axis=1))
    sums = {}
    slots = {}
    for left, (c, t, _) in zip(inner, work):
        right = jnp.concatenate([r_ref[c + 5 * k, t] for k in range(PER)], axis=1)
        term = lax.dot_general(left, right, (((1,), (1,)), ((), ())), preferred_element_type=F32)
        key = id(t)
        sums[key] = sums[key] + term if key in sums else term
        slots[key] = t
    for key, t in slots.items():
        acc_ref[t] = sums[key] if fresh else acc_ref[t] + sums[key]


def main_kernel(
    nsec, off_ref, dims_ref, rank_ref, x_ref, l_hbm, r_hbm,
    prev_ref, rel1, rel2, kept_ref, flag_ref, state_ref, hstate_ref, coef_ref,
    lv, rv, xs, va, v3, v4, gs, ga, g3, g4, recv_v, recv_g, send_v, send_g, h0, h1, v1, vs, kept, st, hst,
    ranks, ranks_all, sums, sums_all, qt, qt_all, part_n, part_p, part_r, alphas, alpha_all, flags,
    l_sem, r_sem, side_s, side_r, p1s, p1r, p2s, p2r, ts, tr, loc, zs, zr, ks, kr, fs, fr, fin
):
    me = lax.axis_index("blk")
    sec = lax.axis_index("sec")
    odd = sec % 2 == 1
    par = me // NCH
    lo = pl.multiple_of((me % NCH) * ROWS, ROWS)

    def section(by):
        return {"sec": (sec + by + nsec) % nsec}

    def peer(k):
        return {"blk": (me + k) % NB}

    def remote(src, dst, send, recv, where):
        return pltpu.make_async_remote_copy(
            src_ref=src, dst_ref=dst, send_sem=send, recv_sem=recv, device_id=where, device_id_type=MESH
        )

    barrier = pltpu.get_barrier_semaphore()
    for k in range(1, NB):
        pl.semaphore_signal(barrier, inc=1, device_id=peer(k), device_id_type=MESH)
    for by in (1, -1, 2, -2, 3, -3):
        pl.semaphore_signal(barrier, inc=1, device_id=section(by), device_id_type=MESH)

    def load(w, i):
        src, dst, sem = ((l_hbm, lv, l_sem), (r_hbm, rv, r_sem))[i]
        return pltpu.make_async_copy(src.at[w], dst.at[w], sem.at[w])

    for c in (0, 3, 4, 1, 2):
        for k in range(PER):
            load(c + 5 * k, 0).start()
            load(c + 5 * k, 1).start()

    def loaded(c):
        for k in range(PER):
            load(c + 5 * k, 0).wait()
            load(c + 5 * k, 1).wait()

    for u in range(NU):
        on = slot_mask(dims_ref[0, 0, u], dims_ref[0, 1, u])
        xs[u // 2, u % 2] = jnp.where(on, x_ref[u // 2, u % 2], jnp.zeros((SB, SB), BF16))
    ranks[...] = slot_tile([rank_ref[0, u].astype(F32) for u in range(NU)])
    down = [jnp.where(exists(off_ref, u, 3), 1.0, 0.0) for u in range(NU)]
    above_it = [jnp.where(exists(off_ref, u, 4), 1.0, 0.0) for u in range(NU)]
    line = lax.broadcasted_iota(jnp.int32, (16, SB), 1)
    flags[...] = jnp.where(line == 0, slot_tile(down), slot_tile(above_it))
    for ref in (part_n, part_p, part_r):
        ref[...] = jnp.zeros((16, SB), F32)
    pl.semaphore_wait(barrier, NB + 5)

    state_of = (xs, gs)
    recv_of = (recv_v, recv_g)
    send_of = (send_v, send_g)
    wide_of = (va, ga)
    side_of = ((v3, v4), (g3, g4))
    tile_of = (ranks, sums, qt)
    tiles_of = (ranks_all, sums_all, qt_all)

    def phase1(i, k):
        to = (me + k) % NB
        at = pl.multiple_of((to % NCH) * ROWS, ROWS)
        return remote(
            state_of[i].at[:, to // NCH, pl.ds(at, ROWS), :], recv_of[i].at[me], p1s.at[i, k], p1r.at[i, k], peer(k)
        )

    def mine(ref):
        return ref.at[:, pl.ds(par, HALF), 1 - par, pl.ds(lo, ROWS), :]

    def phase2(i, k):
        return remote(send_of[i].at[(me + k) % NB], mine(wide_of[i]), p2s.at[i, k], p2r.at[i, k], peer(k))

    def side(i, j):
        return remote(state_of[i], side_of[i][j], side_s.at[i, j], side_r.at[i, j], peer((1, NB - 1)[j]))

    def tiny(i, k):
        return remote(tile_of[i], tiles_of[i].at[me], ts.at[i, k], tr.at[i, k], peer(k))

    def own1(i):
        return pltpu.make_async_copy(state_of[i].at[:, par, pl.ds(lo, ROWS), :], recv_of[i].at[me], loc.at[i, 0])

    def own2(i):
        return pltpu.make_async_copy(send_of[i].at[me], mine(wide_of[i]), loc.at[i, 1])

    def direct(channels):
        part = pl.ds(0, channels)
        return remote(l_hbm.at[part], prev_ref.at[part], zs.at[0], zr.at[0], section(1))

    far = pl.ds(NC - FAR, FAR)
    flag_copy = remote(flags, flag_ref, ks.at[3], kr.at[3], section(1))

    def hop(i):
        if i == 0:
            return remote(l_hbm.at[far], rel1, zs.at[1], zr.at[1], section(-2))
        if i == 1:
            return remote(rel1, rel2, zs.at[2], zr.at[2], section(-2))
        return remote(rel2, prev_ref.at[far], zs.at[3], zr.at[3], section(-3))

    def begin(i):
        @pl.loop(1, NB)
        def _(k):
            phase1(i, k).start()

        own1(i).start()

    def middle(i):
        own1(i).wait()

        @pl.loop(1, NB)
        def _(k):
            phase1(i, k).wait_recv()

        @pl.loop(0, NB)
        def _(t):
            for r in range(HALF):
                up = 2 * r + par
                own = off_ref[0, up] + t + NB
                above = (own - off_ref[0, jnp.minimum(up + 1, NU - 1)]) & (NB - 1)
                below = (own - off_ref[0, jnp.maximum(up - 1, 0)]) & (NB - 1)
                send_of[i][t, 0, r] = recv_of[i][above, r]
                send_of[i][t, 1, r] = recv_of[i][below, r]

        @pl.loop(1, NB)
        def _(k):
            phase2(i, k).start()

        own2(i).start()

    def end(i):
        own2(i).wait()

        @pl.loop(1, NB)
        def _(k):
            phase2(i, k).wait_recv()

    begin(0)

    @pl.when(odd)
    def _():
        direct(NC - FAR).start()
        hop(0).start()

    @pl.when(jnp.logical_not(odd))
    def _():
        direct(NC).start()

    for j in range(2):
        side(0, j).start()

    @pl.loop(1, NB)
    def _(k):
        tiny(0, k).start()

    flag_copy.start()
    ranks_all[me] = ranks[...]
    middle(0)

    def own_v(t):
        return xs[t // 2, t % 2]

    def source(i, c, t):
        if c == 1:
            at = jnp.maximum(t, 1)
            return wide_of[i][0, at // 2, at % 2]
        if c == 2:
            at = jnp.minimum(t + 2, NU)
            return wide_of[i][1, at // 2, at % 2]
        return side_of[i][c - 3][t // 2, t % 2]

    def first_source(c, t):
        return jnp.where(exists(off_ref, t, c), source(0, c, t), jnp.zeros((SB, SB), BF16))

    loaded(0)

    @pl.loop(0, NU, step=2)
    def _(t0):
        pair = [t0, t0 + 1]
        products(lv, rv, h0, [(0, t, own_v(t)) for t in pair], True)
        for t in pair:
            v = own_v(t).astype(F32)
            part_n[pl.ds(t, 1), :] = jnp.sum(v * v, axis=0, keepdims=True)

    for j in range(2):
        side(0, j).wait_recv()
    loaded(3)
    loaded(4)

    @pl.loop(0, NU)
    def _(t):
        products(lv, rv, h0, [(c, t, first_source(c, t)) for c in (3, 4)], False)

    end(0)
    loaded(1)
    loaded(2)

    @pl.loop(0, NU, step=2)
    def _(t0):
        pair = [t0, t0 + 1]
        products(lv, rv, h0, [(c, t, first_source(c, t)) for t in pair for c in (1, 2)], False)
        for t in pair:
            h = jnp.where(slot_mask(dims_ref[0, 0, t], dims_ref[0, 1, t]), h0[t], 0.0)
            h0[t] = h
            part_p[pl.ds(t, 1), :] = jnp.sum(own_v(t).astype(F32) * h, axis=0, keepdims=True)

    @pl.when(odd)
    def _():
        hop(0).wait_recv()
        hop(1).start()

    n_own = jnp.sum(part_n[...], axis=1, keepdims=True)
    p_own = jnp.sum(part_p[...], axis=1, keepdims=True)
    alpha_own = jnp.where(n_own > 0.0, p_own / jnp.where(n_own > 0.0, n_own, 1.0), 0.0)
    alphas[...] = jnp.broadcast_to(alpha_own, (16, SB))

    @pl.loop(0, NU, step=2)
    def _(t0):
        for t in (t0, t0 + 1):
            g = h0[t] - alphas[pl.ds(t, 1), :] * own_v(t).astype(F32)
            gs[t // 2, t % 2] = g.astype(BF16)
            part_r[pl.ds(t, 1), :] = jnp.sum(g * g, axis=0, keepdims=True)

    r_own = jnp.sum(part_r[...], axis=1, keepdims=True)
    lanes = lax.broadcasted_iota(jnp.int32, (16, SB), 1)
    sums[...] = jnp.where(lanes == 0, n_own, jnp.where(lanes == 1, p_own, jnp.where(lanes == 2, r_own, alpha_own)))
    begin(1)

    @pl.loop(1, NB)
    def _(k):
        tiny(1, k).start()

    for j in range(2):
        side(1, j).start()
    sums_all[me] = sums[...]

    @pl.loop(1, NB)
    def _(k):
        tiny(1, k).wait_recv()

    every = sums_all[...]
    place = lax.broadcasted_iota(jnp.int32, (NB, 16, SB), 2)
    nt, pt, rt, at = [jnp.sum(jnp.where(place == i, every, 0.0), axis=2, keepdims=True) for i in range(4)]
    alpha_all[...] = jnp.broadcast_to(at, (NB, 16, SB))
    norm = total(jnp.sum(nt, axis=0))
    a0 = total(jnp.sum(pt, axis=0)) / norm
    gap = at - a0
    beta = jnp.sqrt(total(jnp.sum(rt + gap * gap * nt, axis=0)) / norm + 1e-6)
    scale = jnp.sqrt(CELLS / norm)
    kappa = scale / beta

    def second_source(c, t):
        alpha = alpha_all[source_device(off_ref, t, c), pl.ds(source_slot(t, c), 1), :]
        x = kappa * (source(1, c, t).astype(F32) + (alpha - a0) * source(0, c, t).astype(F32))
        x = jnp.where(exists(off_ref, t, c), x, 0.0).astype(BF16)
        if c < 3:
            vs[c - 1, t] = x
        return x

    middle(1)

    @pl.loop(0, NU, step=2)
    def _(t0):
        work = []
        for t in (t0, t0 + 1):
            x = (kappa * (h0[t] - a0 * own_v(t).astype(F32))).astype(BF16)
            v1[t] = x
            work.append((0, t, x))
        products(lv, rv, h1, work, True)

    for j in range(2):
        side(1, j).wait_recv()

    @pl.loop(0, NU)
    def _(t):
        products(lv, rv, h1, [(c, t, second_source(c, t)) for c in (3, 4)], False)

    end(1)

    @pl.when(odd)
    def _():
        hop(1).wait_recv()
        hop(2).start()

    qt[...] = jnp.zeros((8, SB), F32)

    @pl.loop(0, NU, step=2)
    def _(t0):
        pair = [t0, t0 + 1]
        products(lv, rv, h1, [(c, t, second_source(c, t)) for t in pair for c in (1, 2)], False)
        for t in pair:
            h = jnp.where(slot_mask(dims_ref[0, 0, t], dims_ref[0, 1, t]), h1[t], 0.0)
            h1[t] = h
            qt[0:1, :] += jnp.sum(v1[t].astype(F32) * h, axis=0, keepdims=True)

    @pl.loop(1, NB)
    def _(k):
        tiny(2, k).start()

    qt_all[me] = qt[...]

    @pl.loop(1, NB)
    def _(k):
        tiny(0, k).wait_recv()
        tiny(2, k).wait_recv()

    a1 = total(jnp.sum(qt_all[...], axis=0)) / CELLS
    half = (a0 - a1) / 2.0
    ritz = (a0 + a1) / 2.0 - jnp.sqrt(half * half + beta * beta)
    slip = ritz - a0
    length = jnp.sqrt(beta * beta + slip * slip)
    xcoef, ycoef = beta / length, slip / length
    coef_ref[...] = jnp.broadcast_to(ritz, (8, SB))
    lane = lax.broadcasted_iota(jnp.int32, (1, SB), 1).astype(F32)
    v_coef = xcoef * scale

    def onward(c):
        return remote(kept.at[c], kept_ref.at[c], ks.at[c], kr.at[c], section(1))

    def forward(j):
        return remote(kept_ref.at[0], kept_ref.at[3 + j], fs.at[j], fr.at[j], peer((1, NB - 1)[j]))

    for c in range(3):

        @pl.loop(0, NU, step=2)
        def _(t0):
            for t in (t0, t0 + 1):
                if c == 0:
                    x = (v_coef * own_v(t).astype(F32) + ycoef * v1[t].astype(F32)).astype(BF16)
                    st[t] = x
                    on = lane < ranks[pl.ds(t, 1), :]
                else:
                    x = v_coef * source(0, c, t).astype(F32) + ycoef * vs[c - 1, t].astype(F32)
                    rank = ranks_all[source_device(off_ref, t, c), pl.ds(source_slot(t, c), 1), :]
                    on = (lane < rank) & exists(off_ref, t, c)
                kept[c, t] = jnp.where(on, x.astype(F32), 0.0).astype(BF16)

        if c:
            onward(c - 1).start()

    onward(2).start()

    @pl.loop(0, NU)
    def _(t):
        hst[t] = (v_coef * h0[t] + ycoef * h1[t]).astype(BF16)

    outs = [
        pltpu.make_async_copy(st, state_ref, fin.at[0]),
        pltpu.make_async_copy(hst, hstate_ref, fin.at[1]),
    ]
    for copy in outs:
        copy.start()
    onward(0).wait_recv()
    for j in range(2):
        forward(j).start()

    for i in range(2):
        for j in range(2):
            side(i, j).wait_send()

    @pl.loop(1, NB)
    def _(k):
        for i in range(2):
            phase1(i, k).wait_send()
            phase2(i, k).wait_send()
        for i in range(3):
            tiny(i, k).wait_send()

    for copy in outs:
        copy.wait()

    @pl.when(odd)
    def _():
        direct(NC - FAR).wait_send()
        for i in range(3):
            hop(i).wait_send()
        direct(NC).wait_recv()

    @pl.when(jnp.logical_not(odd))
    def _():
        direct(NC).wait_send()
        direct(NC - FAR).wait_recv()
        hop(2).wait_recv()

    onward(0).wait_send()
    for c in (1, 2):
        onward(c).wait()
    flag_copy.wait()
    for j in range(2):
        forward(j).wait()


def main_call(nsec, offsets, dims, ranks, x, lenv, renv):
    pair = (HALF, 2, SB, SB)
    flat = (NU, SB, SB)
    tile, slots = (8, SB), (16, SB)
    far = jax.ShapeDtypeStruct((FAR, NU, SB, SB), BF16)
    wide = pltpu.VMEM((2, HALF + 1, 2, SB, SB), BF16)
    bf = lambda *shape: pltpu.VMEM(shape, BF16)
    f32 = lambda *shape: pltpu.VMEM(shape, F32)
    dma = lambda *shape: pltpu.SemaphoreType.DMA(shape)
    return pl.pallas_call(
        functools.partial(main_kernel, nsec),
        out_shape=[
            jax.ShapeDtypeStruct((NC,) + flat, BF16),
            far,
            far,
            jax.ShapeDtypeStruct((5,) + flat, BF16),
            jax.ShapeDtypeStruct(slots, F32),
            jax.ShapeDtypeStruct(flat, BF16),
            jax.ShapeDtypeStruct(flat, BF16),
            jax.ShapeDtypeStruct(tile, F32),
        ],
        in_specs=[SMEM_SPEC, SMEM_SPEC, SMEM_SPEC, VMEM_SPEC, ANY_SPEC, ANY_SPEC],
        out_specs=[ANY_SPEC] * 7 + [VMEM_SPEC],
        scratch_shapes=[
            bf(NC, *flat), bf(NC, *flat), bf(*pair), wide, bf(*pair), bf(*pair), bf(*pair), wide, bf(*pair), bf(*pair),
            bf(NB, HALF, ROWS, SB), bf(NB, HALF, ROWS, SB),
            bf(NB, 2, HALF, ROWS, SB), bf(NB, 2, HALF, ROWS, SB),
            f32(*flat), f32(*flat), bf(*flat), bf(2, *flat), bf(3, *flat), bf(*flat), bf(*flat),
            f32(*slots), f32(NB, *slots), f32(*slots), f32(NB, *slots), f32(*tile), f32(NB, *tile),
            f32(*slots), f32(*slots), f32(*slots), f32(*slots), f32(NB, *slots), f32(*slots),
            dma(NC), dma(NC), dma(2, 2), dma(2, 2), dma(2, NB), dma(2, NB), dma(2, NB), dma(2, NB),
            dma(3, NB), dma(3, NB), dma(2, 2), dma(4), dma(4), dma(4), dma(4), dma(2), dma(2), dma(2),
        ],
        compiler_params=pltpu.CompilerParams(collective_id=0, has_side_effects=True),
        name="davidson",
    )(offsets, dims, ranks, x, lenv, renv)


def update_kernel(
    flag_ref, coef_ref, l_hbm, prev_hbm, kept_hbm, state_hbm, hstate_hbm, next_hbm, s_hbm, hs_hbm, e_ref,
    lp, kp, out, st, hst, l_sem, k_sem, o_sem, s_sem
):
    first_section = lax.axis_index("sec") == 0

    def fetch(src, t):
        return pltpu.make_async_copy(src.at[:, t], lp.at[:, t], l_sem.at[t])

    def fetch_kept(t):
        return pltpu.make_async_copy(kept_hbm.at[:, t], kp.at[:, t], k_sem.at[t])

    def write(src, t):
        return pltpu.make_async_copy(src.at[:, t], next_hbm.at[:, t], o_sem.at[t])

    states = [(state_hbm, st, s_hbm), (hstate_hbm, hst, hs_hbm)]
    takes = [pltpu.make_async_copy(src, at, s_sem.at[i]) for i, (src, at, _) in enumerate(states)]
    gives = [pltpu.make_async_copy(at, dst, s_sem.at[2 + i]) for i, (_, at, dst) in enumerate(states)]

    @pl.when(first_section)
    def _():
        @pl.loop(0, NU)
        def _(t):
            fetch(l_hbm, t).start()

    @pl.when(jnp.logical_not(first_section))
    def _():
        @pl.loop(0, NU)
        def _(t):
            fetch_kept(t).start()
            fetch(prev_hbm, t).start()

    for copy in takes:
        copy.start()
    e_ref[0] = coef_ref[0, 0]

    @pl.when(first_section)
    def _():
        @pl.loop(0, NU)
        def _(t):
            fetch(l_hbm, t).wait()
            write(lp, t).start()

        for take, give in zip(takes, gives):
            take.wait()
            give.start()

        @pl.loop(0, NU)
        def _(t):
            write(lp, t).wait()

    @pl.when(jnp.logical_not(first_section))
    def _():
        def one(t):
            kept = kp[0, t]
            for c in range(5):
                stack = jnp.concatenate([lp[c + 5 * k, t] for k in range(PER)], axis=0)
                x = kp[c, t]
                if c > 2:
                    x = jnp.where(flag_ref[t, c - 3] > 0.5, x, jnp.zeros_like(x))
                inner = jnp.dot(stack, x, preferred_element_type=F32).astype(BF16)
                wide = jnp.concatenate([inner[k * SB : (k + 1) * SB] for k in range(PER)], axis=1)
                new = lax.dot_general(kept, wide, (((0,), (0,)), ((), ())), preferred_element_type=F32).astype(BF16)
                for k in range(PER):
                    out[c + 5 * k, t] = new[:, k * SB : (k + 1) * SB]

        @pl.loop(0, NU)
        def _(t):
            fetch_kept(t).wait()
            fetch(prev_hbm, t).wait()
            one(t)

            @pl.when(t > 0)
            def _():
                write(out, t - 1).start()

        for take, give in zip(takes, gives):
            take.wait()
            give.start()
        write(out, NU - 1).start()

        @pl.loop(0, NU)
        def _(t):
            write(out, t).wait()

    for give in gives:
        give.wait()


def update(flags, coef, lenv, prev, kept, state, hstate):
    flat = (NU, SB, SB)
    return pl.pallas_call(
        update_kernel,
        in_specs=[SMEM_SPEC, SMEM_SPEC] + [ANY_SPEC] * 5,
        out_specs=[ANY_SPEC] * 3 + [SMEM_SPEC],
        out_shape=[
            jax.ShapeDtypeStruct((NC,) + flat, BF16),
            jax.ShapeDtypeStruct(flat, BF16),
            jax.ShapeDtypeStruct(flat, BF16),
            jax.ShapeDtypeStruct((1,), F32),
        ],
        scratch_shapes=[
            pltpu.VMEM((NC,) + flat, BF16),
            pltpu.VMEM((5,) + flat, BF16),
            pltpu.VMEM((NC,) + flat, BF16),
            pltpu.VMEM(flat, BF16),
            pltpu.VMEM(flat, BF16),
            pltpu.SemaphoreType.DMA((NU,)),
            pltpu.SemaphoreType.DMA((NU,)),
            pltpu.SemaphoreType.DMA((NU,)),
            pltpu.SemaphoreType.DMA((4,)),
        ],
        name="update",
    )(flags, coef, lenv, prev, kept, state, hstate)


def shards(wavefunction, left_env, right_env, offsets, dims, ranks):
    nsec = lax.axis_size("sec")
    lenv, renv = left_env[0], right_env[0]
    prev, _, _, kept, flags, state, hstate, coef = main_call(
        nsec, offsets, dims.transpose(0, 2, 1), ranks, wavefunction[0].reshape((HALF, 2, SB, SB)), lenv, renv
    )
    next_left, state, hstate, energy = update(flags, coef, lenv, prev, kept, state, hstate)
    return state[None], hstate[None], energy, next_left[None]


def solution(mesh):
    placed = (
        P("sec", "blk", None, None),
        P("sec", None, "blk", None, None),
        P("sec", None, "blk", None, None),
        P("sec", None),
        P("sec", "blk", None),
        P("sec", "blk"),
    )
    return jax.shard_map(
        shards,
        mesh=mesh,
        in_specs=placed,
        out_specs=(
            P("sec", "blk", None, None),
            P("sec", "blk", None, None),
            P("sec"),
            P("sec", None, "blk", None, None),
        ),
        check_vma=False,
    )
```

```python
import functools

import jax
import jax.numpy as jnp
from jax import lax
from jax.experimental import pallas as pl
from jax.experimental.pallas import tpu as pltpu
from jax.sharding import PartitionSpec as P

MESH = pl.DeviceIdType.MESH
VMEM_SPEC = pl.BlockSpec(memory_space=pltpu.VMEM)
SMEM_SPEC = pl.BlockSpec(memory_space=pltpu.SMEM)
ANY_SPEC = pl.BlockSpec(memory_space=pl.ANY)
F32 = jnp.float32
BF16 = jnp.bfloat16
NB = 16
NU = 12
NC = 20
SB = 128
HALF = NU // 2
ROWS = 16
NCH = SB // ROWS
PER = NC // 5
FAR = 5
LATE = 1
SOON = NC - FAR - LATE
CELLS = float(NB * NU * SB * SB)


def slot_tile(entries):
    row = lax.broadcasted_iota(jnp.int32, (16, SB), 0)
    tile = jnp.zeros((16, SB), F32)
    for u, entry in enumerate(entries):
        tile = jnp.where(row == u, entry, tile)
    return tile


def slot_mask(dim_a, dim_b):
    line_a = lax.broadcasted_iota(jnp.int32, (SB, SB), 0)
    line_b = lax.broadcasted_iota(jnp.int32, (SB, SB), 1)
    return (line_a < dim_a) & (line_b < dim_b)


def exists(off_ref, t, c):
    if c == 1:
        return t >= 1
    if c == 2:
        return t <= NU - 2
    down = (lax.axis_index("blk") + NB - off_ref[0, t]) & (NB - 1)
    return down >= 1 if c == 3 else down <= NB - 2


def source_device(off_ref, t, c):
    me = lax.axis_index("blk")
    if c == 1:
        return (me + NB - off_ref[0, t] + off_ref[0, jnp.maximum(t - 1, 0)]) & (NB - 1)
    if c == 2:
        return (me + NB - off_ref[0, t] + off_ref[0, jnp.minimum(t + 1, NU - 1)]) & (NB - 1)
    return (me + (NB - 1 if c == 3 else 1)) & (NB - 1)


def source_slot(t, c):
    if c == 1:
        return jnp.maximum(t - 1, 0)
    if c == 2:
        return jnp.minimum(t + 1, NU - 1)
    return t


def total(x):
    return jnp.sum(jnp.sum(x, axis=0, keepdims=True), axis=1, keepdims=True)


def products(l_ref, r_ref, acc_ref, work, fresh):
    inner = []
    for c, t, x in work:
        stack = jnp.concatenate([l_ref[c + 5 * k, t] for k in range(PER)], axis=0)
        product = jnp.dot(stack, x, preferred_element_type=F32).astype(BF16)
        inner.append(jnp.concatenate([product[k * SB : (k + 1) * SB] for k in range(PER)], axis=1))
    sums = {}
    slots = {}
    for left, (c, t, _) in zip(inner, work):
        right = jnp.concatenate([r_ref[c + 5 * k, t] for k in range(PER)], axis=1)
        term = lax.dot_general(left, right, (((1,), (1,)), ((), ())), preferred_element_type=F32)
        key = id(t)
        sums[key] = sums[key] + term if key in sums else term
        slots[key] = t
    for key, t in slots.items():
        acc_ref[t] = sums[key] if fresh else acc_ref[t] + sums[key]


def main_kernel(
    nsec, off_ref, dims_ref, rank_ref, x_ref, l_hbm, r_hbm,
    prev_ref, rel1, rel2, kept_ref, flag_ref, state_ref, hstate_ref, coef_ref,
    lv, rv, xs, va, v3, v4, gs, ga, g3, g4, recv_v, recv_g, send_v, send_g, h0, h1, v1, vs, kept, st, hst,
    ranks, ranks_all, sums, sums_all, qt, qt_all, part_n, part_p, part_r, alphas, alpha_all, flags,
    l_sem, r_sem, side_s, side_r, p1s, p1r, p2s, p2r, ts, tr, loc, zs, zr, ks, kr, fs, fr, fin
):
    me = lax.axis_index("blk")
    sec = lax.axis_index("sec")
    odd = sec % 2 == 1
    par = me // NCH
    lo = pl.multiple_of((me % NCH) * ROWS, ROWS)

    def section(by):
        return {"sec": (sec + by + nsec) % nsec}

    def peer(k):
        return {"blk": (me + k) % NB}

    def remote(src, dst, send, recv, where):
        return pltpu.make_async_remote_copy(
            src_ref=src, dst_ref=dst, send_sem=send, recv_sem=recv, device_id=where, device_id_type=MESH
        )

    barrier = pltpu.get_barrier_semaphore()
    for k in range(1, NB):
        pl.semaphore_signal(barrier, inc=1, device_id=peer(k), device_id_type=MESH)
    for by in (1, -1, 2, -2, 3, -3):
        pl.semaphore_signal(barrier, inc=1, device_id=section(by), device_id_type=MESH)

    def load(w, i):
        src, dst, sem = ((l_hbm, lv, l_sem), (r_hbm, rv, r_sem))[i]
        return pltpu.make_async_copy(src.at[w], dst.at[w], sem.at[w])

    for c in (0, 3, 4, 1, 2):
        for k in range(PER):
            load(c + 5 * k, 0).start()
            load(c + 5 * k, 1).start()

    def loaded(c):
        for k in range(PER):
            load(c + 5 * k, 0).wait()
            load(c + 5 * k, 1).wait()

    for u in range(NU):
        on = slot_mask(dims_ref[0, 0, u], dims_ref[0, 1, u])
        xs[u // 2, u % 2] = jnp.where(on, x_ref[u // 2, u % 2], jnp.zeros((SB, SB), BF16))
    ranks[...] = slot_tile([rank_ref[0, u].astype(F32) for u in range(NU)])
    down = [jnp.where(exists(off_ref, u, 3), 1.0, 0.0) for u in range(NU)]
    above_it = [jnp.where(exists(off_ref, u, 4), 1.0, 0.0) for u in range(NU)]
    line = lax.broadcasted_iota(jnp.int32, (16, SB), 1)
    flags[...] = jnp.where(line == 0, slot_tile(down), slot_tile(above_it))
    for ref in (part_n, part_p, part_r):
        ref[...] = jnp.zeros((16, SB), F32)
    pl.semaphore_wait(barrier, NB + 5)

    state_of = (xs, gs)
    recv_of = (recv_v, recv_g)
    send_of = (send_v, send_g)
    wide_of = (va, ga)
    side_of = ((v3, v4), (g3, g4))
    tile_of = (ranks, sums, qt)
    tiles_of = (ranks_all, sums_all, qt_all)

    def phase1(i, k):
        to = (me + k) % NB
        at = pl.multiple_of((to % NCH) * ROWS, ROWS)
        return remote(
            state_of[i].at[:, to // NCH, pl.ds(at, ROWS), :], recv_of[i].at[me], p1s.at[i, k], p1r.at[i, k], peer(k)
        )

    def mine(ref):
        return ref.at[:, pl.ds(par, HALF), 1 - par, pl.ds(lo, ROWS), :]

    def phase2(i, k):
        return remote(send_of[i].at[(me + k) % NB], mine(wide_of[i]), p2s.at[i, k], p2r.at[i, k], peer(k))

    def side(i, j):
        return remote(state_of[i], side_of[i][j], side_s.at[i, j], side_r.at[i, j], peer((1, NB - 1)[j]))

    def tiny(i, k):
        return remote(tile_of[i], tiles_of[i].at[me], ts.at[i, k], tr.at[i, k], peer(k))

    def own1(i):
        return pltpu.make_async_copy(state_of[i].at[:, par, pl.ds(lo, ROWS), :], recv_of[i].at[me], loc.at[i, 0])

    def own2(i):
        return pltpu.make_async_copy(send_of[i].at[me], mine(wide_of[i]), loc.at[i, 1])

    def direct(channels, start=0, i=0):
        part = pl.ds(start, channels)
        return remote(l_hbm.at[part], prev_ref.at[part], zs.at[i], zr.at[i], section(1))

    def late():
        return direct(LATE, SOON, 4)

    far = pl.ds(NC - FAR, FAR)
    flag_copy = remote(flags, flag_ref, ks.at[3], kr.at[3], section(1))

    def hop(i):
        if i == 0:
            return remote(l_hbm.at[far], rel1, zs.at[1], zr.at[1], section(-2))
        if i == 1:
            return remote(rel1, rel2, zs.at[2], zr.at[2], section(-2))
        return remote(rel2, prev_ref.at[far], zs.at[3], zr.at[3], section(-3))

    def begin(i):
        @pl.loop(1, NB)
        def _(k):
            phase1(i, k).start()

        own1(i).start()

    def middle(i):
        own1(i).wait()

        @pl.loop(1, NB)
        def _(k):
            phase1(i, k).wait_recv()

        @pl.loop(0, NB)
        def _(t):
            for r in range(HALF):
                up = 2 * r + par
                own = off_ref[0, up] + t + NB
                above = (own - off_ref[0, jnp.minimum(up + 1, NU - 1)]) & (NB - 1)
                below = (own - off_ref[0, jnp.maximum(up - 1, 0)]) & (NB - 1)
                send_of[i][t, 0, r] = recv_of[i][above, r]
                send_of[i][t, 1, r] = recv_of[i][below, r]

        @pl.loop(1, NB)
        def _(k):
            phase2(i, k).start()

        own2(i).start()

    def end(i):
        own2(i).wait()

        @pl.loop(1, NB)
        def _(k):
            phase2(i, k).wait_recv()

    begin(0)

    @pl.when(odd)
    def _():
        direct(SOON).start()
        hop(0).start()

    @pl.when(jnp.logical_not(odd))
    def _():
        direct(NC).start()

    for j in range(2):
        side(0, j).start()

    @pl.loop(1, NB)
    def _(k):
        tiny(0, k).start()

    flag_copy.start()
    ranks_all[me] = ranks[...]
    middle(0)

    def own_v(t):
        return xs[t // 2, t % 2]

    def source(i, c, t):
        if c == 1:
            at = jnp.maximum(t, 1)
            return wide_of[i][0, at // 2, at % 2]
        if c == 2:
            at = jnp.minimum(t + 2, NU)
            return wide_of[i][1, at // 2, at % 2]
        return side_of[i][c - 3][t // 2, t % 2]

    def first_source(c, t):
        return jnp.where(exists(off_ref, t, c), source(0, c, t), jnp.zeros((SB, SB), BF16))

    loaded(0)

    @pl.loop(0, NU, step=2)
    def _(t0):
        pair = [t0, t0 + 1]
        products(lv, rv, h0, [(0, t, own_v(t)) for t in pair], True)
        for t in pair:
            v = own_v(t).astype(F32)
            part_n[pl.ds(t, 1), :] = jnp.sum(v * v, axis=0, keepdims=True)

    for j in range(2):
        side(0, j).wait_recv()
    loaded(3)
    loaded(4)

    @pl.loop(0, NU)
    def _(t):
        products(lv, rv, h0, [(c, t, first_source(c, t)) for c in (3, 4)], False)

    end(0)
    loaded(1)
    loaded(2)

    @pl.loop(0, NU, step=2)
    def _(t0):
        pair = [t0, t0 + 1]
        products(lv, rv, h0, [(c, t, first_source(c, t)) for t in pair for c in (1, 2)], False)
        for t in pair:
            h = jnp.where(slot_mask(dims_ref[0, 0, t], dims_ref[0, 1, t]), h0[t], 0.0)
            h0[t] = h
            part_p[pl.ds(t, 1), :] = jnp.sum(own_v(t).astype(F32) * h, axis=0, keepdims=True)

    @pl.when(odd)
    def _():
        hop(0).wait_recv()
        hop(1).start()

    n_own = jnp.sum(part_n[...], axis=1, keepdims=True)
    p_own = jnp.sum(part_p[...], axis=1, keepdims=True)
    alpha_own = jnp.where(n_own > 0.0, p_own / jnp.where(n_own > 0.0, n_own, 1.0), 0.0)
    alphas[...] = jnp.broadcast_to(alpha_own, (16, SB))

    @pl.loop(0, NU, step=2)
    def _(t0):
        for t in (t0, t0 + 1):
            g = h0[t] - alphas[pl.ds(t, 1), :] * own_v(t).astype(F32)
            gs[t // 2, t % 2] = g.astype(BF16)
            part_r[pl.ds(t, 1), :] = jnp.sum(g * g, axis=0, keepdims=True)

    r_own = jnp.sum(part_r[...], axis=1, keepdims=True)
    lanes = lax.broadcasted_iota(jnp.int32, (16, SB), 1)
    sums[...] = jnp.where(lanes == 0, n_own, jnp.where(lanes == 1, p_own, jnp.where(lanes == 2, r_own, alpha_own)))
    begin(1)

    @pl.loop(1, NB)
    def _(k):
        tiny(1, k).start()

    for j in range(2):
        side(1, j).start()
    sums_all[me] = sums[...]

    @pl.loop(1, NB)
    def _(k):
        tiny(1, k).wait_recv()

    every = sums_all[...]
    place = lax.broadcasted_iota(jnp.int32, (NB, 16, SB), 2)
    nt, pt, rt, at = [jnp.sum(jnp.where(place == i, every, 0.0), axis=2, keepdims=True) for i in range(4)]
    alpha_all[...] = jnp.broadcast_to(at, (NB, 16, SB))
    norm = total(jnp.sum(nt, axis=0))
    a0 = total(jnp.sum(pt, axis=0)) / norm
    gap = at - a0
    beta = jnp.sqrt(total(jnp.sum(rt + gap * gap * nt, axis=0)) / norm + 1e-6)
    scale = jnp.sqrt(CELLS / norm)
    kappa = scale / beta

    def second_source(c, t):
        alpha = alpha_all[source_device(off_ref, t, c), pl.ds(source_slot(t, c), 1), :]
        x = kappa * (source(1, c, t).astype(F32) + (alpha - a0) * source(0, c, t).astype(F32))
        x = jnp.where(exists(off_ref, t, c), x, 0.0).astype(BF16)
        if c < 3:
            vs[c - 1, t] = x
        return x

    middle(1)

    @pl.loop(0, NU, step=2)
    def _(t0):
        work = []
        for t in (t0, t0 + 1):
            x = (kappa * (h0[t] - a0 * own_v(t).astype(F32))).astype(BF16)
            v1[t] = x
            work.append((0, t, x))
        products(lv, rv, h1, work, True)

    for j in range(2):
        side(1, j).wait_recv()

    @pl.loop(0, NU)
    def _(t):
        products(lv, rv, h1, [(c, t, second_source(c, t)) for c in (3, 4)], False)

    end(1)

    @pl.when(odd)
    def _():
        hop(1).wait_recv()
        hop(2).start()

    qt[...] = jnp.zeros((8, SB), F32)

    @pl.loop(0, NU, step=2)
    def _(t0):
        pair = [t0, t0 + 1]
        products(lv, rv, h1, [(c, t, second_source(c, t)) for t in pair for c in (1, 2)], False)
        for t in pair:
            h = jnp.where(slot_mask(dims_ref[0, 0, t], dims_ref[0, 1, t]), h1[t], 0.0)
            h1[t] = h
            qt[0:1, :] += jnp.sum(v1[t].astype(F32) * h, axis=0, keepdims=True)

    @pl.loop(1, NB)
    def _(k):
        tiny(2, k).start()

    qt_all[me] = qt[...]

    @pl.loop(1, NB)
    def _(k):
        tiny(0, k).wait_recv()
        tiny(2, k).wait_recv()

    a1 = total(jnp.sum(qt_all[...], axis=0)) / CELLS
    half = (a0 - a1) / 2.0
    ritz = (a0 + a1) / 2.0 - jnp.sqrt(half * half + beta * beta)
    slip = ritz - a0
    length = jnp.sqrt(beta * beta + slip * slip)
    xcoef, ycoef = beta / length, slip / length
    coef_ref[...] = jnp.broadcast_to(ritz, (8, SB))
    lane = lax.broadcasted_iota(jnp.int32, (1, SB), 1).astype(F32)
    v_coef = xcoef * scale

    def onward(c):
        return remote(kept.at[c], kept_ref.at[c], ks.at[c], kr.at[c], section(1))

    def forward(j):
        return remote(kept_ref.at[0], kept_ref.at[3 + j], fs.at[j], fr.at[j], peer((1, NB - 1)[j]))

    for c in range(3):

        @pl.loop(0, NU, step=2)
        def _(t0):
            for t in (t0, t0 + 1):
                if c == 0:
                    x = (v_coef * own_v(t).astype(F32) + ycoef * v1[t].astype(F32)).astype(BF16)
                    st[t] = x
                    on = lane < ranks[pl.ds(t, 1), :]
                else:
                    x = v_coef * source(0, c, t).astype(F32) + ycoef * vs[c - 1, t].astype(F32)
                    rank = ranks_all[source_device(off_ref, t, c), pl.ds(source_slot(t, c), 1), :]
                    on = (lane < rank) & exists(off_ref, t, c)
                kept[c, t] = jnp.where(on, x.astype(F32), 0.0).astype(BF16)

        if c:
            onward(c - 1).start()
        if c == 1:

            @pl.when(odd)
            def _():
                late().start()


    onward(2).start()

    @pl.loop(0, NU)
    def _(t):
        hst[t] = (v_coef * h0[t] + ycoef * h1[t]).astype(BF16)

    outs = [
        pltpu.make_async_copy(st, state_ref, fin.at[0]),
        pltpu.make_async_copy(hst, hstate_ref, fin.at[1]),
    ]
    for copy in outs:
        copy.start()
    onward(0).wait_recv()
    for j in range(2):
        forward(j).start()

    for i in range(2):
        for j in range(2):
            side(i, j).wait_send()

    @pl.loop(1, NB)
    def _(k):
        for i in range(2):
            phase1(i, k).wait_send()
            phase2(i, k).wait_send()
        for i in range(3):
            tiny(i, k).wait_send()

    for copy in outs:
        copy.wait()

    @pl.when(odd)
    def _():
        direct(SOON).wait_send()
        late().wait_send()
        for i in range(3):
            hop(i).wait_send()
        direct(NC).wait_recv()

    @pl.when(jnp.logical_not(odd))
    def _():
        direct(NC).wait_send()
        direct(SOON).wait_recv()
        late().wait_recv()
        hop(2).wait_recv()

    onward(0).wait_send()
    for c in (1, 2):
        onward(c).wait()
    flag_copy.wait()
    for j in range(2):
        forward(j).wait()


def main_call(nsec, offsets, dims, ranks, x, lenv, renv):
    pair = (HALF, 2, SB, SB)
    flat = (NU, SB, SB)
    tile, slots = (8, SB), (16, SB)
    far = jax.ShapeDtypeStruct((FAR, NU, SB, SB), BF16)
    wide = pltpu.VMEM((2, HALF + 1, 2, SB, SB), BF16)
    bf = lambda *shape: pltpu.VMEM(shape, BF16)
    f32 = lambda *shape: pltpu.VMEM(shape, F32)
    dma = lambda *shape: pltpu.SemaphoreType.DMA(shape)
    return pl.pallas_call(
        functools.partial(main_kernel, nsec),
        out_shape=[
            jax.ShapeDtypeStruct((NC,) + flat, BF16),
            far,
            far,
            jax.ShapeDtypeStruct((5,) + flat, BF16),
            jax.ShapeDtypeStruct(slots, F32),
            jax.ShapeDtypeStruct(flat, BF16),
            jax.ShapeDtypeStruct(flat, BF16),
            jax.ShapeDtypeStruct(tile, F32),
        ],
        in_specs=[SMEM_SPEC, SMEM_SPEC, SMEM_SPEC, VMEM_SPEC, ANY_SPEC, ANY_SPEC],
        out_specs=[ANY_SPEC] * 7 + [VMEM_SPEC],
        scratch_shapes=[
            bf(NC, *flat), bf(NC, *flat), bf(*pair), wide, bf(*pair), bf(*pair), bf(*pair), wide, bf(*pair), bf(*pair),
            bf(NB, HALF, ROWS, SB), bf(NB, HALF, ROWS, SB),
            bf(NB, 2, HALF, ROWS, SB), bf(NB, 2, HALF, ROWS, SB),
            f32(*flat), f32(*flat), bf(*flat), bf(2, *flat), bf(3, *flat), bf(*flat), bf(*flat),
            f32(*slots), f32(NB, *slots), f32(*slots), f32(NB, *slots), f32(*tile), f32(NB, *tile),
            f32(*slots), f32(*slots), f32(*slots), f32(*slots), f32(NB, *slots), f32(*slots),
            dma(NC), dma(NC), dma(2, 2), dma(2, 2), dma(2, NB), dma(2, NB), dma(2, NB), dma(2, NB),
            dma(3, NB), dma(3, NB), dma(2, 2), dma(5), dma(5), dma(4), dma(4), dma(2), dma(2), dma(2),
        ],
        compiler_params=pltpu.CompilerParams(collective_id=0, has_side_effects=True),
        name="davidson",
    )(offsets, dims, ranks, x, lenv, renv)


def update_kernel(
    flag_ref, coef_ref, l_hbm, prev_hbm, kept_hbm, state_hbm, hstate_hbm, next_hbm, s_hbm, hs_hbm, e_ref,
    lp, kp, out, st, hst, l_sem, k_sem, o_sem, s_sem
):
    first_section = lax.axis_index("sec") == 0

    def fetch(src, t):
        return pltpu.make_async_copy(src.at[:, t], lp.at[:, t], l_sem.at[t])

    def fetch_kept(t):
        return pltpu.make_async_copy(kept_hbm.at[:, t], kp.at[:, t], k_sem.at[t])

    def write(src, t):
        return pltpu.make_async_copy(src.at[:, t], next_hbm.at[:, t], o_sem.at[t])

    states = [(state_hbm, st, s_hbm), (hstate_hbm, hst, hs_hbm)]
    takes = [pltpu.make_async_copy(src, at, s_sem.at[i]) for i, (src, at, _) in enumerate(states)]
    gives = [pltpu.make_async_copy(at, dst, s_sem.at[2 + i]) for i, (_, at, dst) in enumerate(states)]

    @pl.when(first_section)
    def _():
        @pl.loop(0, NU)
        def _(t):
            fetch(l_hbm, t).start()

    @pl.when(jnp.logical_not(first_section))
    def _():
        @pl.loop(0, NU)
        def _(t):
            fetch_kept(t).start()
            fetch(prev_hbm, t).start()

    for copy in takes:
        copy.start()
    e_ref[0] = coef_ref[0, 0]

    @pl.when(first_section)
    def _():
        @pl.loop(0, NU)
        def _(t):
            fetch(l_hbm, t).wait()
            write(lp, t).start()

        for take, give in zip(takes, gives):
            take.wait()
            give.start()

        @pl.loop(0, NU)
        def _(t):
            write(lp, t).wait()

    @pl.when(jnp.logical_not(first_section))
    def _():
        def one(t):
            kept = kp[0, t]
            for c in range(5):
                stack = jnp.concatenate([lp[c + 5 * k, t] for k in range(PER)], axis=0)
                x = kp[c, t]
                if c > 2:
                    x = jnp.where(flag_ref[t, c - 3] > 0.5, x, jnp.zeros_like(x))
                inner = jnp.dot(stack, x, preferred_element_type=F32).astype(BF16)
                wide = jnp.concatenate([inner[k * SB : (k + 1) * SB] for k in range(PER)], axis=1)
                new = lax.dot_general(kept, wide, (((0,), (0,)), ((), ())), preferred_element_type=F32).astype(BF16)
                for k in range(PER):
                    out[c + 5 * k, t] = new[:, k * SB : (k + 1) * SB]

        @pl.loop(0, NU, step=2)
        def _(t0):
            for i in range(2):
                fetch_kept(t0 + i).wait()
                fetch(prev_hbm, t0 + i).wait()
            for i in range(2):
                one(t0 + i)

            @pl.when(t0 > 0)
            def _():
                for i in range(2):
                    write(out, t0 + i - 2).start()

        for take, give in zip(takes, gives):
            take.wait()
            give.start()
        for i in range(2):
            write(out, NU - 2 + i).start()

        @pl.loop(0, NU)
        def _(t):
            write(out, t).wait()

    for give in gives:
        give.wait()


def update(flags, coef, lenv, prev, kept, state, hstate):
    flat = (NU, SB, SB)
    return pl.pallas_call(
        update_kernel,
        in_specs=[SMEM_SPEC, SMEM_SPEC] + [ANY_SPEC] * 5,
        out_specs=[ANY_SPEC] * 3 + [SMEM_SPEC],
        out_shape=[
            jax.ShapeDtypeStruct((NC,) + flat, BF16),
            jax.ShapeDtypeStruct(flat, BF16),
            jax.ShapeDtypeStruct(flat, BF16),
            jax.ShapeDtypeStruct((1,), F32),
        ],
        scratch_shapes=[
            pltpu.VMEM((NC,) + flat, BF16),
            pltpu.VMEM((5,) + flat, BF16),
            pltpu.VMEM((NC,) + flat, BF16),
            pltpu.VMEM(flat, BF16),
            pltpu.VMEM(flat, BF16),
            pltpu.SemaphoreType.DMA((NU,)),
            pltpu.SemaphoreType.DMA((NU,)),
            pltpu.SemaphoreType.DMA((NU,)),
            pltpu.SemaphoreType.DMA((4,)),
        ],
        name="update",
    )(flags, coef, lenv, prev, kept, state, hstate)


def shards(wavefunction, left_env, right_env, offsets, dims, ranks):
    nsec = lax.axis_size("sec")
    lenv, renv = left_env[0], right_env[0]
    prev, _, _, kept, flags, state, hstate, coef = main_call(
        nsec, offsets, dims.transpose(0, 2, 1), ranks, wavefunction[0].reshape((HALF, 2, SB, SB)), lenv, renv
    )
    next_left, state, hstate, energy = update(flags, coef, lenv, prev, kept, state, hstate)
    return state[None], hstate[None], energy, next_left[None]


def solution(mesh):
    placed = (
        P("sec", "blk", None, None),
        P("sec", None, "blk", None, None),
        P("sec", None, "blk", None, None),
        P("sec", None),
        P("sec", "blk", None),
        P("sec", "blk"),
    )
    return jax.shard_map(
        shards,
        mesh=mesh,
        in_specs=placed,
        out_specs=(
            P("sec", "blk", None, None),
            P("sec", "blk", None, None),
            P("sec"),
            P("sec", None, "blk", None, None),
        ),
        check_vma=False,
    )
```

```python
import functools

import jax
import jax.numpy as jnp
from jax import lax
from jax.experimental import pallas as pl
from jax.experimental.pallas import tpu as pltpu
from jax.sharding import PartitionSpec as P

MESH = pl.DeviceIdType.MESH
VMEM_SPEC = pl.BlockSpec(memory_space=pltpu.VMEM)
SMEM_SPEC = pl.BlockSpec(memory_space=pltpu.SMEM)
ANY_SPEC = pl.BlockSpec(memory_space=pl.ANY)
F32 = jnp.float32
BF16 = jnp.bfloat16
NB = 16
NU = 12
NC = 20
SB = 128
HALF = NU // 2
ROWS = 16
NCH = SB // ROWS
PER = NC // 5
FAR = 5
CELLS = float(NB * NU * SB * SB)


def slot_tile(entries):
    row = lax.broadcasted_iota(jnp.int32, (16, SB), 0)
    tile = jnp.zeros((16, SB), F32)
    for u, entry in enumerate(entries):
        tile = jnp.where(row == u, entry, tile)
    return tile


def slot_mask(dim_a, dim_b):
    line_a = lax.broadcasted_iota(jnp.int32, (SB, SB), 0)
    line_b = lax.broadcasted_iota(jnp.int32, (SB, SB), 1)
    return (line_a < dim_a) & (line_b < dim_b)


def exists(off_ref, t, c):
    if c == 1:
        return t >= 1
    if c == 2:
        return t <= NU - 2
    down = (lax.axis_index("blk") + NB - off_ref[0, t]) & (NB - 1)
    return down >= 1 if c == 3 else down <= NB - 2


def source_device(off_ref, t, c):
    me = lax.axis_index("blk")
    if c == 1:
        return (me + NB - off_ref[0, t] + off_ref[0, jnp.maximum(t - 1, 0)]) & (NB - 1)
    if c == 2:
        return (me + NB - off_ref[0, t] + off_ref[0, jnp.minimum(t + 1, NU - 1)]) & (NB - 1)
    return (me + (NB - 1 if c == 3 else 1)) & (NB - 1)


def source_slot(t, c):
    if c == 1:
        return jnp.maximum(t - 1, 0)
    if c == 2:
        return jnp.minimum(t + 1, NU - 1)
    return t


def total(x):
    return jnp.sum(jnp.sum(x, axis=0, keepdims=True), axis=1, keepdims=True)


def products(l_ref, r_ref, acc_ref, work, fresh):
    inner = []
    for c, t, x in work:
        stack = jnp.concatenate([l_ref[c + 5 * k, t] for k in range(PER)], axis=0)
        product = jnp.dot(stack, x, preferred_element_type=F32).astype(BF16)
        inner.append(jnp.concatenate([product[k * SB : (k + 1) * SB] for k in range(PER)], axis=1))
    sums = {}
    slots = {}
    for left, (c, t, _) in zip(inner, work):
        right = jnp.concatenate([r_ref[c + 5 * k, t] for k in range(PER)], axis=1)
        term = lax.dot_general(left, right, (((1,), (1,)), ((), ())), preferred_element_type=F32)
        key = id(t)
        sums[key] = sums[key] + term if key in sums else term
        slots[key] = t
    for key, t in slots.items():
        acc_ref[t] = sums[key] if fresh else acc_ref[t] + sums[key]


def main_kernel(
    nsec, off_ref, dims_ref, rank_ref, x_ref, l_hbm, r_hbm,
    prev_ref, rel1, rel2, kept_ref, flag_ref, state_ref, hstate_ref, coef_ref,
    lv, rv, xs, va, v3, v4, gs, ga, g3, g4, recv_v, recv_g, send_v, send_g, h0, h1, v1, vs, kept, st, hst,
    ranks, ranks_all, sums, sums_all, qt, qt_all, part_n, part_p, part_r, alphas, alpha_all, flags,
    l_sem, r_sem, side_s, side_r, p1s, p1r, p2s, p2r, ts, tr, loc, zs, zr, ks, kr, fs, fr, fin
):
    me = lax.axis_index("blk")
    sec = lax.axis_index("sec")
    odd = sec % 2 == 1
    par = me // NCH
    lo = pl.multiple_of((me % NCH) * ROWS, ROWS)

    def section(by):
        return {"sec": (sec + by + nsec) % nsec}

    def peer(k):
        return {"blk": (me + k) % NB}

    def remote(src, dst, send, recv, where):
        return pltpu.make_async_remote_copy(
            src_ref=src, dst_ref=dst, send_sem=send, recv_sem=recv, device_id=where, device_id_type=MESH
        )

    barrier = pltpu.get_barrier_semaphore()
    for k in range(1, NB):
        pl.semaphore_signal(barrier, inc=1, device_id=peer(k), device_id_type=MESH)
    for by in (1, -1, 2, -2, 3, -3):
        pl.semaphore_signal(barrier, inc=1, device_id=section(by), device_id_type=MESH)

    def load(w, i):
        src, dst, sem = ((l_hbm, lv, l_sem), (r_hbm, rv, r_sem))[i]
        return pltpu.make_async_copy(src.at[w], dst.at[w], sem.at[w])

    for c in (0, 3, 4, 1, 2):
        for k in range(PER):
            load(c + 5 * k, 0).start()
            load(c + 5 * k, 1).start()

    def loaded(c):
        for k in range(PER):
            load(c + 5 * k, 0).wait()
            load(c + 5 * k, 1).wait()

    for u in range(NU):
        on = slot_mask(dims_ref[0, 0, u], dims_ref[0, 1, u])
        xs[u // 2, u % 2] = jnp.where(on, x_ref[u // 2, u % 2], jnp.zeros((SB, SB), BF16))
    ranks[...] = slot_tile([rank_ref[0, u].astype(F32) for u in range(NU)])
    down = [jnp.where(exists(off_ref, u, 3), 1.0, 0.0) for u in range(NU)]
    above_it = [jnp.where(exists(off_ref, u, 4), 1.0, 0.0) for u in range(NU)]
    line = lax.broadcasted_iota(jnp.int32, (16, SB), 1)
    flags[...] = jnp.where(line == 0, slot_tile(down), slot_tile(above_it))
    for ref in (part_n, part_p, part_r):
        ref[...] = jnp.zeros((16, SB), F32)
    pl.semaphore_wait(barrier, NB + 5)

    state_of = (xs, gs)
    recv_of = (recv_v, recv_g)
    send_of = (send_v, send_g)
    wide_of = (va, ga)
    side_of = ((v3, v4), (g3, g4))
    tile_of = (ranks, sums, qt)
    tiles_of = (ranks_all, sums_all, qt_all)

    def phase1(i, k):
        to = (me + k) % NB
        at = pl.multiple_of((to % NCH) * ROWS, ROWS)
        return remote(
            state_of[i].at[:, to // NCH, pl.ds(at, ROWS), :], recv_of[i].at[me], p1s.at[i, k], p1r.at[i, k], peer(k)
        )

    def mine(ref):
        return ref.at[:, pl.ds(par, HALF), 1 - par, pl.ds(lo, ROWS), :]

    def phase2(i, k):
        return remote(send_of[i].at[(me + k) % NB], mine(wide_of[i]), p2s.at[i, k], p2r.at[i, k], peer(k))

    def side(i, j):
        return remote(state_of[i], side_of[i][j], side_s.at[i, j], side_r.at[i, j], peer((1, NB - 1)[j]))

    def tiny(i, k):
        return remote(tile_of[i], tiles_of[i].at[me], ts.at[i, k], tr.at[i, k], peer(k))

    def own1(i):
        return pltpu.make_async_copy(state_of[i].at[:, par, pl.ds(lo, ROWS), :], recv_of[i].at[me], loc.at[i, 0])

    def own2(i):
        return pltpu.make_async_copy(send_of[i].at[me], mine(wide_of[i]), loc.at[i, 1])

    def direct(channels):
        part = pl.ds(0, channels)
        return remote(l_hbm.at[part], prev_ref.at[part], zs.at[0], zr.at[0], section(1))

    far = pl.ds(NC - FAR, FAR)
    flag_copy = remote(flags, flag_ref, ks.at[3], kr.at[3], section(1))

    def hop(i):
        if i == 0:
            return remote(l_hbm.at[far], rel1, zs.at[1], zr.at[1], section(-2))
        if i == 1:
            return remote(rel1, rel2, zs.at[2], zr.at[2], section(-2))
        return remote(rel2, prev_ref.at[far], zs.at[3], zr.at[3], section(-3))

    def begin(i):
        @pl.loop(1, NB)
        def _(k):
            phase1(i, k).start()

        own1(i).start()

    def middle(i):
        own1(i).wait()

        @pl.loop(1, NB)
        def _(k):
            phase1(i, k).wait_recv()

        @pl.loop(0, NB)
        def _(t):
            for r in range(HALF):
                up = 2 * r + par
                own = off_ref[0, up] + t + NB
                above = (own - off_ref[0, jnp.minimum(up + 1, NU - 1)]) & (NB - 1)
                below = (own - off_ref[0, jnp.maximum(up - 1, 0)]) & (NB - 1)
                send_of[i][t, 0, r] = recv_of[i][above, r]
                send_of[i][t, 1, r] = recv_of[i][below, r]

        @pl.loop(1, NB)
        def _(k):
            phase2(i, k).start()

        own2(i).start()

    def end(i):
        own2(i).wait()

        @pl.loop(1, NB)
        def _(k):
            phase2(i, k).wait_recv()

    begin(0)

    @pl.when(odd)
    def _():
        direct(NC - FAR).start()
        hop(0).start()

    @pl.when(jnp.logical_not(odd))
    def _():
        direct(NC).start()

    for j in range(2):
        side(0, j).start()

    @pl.loop(1, NB)
    def _(k):
        tiny(0, k).start()

    flag_copy.start()
    ranks_all[me] = ranks[...]
    middle(0)

    def own_v(t):
        return xs[t // 2, t % 2]

    def source(i, c, t):
        if c == 1:
            at = jnp.maximum(t, 1)
            return wide_of[i][0, at // 2, at % 2]
        if c == 2:
            at = jnp.minimum(t + 2, NU)
            return wide_of[i][1, at // 2, at % 2]
        return side_of[i][c - 3][t // 2, t % 2]

    def first_source(c, t):
        return jnp.where(exists(off_ref, t, c), source(0, c, t), jnp.zeros((SB, SB), BF16))

    loaded(0)

    @pl.loop(0, NU, step=2)
    def _(t0):
        pair = [t0, t0 + 1]
        products(lv, rv, h0, [(0, t, own_v(t)) for t in pair], True)
        for t in pair:
            v = own_v(t).astype(F32)
            part_n[pl.ds(t, 1), :] = jnp.sum(v * v, axis=0, keepdims=True)

    for j in range(2):
        side(0, j).wait_recv()
    loaded(3)
    loaded(4)

    @pl.loop(0, NU)
    def _(t):
        products(lv, rv, h0, [(c, t, first_source(c, t)) for c in (3, 4)], False)

    end(0)
    loaded(1)
    loaded(2)

    @pl.loop(0, NU, step=2)
    def _(t0):
        pair = [t0, t0 + 1]
        products(lv, rv, h0, [(c, t, first_source(c, t)) for t in pair for c in (1, 2)], False)
        for t in pair:
            h = jnp.where(slot_mask(dims_ref[0, 0, t], dims_ref[0, 1, t]), h0[t], 0.0)
            h0[t] = h
            part_p[pl.ds(t, 1), :] = jnp.sum(own_v(t).astype(F32) * h, axis=0, keepdims=True)

    @pl.when(odd)
    def _():
        hop(0).wait_recv()
        hop(1).start()

    n_own = jnp.sum(part_n[...], axis=1, keepdims=True)
    p_own = jnp.sum(part_p[...], axis=1, keepdims=True)
    alpha_own = jnp.where(n_own > 0.0, p_own / jnp.where(n_own > 0.0, n_own, 1.0), 0.0)
    alphas[...] = jnp.broadcast_to(alpha_own, (16, SB))

    @pl.loop(0, NU, step=2)
    def _(t0):
        for t in (t0, t0 + 1):
            g = h0[t] - alphas[pl.ds(t, 1), :] * own_v(t).astype(F32)
            gs[t // 2, t % 2] = g.astype(BF16)
            part_r[pl.ds(t, 1), :] = jnp.sum(g * g, axis=0, keepdims=True)

    r_own = jnp.sum(part_r[...], axis=1, keepdims=True)
    lanes = lax.broadcasted_iota(jnp.int32, (16, SB), 1)
    sums[...] = jnp.where(lanes == 0, n_own, jnp.where(lanes == 1, p_own, jnp.where(lanes == 2, r_own, alpha_own)))
    begin(1)

    @pl.loop(1, NB)
    def _(k):
        tiny(1, k).start()

    for j in range(2):
        side(1, j).start()
    sums_all[me] = sums[...]

    @pl.loop(1, NB)
    def _(k):
        tiny(1, k).wait_recv()

    every = sums_all[...]
    place = lax.broadcasted_iota(jnp.int32, (NB, 16, SB), 2)
    nt, pt, rt, at = [jnp.sum(jnp.where(place == i, every, 0.0), axis=2, keepdims=True) for i in range(4)]
    alpha_all[...] = jnp.broadcast_to(at, (NB, 16, SB))
    norm = total(jnp.sum(nt, axis=0))
    a0 = total(jnp.sum(pt, axis=0)) / norm
    gap = at - a0
    beta = jnp.sqrt(total(jnp.sum(rt + gap * gap * nt, axis=0)) / norm + 1e-6)
    scale = jnp.sqrt(CELLS / norm)
    kappa = scale / beta

    def second_source(c, t):
        alpha = alpha_all[source_device(off_ref, t, c), pl.ds(source_slot(t, c), 1), :]
        x = kappa * (source(1, c, t).astype(F32) + (alpha - a0) * source(0, c, t).astype(F32))
        x = jnp.where(exists(off_ref, t, c), x, 0.0).astype(BF16)
        if c < 3:
            vs[c - 1, t] = x
        return x

    middle(1)

    @pl.loop(0, NU, step=2)
    def _(t0):
        work = []
        for t in (t0, t0 + 1):
            x = (kappa * (h0[t] - a0 * own_v(t).astype(F32))).astype(BF16)
            v1[t] = x
            work.append((0, t, x))
        products(lv, rv, h1, work, True)

    for j in range(2):
        side(1, j).wait_recv()

    @pl.loop(0, NU)
    def _(t):
        products(lv, rv, h1, [(c, t, second_source(c, t)) for c in (3, 4)], False)

    end(1)

    @pl.when(odd)
    def _():
        hop(1).wait_recv()
        hop(2).start()

    qt[...] = jnp.zeros((8, SB), F32)

    @pl.loop(0, NU, step=2)
    def _(t0):
        pair = [t0, t0 + 1]
        products(lv, rv, h1, [(c, t, second_source(c, t)) for t in pair for c in (1, 2)], False)
        for t in pair:
            h = jnp.where(slot_mask(dims_ref[0, 0, t], dims_ref[0, 1, t]), h1[t], 0.0)
            h1[t] = h
            qt[0:1, :] += jnp.sum(v1[t].astype(F32) * h, axis=0, keepdims=True)

    @pl.loop(1, NB)
    def _(k):
        tiny(2, k).start()

    qt_all[me] = qt[...]

    @pl.loop(1, NB)
    def _(k):
        tiny(0, k).wait_recv()
        tiny(2, k).wait_recv()

    a1 = total(jnp.sum(qt_all[...], axis=0)) / CELLS
    half = (a0 - a1) / 2.0
    ritz = (a0 + a1) / 2.0 - jnp.sqrt(half * half + beta * beta)
    slip = ritz - a0
    length = jnp.sqrt(beta * beta + slip * slip)
    xcoef, ycoef = beta / length, slip / length
    coef_ref[...] = jnp.broadcast_to(ritz, (8, SB))
    lane = lax.broadcasted_iota(jnp.int32, (1, SB), 1).astype(F32)
    v_coef = xcoef * scale

    def onward(c):
        return remote(kept.at[c], kept_ref.at[c], ks.at[c], kr.at[c], section(1))

    def forward(j):
        return remote(kept_ref.at[0], kept_ref.at[3 + j], fs.at[j], fr.at[j], peer((1, NB - 1)[j]))

    def keep(c, t):
        if c == 0:
            x = (v_coef * own_v(t).astype(F32) + ycoef * v1[t].astype(F32)).astype(BF16)
            st[t] = x
            on = lane < ranks[pl.ds(t, 1), :]
        else:
            x = v_coef * source(0, c, t).astype(F32) + ycoef * vs[c - 1, t].astype(F32)
            rank = ranks_all[source_device(off_ref, t, c), pl.ds(source_slot(t, c), 1), :]
            on = (lane < rank) & exists(off_ref, t, c)
        kept[c, t] = jnp.where(on, x.astype(F32), 0.0).astype(BF16)

    for c in range(3):
        done = 0
        if c:
            for t in range(2):
                keep(c, jnp.int32(t))
            onward(c - 1).start()
            done = 2

        @pl.loop(done, NU, step=2)
        def _(t0):
            for i in range(2):
                keep(c, t0 + i)

    onward(2).start()

    @pl.loop(0, NU)
    def _(t):
        hst[t] = (v_coef * h0[t] + ycoef * h1[t]).astype(BF16)

    outs = [
        pltpu.make_async_copy(st, state_ref, fin.at[0]),
        pltpu.make_async_copy(hst, hstate_ref, fin.at[1]),
    ]
    for copy in outs:
        copy.start()
    onward(0).wait_recv()
    for j in range(2):
        forward(j).start()

    for i in range(2):
        for j in range(2):
            side(i, j).wait_send()

    @pl.loop(1, NB)
    def _(k):
        for i in range(2):
            phase1(i, k).wait_send()
            phase2(i, k).wait_send()
        for i in range(3):
            tiny(i, k).wait_send()

    for copy in outs:
        copy.wait()

    @pl.when(odd)
    def _():
        direct(NC - FAR).wait_send()
        for i in range(3):
            hop(i).wait_send()
        direct(NC).wait_recv()

    @pl.when(jnp.logical_not(odd))
    def _():
        direct(NC).wait_send()
        direct(NC - FAR).wait_recv()
        hop(2).wait_recv()

    onward(0).wait_send()
    for c in (1, 2):
        onward(c).wait()
    flag_copy.wait()
    for j in range(2):
        forward(j).wait()


def main_call(nsec, offsets, dims, ranks, x, lenv, renv):
    pair = (HALF, 2, SB, SB)
    flat = (NU, SB, SB)
    tile, slots = (8, SB), (16, SB)
    far = jax.ShapeDtypeStruct((FAR, NU, SB, SB), BF16)
    wide = pltpu.VMEM((2, HALF + 1, 2, SB, SB), BF16)
    bf = lambda *shape: pltpu.VMEM(shape, BF16)
    f32 = lambda *shape: pltpu.VMEM(shape, F32)
    dma = lambda *shape: pltpu.SemaphoreType.DMA(shape)
    return pl.pallas_call(
        functools.partial(main_kernel, nsec),
        out_shape=[
            jax.ShapeDtypeStruct((NC,) + flat, BF16),
            far,
            far,
            jax.ShapeDtypeStruct((5,) + flat, BF16),
            jax.ShapeDtypeStruct(slots, F32),
            jax.ShapeDtypeStruct(flat, BF16),
            jax.ShapeDtypeStruct(flat, BF16),
            jax.ShapeDtypeStruct(tile, F32),
        ],
        in_specs=[SMEM_SPEC, SMEM_SPEC, SMEM_SPEC, VMEM_SPEC, ANY_SPEC, ANY_SPEC],
        out_specs=[ANY_SPEC] * 7 + [VMEM_SPEC],
        scratch_shapes=[
            bf(NC, *flat), bf(NC, *flat), bf(*pair), wide, bf(*pair), bf(*pair), bf(*pair), wide, bf(*pair), bf(*pair),
            bf(NB, HALF, ROWS, SB), bf(NB, HALF, ROWS, SB),
            bf(NB, 2, HALF, ROWS, SB), bf(NB, 2, HALF, ROWS, SB),
            f32(*flat), f32(*flat), bf(*flat), bf(2, *flat), bf(3, *flat), bf(*flat), bf(*flat),
            f32(*slots), f32(NB, *slots), f32(*slots), f32(NB, *slots), f32(*tile), f32(NB, *tile),
            f32(*slots), f32(*slots), f32(*slots), f32(*slots), f32(NB, *slots), f32(*slots),
            dma(NC), dma(NC), dma(2, 2), dma(2, 2), dma(2, NB), dma(2, NB), dma(2, NB), dma(2, NB),
            dma(3, NB), dma(3, NB), dma(2, 2), dma(4), dma(4), dma(4), dma(4), dma(2), dma(2), dma(2),
        ],
        compiler_params=pltpu.CompilerParams(collective_id=0, has_side_effects=True),
        name="davidson",
    )(offsets, dims, ranks, x, lenv, renv)


def update_kernel(
    flag_ref, coef_ref, l_hbm, prev_hbm, kept_hbm, state_hbm, hstate_hbm, next_hbm, s_hbm, hs_hbm, e_ref,
    lp, kp, out, st, hst, l_sem, k_sem, o_sem, s_sem
):
    first_section = lax.axis_index("sec") == 0

    def fetch(src, t):
        return pltpu.make_async_copy(src.at[:, t], lp.at[:, t], l_sem.at[t])

    def fetch_kept(t):
        return pltpu.make_async_copy(kept_hbm.at[:, t], kp.at[:, t], k_sem.at[t])

    def write(src, t):
        return pltpu.make_async_copy(src.at[:, t], next_hbm.at[:, t], o_sem.at[t])

    states = [(state_hbm, st, s_hbm), (hstate_hbm, hst, hs_hbm)]
    takes = [pltpu.make_async_copy(src, at, s_sem.at[i]) for i, (src, at, _) in enumerate(states)]
    gives = [pltpu.make_async_copy(at, dst, s_sem.at[2 + i]) for i, (_, at, dst) in enumerate(states)]

    @pl.when(first_section)
    def _():
        @pl.loop(0, NU)
        def _(t):
            fetch(l_hbm, t).start()

    @pl.when(jnp.logical_not(first_section))
    def _():
        @pl.loop(0, NU)
        def _(t):
            fetch_kept(t).start()
            fetch(prev_hbm, t).start()

    for copy in takes:
        copy.start()
    e_ref[0] = coef_ref[0, 0]

    @pl.when(first_section)
    def _():
        @pl.loop(0, NU)
        def _(t):
            fetch(l_hbm, t).wait()
            write(lp, t).start()

        for take, give in zip(takes, gives):
            take.wait()
            give.start()

        @pl.loop(0, NU)
        def _(t):
            write(lp, t).wait()

    @pl.when(jnp.logical_not(first_section))
    def _():
        def one(t):
            kept = kp[0, t]
            for c in range(5):
                stack = jnp.concatenate([lp[c + 5 * k, t] for k in range(PER)], axis=0)
                x = kp[c, t]
                if c > 2:
                    x = jnp.where(flag_ref[t, c - 3] > 0.5, x, jnp.zeros_like(x))
                inner = jnp.dot(stack, x, preferred_element_type=F32).astype(BF16)
                wide = jnp.concatenate([inner[k * SB : (k + 1) * SB] for k in range(PER)], axis=1)
                new = lax.dot_general(kept, wide, (((0,), (0,)), ((), ())), preferred_element_type=F32).astype(BF16)
                for k in range(PER):
                    out[c + 5 * k, t] = new[:, k * SB : (k + 1) * SB]

        @pl.loop(0, NU, step=2)
        def _(t0):
            for i in range(2):
                fetch_kept(t0 + i).wait()
                fetch(prev_hbm, t0 + i).wait()
            for i in range(2):
                one(t0 + i)

            @pl.when(t0 > 0)
            def _():
                for i in range(2):
                    write(out, t0 + i - 2).start()

        for take, give in zip(takes, gives):
            take.wait()
            give.start()
        for i in range(2):
            write(out, NU - 2 + i).start()

        @pl.loop(0, NU)
        def _(t):
            write(out, t).wait()

    for give in gives:
        give.wait()


def update(flags, coef, lenv, prev, kept, state, hstate):
    flat = (NU, SB, SB)
    return pl.pallas_call(
        update_kernel,
        in_specs=[SMEM_SPEC, SMEM_SPEC] + [ANY_SPEC] * 5,
        out_specs=[ANY_SPEC] * 3 + [SMEM_SPEC],
        out_shape=[
            jax.ShapeDtypeStruct((NC,) + flat, BF16),
            jax.ShapeDtypeStruct(flat, BF16),
            jax.ShapeDtypeStruct(flat, BF16),
            jax.ShapeDtypeStruct((1,), F32),
        ],
        scratch_shapes=[
            pltpu.VMEM((NC,) + flat, BF16),
            pltpu.VMEM((5,) + flat, BF16),
            pltpu.VMEM((NC,) + flat, BF16),
            pltpu.VMEM(flat, BF16),
            pltpu.VMEM(flat, BF16),
            pltpu.SemaphoreType.DMA((NU,)),
            pltpu.SemaphoreType.DMA((NU,)),
            pltpu.SemaphoreType.DMA((NU,)),
            pltpu.SemaphoreType.DMA((4,)),
        ],
        name="update",
    )(flags, coef, lenv, prev, kept, state, hstate)


def shards(wavefunction, left_env, right_env, offsets, dims, ranks):
    nsec = lax.axis_size("sec")
    lenv, renv = left_env[0], right_env[0]
    prev, _, _, kept, flags, state, hstate, coef = main_call(
        nsec, offsets, dims.transpose(0, 2, 1), ranks, wavefunction[0].reshape((HALF, 2, SB, SB)), lenv, renv
    )
    next_left, state, hstate, energy = update(flags, coef, lenv, prev, kept, state, hstate)
    return state[None], hstate[None], energy, next_left[None]


def solution(mesh):
    placed = (
        P("sec", "blk", None, None),
        P("sec", None, "blk", None, None),
        P("sec", None, "blk", None, None),
        P("sec", None),
        P("sec", "blk", None),
        P("sec", "blk"),
    )
    return jax.shard_map(
        shards,
        mesh=mesh,
        in_specs=placed,
        out_specs=(
            P("sec", "blk", None, None),
            P("sec", "blk", None, None),
            P("sec"),
            P("sec", None, "blk", None, None),
        ),
        check_vma=False,
    )
```

```python
import functools

import jax
import jax.numpy as jnp
from jax import lax
from jax.experimental import pallas as pl
from jax.experimental.pallas import tpu as pltpu
from jax.sharding import PartitionSpec as P

MESH = pl.DeviceIdType.MESH
VMEM_SPEC = pl.BlockSpec(memory_space=pltpu.VMEM)
SMEM_SPEC = pl.BlockSpec(memory_space=pltpu.SMEM)
ANY_SPEC = pl.BlockSpec(memory_space=pl.ANY)
F32 = jnp.float32
BF16 = jnp.bfloat16
NB = 16
NU = 12
NC = 20
SB = 128
HALF = NU // 2
ROWS = 16
NCH = SB // ROWS
PER = NC // 5
FAR = 5
CELLS = float(NB * NU * SB * SB)


def slot_tile(entries):
    row = lax.broadcasted_iota(jnp.int32, (16, SB), 0)
    tile = jnp.zeros((16, SB), F32)
    for u, entry in enumerate(entries):
        tile = jnp.where(row == u, entry, tile)
    return tile


def slot_mask(dim_a, dim_b):
    line_a = lax.broadcasted_iota(jnp.int32, (SB, SB), 0)
    line_b = lax.broadcasted_iota(jnp.int32, (SB, SB), 1)
    return (line_a < dim_a) & (line_b < dim_b)


def exists(off_ref, t, c):
    if c == 1:
        return t >= 1
    if c == 2:
        return t <= NU - 2
    down = (lax.axis_index("blk") + NB - off_ref[0, t]) & (NB - 1)
    return down >= 1 if c == 3 else down <= NB - 2


def source_device(off_ref, t, c):
    me = lax.axis_index("blk")
    if c == 1:
        return (me + NB - off_ref[0, t] + off_ref[0, jnp.maximum(t - 1, 0)]) & (NB - 1)
    if c == 2:
        return (me + NB - off_ref[0, t] + off_ref[0, jnp.minimum(t + 1, NU - 1)]) & (NB - 1)
    return (me + (NB - 1 if c == 3 else 1)) & (NB - 1)


def source_slot(t, c):
    if c == 1:
        return jnp.maximum(t - 1, 0)
    if c == 2:
        return jnp.minimum(t + 1, NU - 1)
    return t


def total(x):
    return jnp.sum(jnp.sum(x, axis=0, keepdims=True), axis=1, keepdims=True)


def products(l_ref, r_ref, acc_ref, work, fresh):
    inner = []
    for c, t, x in work:
        stack = jnp.concatenate([l_ref[c + 5 * k, t] for k in range(PER)], axis=0)
        product = jnp.dot(stack, x, preferred_element_type=F32).astype(BF16)
        inner.append(jnp.concatenate([product[k * SB : (k + 1) * SB] for k in range(PER)], axis=1))
    sums = {}
    slots = {}
    for left, (c, t, _) in zip(inner, work):
        right = jnp.concatenate([r_ref[c + 5 * k, t] for k in range(PER)], axis=1)
        term = lax.dot_general(left, right, (((1,), (1,)), ((), ())), preferred_element_type=F32)
        key = id(t)
        sums[key] = sums[key] + term if key in sums else term
        slots[key] = t
    for key, t in slots.items():
        acc_ref[t] = sums[key] if fresh else acc_ref[t] + sums[key]


def main_kernel(
    nsec, off_ref, dims_ref, rank_ref, x_ref, l_hbm, r_hbm,
    prev_ref, rel1, rel2, kept_ref, flag_ref, state_ref, hstate_ref, coef_ref,
    lv, rv, xs, va, v3, v4, gs, ga, g3, g4, recv_v, recv_g, send_v, send_g, h0, h1, v1, vs, kept, st, hst,
    ranks, ranks_all, sums, sums_all, qt, qt_all, part_n, part_p, part_r, alphas, alpha_all, flags,
    l_sem, r_sem, side_s, side_r, p1s, p1r, p2s, p2r, ts, tr, loc, zs, zr, ks, kr, fs, fr, fin
):
    me = lax.axis_index("blk")
    sec = lax.axis_index("sec")
    odd = sec % 2 == 1
    par = me // NCH
    lo = pl.multiple_of((me % NCH) * ROWS, ROWS)

    def section(by):
        return {"sec": (sec + by + nsec) % nsec}

    def peer(k):
        return {"blk": (me + k) % NB}

    def remote(src, dst, send, recv, where):
        return pltpu.make_async_remote_copy(
            src_ref=src, dst_ref=dst, send_sem=send, recv_sem=recv, device_id=where, device_id_type=MESH
        )

    barrier = pltpu.get_barrier_semaphore()
    for k in range(1, NB):
        pl.semaphore_signal(barrier, inc=1, device_id=peer(k), device_id_type=MESH)
    for by in (1, -1, 2, -2, 3, -3):
        pl.semaphore_signal(barrier, inc=1, device_id=section(by), device_id_type=MESH)

    def load(w, i):
        src, dst, sem = ((l_hbm, lv, l_sem), (r_hbm, rv, r_sem))[i]
        return pltpu.make_async_copy(src.at[w], dst.at[w], sem.at[w])

    for c in (0, 3, 4, 1, 2):
        for k in range(PER):
            load(c + 5 * k, 0).start()
            load(c + 5 * k, 1).start()

    def loaded(c):
        for k in range(PER):
            load(c + 5 * k, 0).wait()
            load(c + 5 * k, 1).wait()

    for u in range(NU):
        on = slot_mask(dims_ref[0, 0, u], dims_ref[0, 1, u])
        xs[u // 2, u % 2] = jnp.where(on, x_ref[u // 2, u % 2], jnp.zeros((SB, SB), BF16))
    ranks[...] = slot_tile([rank_ref[0, u].astype(F32) for u in range(NU)])
    down = [jnp.where(exists(off_ref, u, 3), 1.0, 0.0) for u in range(NU)]
    above_it = [jnp.where(exists(off_ref, u, 4), 1.0, 0.0) for u in range(NU)]
    line = lax.broadcasted_iota(jnp.int32, (16, SB), 1)
    flags[...] = jnp.where(line == 0, slot_tile(down), slot_tile(above_it))
    for ref in (part_n, part_p, part_r):
        ref[...] = jnp.zeros((16, SB), F32)
    pl.semaphore_wait(barrier, NB + 5)

    state_of = (xs, gs)
    recv_of = (recv_v, recv_g)
    send_of = (send_v, send_g)
    wide_of = (va, ga)
    side_of = ((v3, v4), (g3, g4))
    tile_of = (ranks, sums, qt)
    tiles_of = (ranks_all, sums_all, qt_all)

    def phase1(i, k):
        to = (me + k) % NB
        at = pl.multiple_of((to % NCH) * ROWS, ROWS)
        return remote(
            state_of[i].at[:, to // NCH, pl.ds(at, ROWS), :], recv_of[i].at[me], p1s.at[i, k], p1r.at[i, k], peer(k)
        )

    def mine(ref):
        return ref.at[:, pl.ds(par, HALF), 1 - par, pl.ds(lo, ROWS), :]

    def phase2(i, k):
        return remote(send_of[i].at[(me + k) % NB], mine(wide_of[i]), p2s.at[i, k], p2r.at[i, k], peer(k))

    def side(i, j):
        return remote(state_of[i], side_of[i][j], side_s.at[i, j], side_r.at[i, j], peer((1, NB - 1)[j]))

    def tiny(i, k):
        return remote(tile_of[i], tiles_of[i].at[me], ts.at[i, k], tr.at[i, k], peer(k))

    def own1(i):
        return pltpu.make_async_copy(state_of[i].at[:, par, pl.ds(lo, ROWS), :], recv_of[i].at[me], loc.at[i, 0])

    def own2(i):
        return pltpu.make_async_copy(send_of[i].at[me], mine(wide_of[i]), loc.at[i, 1])

    def direct(channels):
        part = pl.ds(0, channels)
        return remote(l_hbm.at[part], prev_ref.at[part], zs.at[0], zr.at[0], section(1))

    far = pl.ds(NC - FAR, FAR)
    flag_copy = remote(flags, flag_ref, ks.at[3], kr.at[3], section(1))

    def hop(i):
        if i == 0:
            return remote(l_hbm.at[far], rel1, zs.at[1], zr.at[1], section(-2))
        if i == 1:
            return remote(rel1, rel2, zs.at[2], zr.at[2], section(-2))
        return remote(rel2, prev_ref.at[far], zs.at[3], zr.at[3], section(-3))

    def begin(i):
        @pl.loop(1, NB)
        def _(k):
            phase1(i, k).start()

        own1(i).start()

    def middle(i):
        own1(i).wait()

        @pl.loop(1, NB)
        def _(k):
            phase1(i, k).wait_recv()

        @pl.loop(0, NB)
        def _(t):
            for r in range(HALF):
                up = 2 * r + par
                own = off_ref[0, up] + t + NB
                above = (own - off_ref[0, jnp.minimum(up + 1, NU - 1)]) & (NB - 1)
                below = (own - off_ref[0, jnp.maximum(up - 1, 0)]) & (NB - 1)
                send_of[i][t, 0, r] = recv_of[i][above, r]
                send_of[i][t, 1, r] = recv_of[i][below, r]

        @pl.loop(1, NB)
        def _(k):
            phase2(i, k).start()

        own2(i).start()

    def end(i):
        own2(i).wait()

        @pl.loop(1, NB)
        def _(k):
            phase2(i, k).wait_recv()

    begin(0)

    @pl.when(odd)
    def _():
        direct(NC - FAR).start()
        hop(0).start()

    @pl.when(jnp.logical_not(odd))
    def _():
        direct(NC).start()

    for j in range(2):
        side(0, j).start()

    @pl.loop(1, NB)
    def _(k):
        tiny(0, k).start()

    flag_copy.start()
    ranks_all[me] = ranks[...]
    middle(0)

    def own_v(t):
        return xs[t // 2, t % 2]

    def source(i, c, t):
        if c == 1:
            at = jnp.maximum(t, 1)
            return wide_of[i][0, at // 2, at % 2]
        if c == 2:
            at = jnp.minimum(t + 2, NU)
            return wide_of[i][1, at // 2, at % 2]
        return side_of[i][c - 3][t // 2, t % 2]

    def first_source(c, t):
        return jnp.where(exists(off_ref, t, c), source(0, c, t), jnp.zeros((SB, SB), BF16))

    loaded(0)

    @pl.loop(0, NU, step=2)
    def _(t0):
        pair = [t0, t0 + 1]
        products(lv, rv, h0, [(0, t, own_v(t)) for t in pair], True)
        for t in pair:
            v = own_v(t).astype(F32)
            part_n[pl.ds(t, 1), :] = jnp.sum(v * v, axis=0, keepdims=True)

    for j in range(2):
        side(0, j).wait_recv()
    loaded(3)
    loaded(4)

    @pl.loop(0, NU)
    def _(t):
        products(lv, rv, h0, [(c, t, first_source(c, t)) for c in (3, 4)], False)

    end(0)
    loaded(1)
    loaded(2)

    @pl.loop(0, NU, step=2)
    def _(t0):
        pair = [t0, t0 + 1]
        products(lv, rv, h0, [(c, t, first_source(c, t)) for t in pair for c in (1, 2)], False)
        for t in pair:
            h = jnp.where(slot_mask(dims_ref[0, 0, t], dims_ref[0, 1, t]), h0[t], 0.0)
            h0[t] = h
            part_p[pl.ds(t, 1), :] = jnp.sum(own_v(t).astype(F32) * h, axis=0, keepdims=True)

    @pl.when(odd)
    def _():
        hop(0).wait_recv()
        hop(1).start()

    n_own = jnp.sum(part_n[...], axis=1, keepdims=True)
    p_own = jnp.sum(part_p[...], axis=1, keepdims=True)
    alpha_own = jnp.where(n_own > 0.0, p_own / jnp.where(n_own > 0.0, n_own, 1.0), 0.0)
    alphas[...] = jnp.broadcast_to(alpha_own, (16, SB))

    @pl.loop(0, NU, step=2)
    def _(t0):
        for t in (t0, t0 + 1):
            g = h0[t] - alphas[pl.ds(t, 1), :] * own_v(t).astype(F32)
            gs[t // 2, t % 2] = g.astype(BF16)
            part_r[pl.ds(t, 1), :] = jnp.sum(g * g, axis=0, keepdims=True)

    r_own = jnp.sum(part_r[...], axis=1, keepdims=True)
    lanes = lax.broadcasted_iota(jnp.int32, (16, SB), 1)
    sums[...] = jnp.where(lanes == 0, n_own, jnp.where(lanes == 1, p_own, jnp.where(lanes == 2, r_own, alpha_own)))
    begin(1)

    @pl.loop(1, NB)
    def _(k):
        tiny(1, k).start()

    for j in range(2):
        side(1, j).start()
    sums_all[me] = sums[...]

    @pl.loop(1, NB)
    def _(k):
        tiny(1, k).wait_recv()

    every = sums_all[...]
    place = lax.broadcasted_iota(jnp.int32, (NB, 16, SB), 2)
    nt, pt, rt, at = [jnp.sum(jnp.where(place == i, every, 0.0), axis=2, keepdims=True) for i in range(4)]
    alpha_all[...] = jnp.broadcast_to(at, (NB, 16, SB))
    norm = total(jnp.sum(nt, axis=0))
    a0 = total(jnp.sum(pt, axis=0)) / norm
    gap = at - a0
    beta = jnp.sqrt(total(jnp.sum(rt + gap * gap * nt, axis=0)) / norm + 1e-6)
    scale = jnp.sqrt(CELLS / norm)
    kappa = scale / beta

    def second_source(c, t):
        alpha = alpha_all[source_device(off_ref, t, c), pl.ds(source_slot(t, c), 1), :]
        x = kappa * (source(1, c, t).astype(F32) + (alpha - a0) * source(0, c, t).astype(F32))
        x = jnp.where(exists(off_ref, t, c), x, 0.0).astype(BF16)
        if c < 3:
            vs[c - 1, t] = x
        return x

    middle(1)

    @pl.loop(0, NU, step=2)
    def _(t0):
        work = []
        for t in (t0, t0 + 1):
            x = (kappa * (h0[t] - a0 * own_v(t).astype(F32))).astype(BF16)
            v1[t] = x
            work.append((0, t, x))
        products(lv, rv, h1, work, True)

    for j in range(2):
        side(1, j).wait_recv()

    @pl.loop(0, NU)
    def _(t):
        products(lv, rv, h1, [(c, t, second_source(c, t)) for c in (3, 4)], False)

    end(1)

    @pl.when(odd)
    def _():
        hop(1).wait_recv()
        hop(2).start()

    qt[...] = jnp.zeros((8, SB), F32)

    @pl.loop(0, NU, step=2)
    def _(t0):
        pair = [t0, t0 + 1]
        products(lv, rv, h1, [(c, t, second_source(c, t)) for t in pair for c in (1, 2)], False)
        for t in pair:
            h = jnp.where(slot_mask(dims_ref[0, 0, t], dims_ref[0, 1, t]), h1[t], 0.0)
            h1[t] = h
            qt[0:1, :] += jnp.sum(v1[t].astype(F32) * h, axis=0, keepdims=True)

    @pl.loop(1, NB)
    def _(k):
        tiny(2, k).start()

    qt_all[me] = qt[...]

    @pl.loop(1, NB)
    def _(k):
        tiny(0, k).wait_recv()
        tiny(2, k).wait_recv()

    a1 = total(jnp.sum(qt_all[...], axis=0)) / CELLS
    half = (a0 - a1) / 2.0
    ritz = (a0 + a1) / 2.0 - jnp.sqrt(half * half + beta * beta)
    slip = ritz - a0
    length = jnp.sqrt(beta * beta + slip * slip)
    xcoef, ycoef = beta / length, slip / length
    coef_ref[...] = jnp.broadcast_to(ritz, (8, SB))
    lane = lax.broadcasted_iota(jnp.int32, (1, SB), 1).astype(F32)
    v_coef = xcoef * scale

    def onward(c):
        return remote(kept.at[c], kept_ref.at[c], ks.at[c], kr.at[c], section(1))

    def forward(j):
        return remote(kept_ref.at[0], kept_ref.at[3 + j], fs.at[j], fr.at[j], peer((1, NB - 1)[j]))

    def keep(c, t):
        if c == 0:
            x = (v_coef * own_v(t).astype(F32) + ycoef * v1[t].astype(F32)).astype(BF16)
            st[t] = x
            on = lane < ranks[pl.ds(t, 1), :]
        else:
            x = v_coef * source(0, c, t).astype(F32) + ycoef * vs[c - 1, t].astype(F32)
            rank = ranks_all[source_device(off_ref, t, c), pl.ds(source_slot(t, c), 1), :]
            on = (lane < rank) & exists(off_ref, t, c)
        kept[c, t] = jnp.where(on, x.astype(F32), 0.0).astype(BF16)

    for c in range(3):
        done = 0
        if c:
            for t in range(2):
                keep(c, jnp.int32(t))
            onward(c - 1).start()
            done = 2

        @pl.loop(done, NU, step=2)
        def _(t0):
            for i in range(2):
                keep(c, t0 + i)

    onward(2).start()

    @pl.loop(0, NU)
    def _(t):
        hst[t] = (v_coef * h0[t] + ycoef * h1[t]).astype(BF16)

    outs = [
        pltpu.make_async_copy(st, state_ref, fin.at[0]),
        pltpu.make_async_copy(hst, hstate_ref, fin.at[1]),
    ]
    for copy in outs:
        copy.start()
    onward(0).wait_recv()
    for j in range(2):
        forward(j).start()

    for i in range(2):
        for j in range(2):
            side(i, j).wait_send()

    @pl.loop(1, NB)
    def _(k):
        for i in range(2):
            phase1(i, k).wait_send()
            phase2(i, k).wait_send()
        for i in range(3):
            tiny(i, k).wait_send()

    for copy in outs:
        copy.wait()

    @pl.when(odd)
    def _():
        direct(NC - FAR).wait_send()
        for i in range(3):
            hop(i).wait_send()
        direct(NC).wait_recv()

    @pl.when(jnp.logical_not(odd))
    def _():
        direct(NC).wait_send()
        direct(NC - FAR).wait_recv()
        hop(2).wait_recv()

    onward(0).wait_send()
    for c in (1, 2):
        onward(c).wait()
    flag_copy.wait()
    for j in range(2):
        forward(j).wait()


def main_call(nsec, offsets, dims, ranks, x, lenv, renv):
    pair = (HALF, 2, SB, SB)
    flat = (NU, SB, SB)
    tile, slots = (8, SB), (16, SB)
    far = jax.ShapeDtypeStruct((FAR, NU, SB, SB), BF16)
    wide = pltpu.VMEM((2, HALF + 1, 2, SB, SB), BF16)
    bf = lambda *shape: pltpu.VMEM(shape, BF16)
    f32 = lambda *shape: pltpu.VMEM(shape, F32)
    dma = lambda *shape: pltpu.SemaphoreType.DMA(shape)
    return pl.pallas_call(
        functools.partial(main_kernel, nsec),
        out_shape=[
            jax.ShapeDtypeStruct((NC,) + flat, BF16),
            far,
            far,
            jax.ShapeDtypeStruct((5,) + flat, BF16),
            jax.ShapeDtypeStruct(slots, F32),
            jax.ShapeDtypeStruct(flat, BF16),
            jax.ShapeDtypeStruct(flat, BF16),
            jax.ShapeDtypeStruct(tile, F32),
        ],
        in_specs=[SMEM_SPEC, SMEM_SPEC, SMEM_SPEC, VMEM_SPEC, ANY_SPEC, ANY_SPEC],
        out_specs=[ANY_SPEC] * 7 + [VMEM_SPEC],
        scratch_shapes=[
            bf(NC, *flat), bf(NC, *flat), bf(*pair), wide, bf(*pair), bf(*pair), bf(*pair), wide, bf(*pair), bf(*pair),
            bf(NB, HALF, ROWS, SB), bf(NB, HALF, ROWS, SB),
            bf(NB, 2, HALF, ROWS, SB), bf(NB, 2, HALF, ROWS, SB),
            f32(*flat), f32(*flat), bf(*flat), bf(2, *flat), bf(3, *flat), bf(*flat), bf(*flat),
            f32(*slots), f32(NB, *slots), f32(*slots), f32(NB, *slots), f32(*tile), f32(NB, *tile),
            f32(*slots), f32(*slots), f32(*slots), f32(*slots), f32(NB, *slots), f32(*slots),
            dma(NC), dma(NC), dma(2, 2), dma(2, 2), dma(2, NB), dma(2, NB), dma(2, NB), dma(2, NB),
            dma(3, NB), dma(3, NB), dma(2, 2), dma(4), dma(4), dma(4), dma(4), dma(2), dma(2), dma(2),
        ],
        compiler_params=pltpu.CompilerParams(collective_id=0, has_side_effects=True),
        name="davidson",
    )(offsets, dims, ranks, x, lenv, renv)


def update_kernel(
    flag_ref, coef_ref, l_hbm, prev_hbm, kept_hbm, state_hbm, hstate_hbm, next_hbm, s_hbm, hs_hbm, e_ref,
    lp, kp, out, st, hst, l_sem, k_sem, o_sem, s_sem
):
    first_section = lax.axis_index("sec") == 0

    def fetch(src, t):
        return pltpu.make_async_copy(src.at[:, t], lp.at[:, t], l_sem.at[t])

    def fetch_kept(t):
        return pltpu.make_async_copy(kept_hbm.at[:, t], kp.at[:, t], k_sem.at[t])

    def write(src, t):
        return pltpu.make_async_copy(src.at[:, t], next_hbm.at[:, t], o_sem.at[t])

    states = [(state_hbm, st, s_hbm), (hstate_hbm, hst, hs_hbm)]
    takes = [pltpu.make_async_copy(src, at, s_sem.at[i]) for i, (src, at, _) in enumerate(states)]
    gives = [pltpu.make_async_copy(at, dst, s_sem.at[2 + i]) for i, (_, at, dst) in enumerate(states)]

    @pl.when(first_section)
    def _():
        @pl.loop(0, NU)
        def _(t):
            fetch(l_hbm, t).start()

    @pl.when(jnp.logical_not(first_section))
    def _():
        @pl.loop(0, NU)
        def _(t):
            fetch_kept(t).start()
            fetch(prev_hbm, t).start()

    for copy in takes:
        copy.start()
    e_ref[0] = coef_ref[0, 0]

    @pl.when(first_section)
    def _():
        @pl.loop(0, NU)
        def _(t):
            fetch(l_hbm, t).wait()
            write(lp, t).start()

        for take, give in zip(takes, gives):
            take.wait()
            give.start()

        @pl.loop(0, NU)
        def _(t):
            write(lp, t).wait()

    @pl.when(jnp.logical_not(first_section))
    def _():
        def one(t):
            kept = kp[0, t]
            wide = []
            for c in range(5):
                stack = jnp.concatenate([lp[c + 5 * k, t] for k in range(PER)], axis=0)
                x = kp[c, t]
                if c > 2:
                    x = jnp.where(flag_ref[t, c - 3] > 0.5, x, jnp.zeros_like(x))
                inner = jnp.dot(stack, x, preferred_element_type=F32).astype(BF16)
                wide += [inner[k * SB : (k + 1) * SB] for k in range(PER)]
            every = jnp.concatenate(wide, axis=1)
            new = lax.dot_general(kept, every, (((0,), (0,)), ((), ())), preferred_element_type=F32).astype(BF16)
            for i in range(NC):
                out[i // PER + 5 * (i % PER), t] = new[:, i * SB : (i + 1) * SB]

        @pl.loop(0, NU, step=2)
        def _(t0):
            for i in range(2):
                fetch_kept(t0 + i).wait()
                fetch(prev_hbm, t0 + i).wait()
            for i in range(2):
                one(t0 + i)

            @pl.when(t0 > 0)
            def _():
                for i in range(2):
                    write(out, t0 + i - 2).start()

        for take, give in zip(takes, gives):
            take.wait()
            give.start()
        for i in range(2):
            write(out, NU - 2 + i).start()

        @pl.loop(0, NU)
        def _(t):
            write(out, t).wait()

    for give in gives:
        give.wait()


def update(flags, coef, lenv, prev, kept, state, hstate):
    flat = (NU, SB, SB)
    return pl.pallas_call(
        update_kernel,
        in_specs=[SMEM_SPEC, SMEM_SPEC] + [ANY_SPEC] * 5,
        out_specs=[ANY_SPEC] * 3 + [SMEM_SPEC],
        out_shape=[
            jax.ShapeDtypeStruct((NC,) + flat, BF16),
            jax.ShapeDtypeStruct(flat, BF16),
            jax.ShapeDtypeStruct(flat, BF16),
            jax.ShapeDtypeStruct((1,), F32),
        ],
        scratch_shapes=[
            pltpu.VMEM((NC,) + flat, BF16),
            pltpu.VMEM((5,) + flat, BF16),
            pltpu.VMEM((NC,) + flat, BF16),
            pltpu.VMEM(flat, BF16),
            pltpu.VMEM(flat, BF16),
            pltpu.SemaphoreType.DMA((NU,)),
            pltpu.SemaphoreType.DMA((NU,)),
            pltpu.SemaphoreType.DMA((NU,)),
            pltpu.SemaphoreType.DMA((4,)),
        ],
        name="update",
    )(flags, coef, lenv, prev, kept, state, hstate)


def shards(wavefunction, left_env, right_env, offsets, dims, ranks):
    nsec = lax.axis_size("sec")
    lenv, renv = left_env[0], right_env[0]
    prev, _, _, kept, flags, state, hstate, coef = main_call(
        nsec, offsets, dims.transpose(0, 2, 1), ranks, wavefunction[0].reshape((HALF, 2, SB, SB)), lenv, renv
    )
    next_left, state, hstate, energy = update(flags, coef, lenv, prev, kept, state, hstate)
    return state[None], hstate[None], energy, next_left[None]


def solution(mesh):
    placed = (
        P("sec", "blk", None, None),
        P("sec", None, "blk", None, None),
        P("sec", None, "blk", None, None),
        P("sec", None),
        P("sec", "blk", None),
        P("sec", "blk"),
    )
    return jax.shard_map(
        shards,
        mesh=mesh,
        in_specs=placed,
        out_specs=(
            P("sec", "blk", None, None),
            P("sec", "blk", None, None),
            P("sec"),
            P("sec", None, "blk", None, None),
        ),
        check_vma=False,
    )
```
